128 devices in a mesh: req: 32 (over z, x, core), tp: 4 (over y).
Axes of the slice: x: 4, y: 4, z: 4, core: 2. Of those that a mesh axis runs over, the one named last changes fastest.
Arguments:
- tokens: bfloat16 [32768, 1280], P('req'), may hold values from -14 to 14
- segments: int32 [32768], P('req'), may hold values from 0 to 30, never falling along the last dimension, each value on 1 to 2048 neighbouring positions
- attend_gain: bfloat16 [1280], replicated, may hold values from 0.25 to 1.75
- attend_weight: bfloat16 [1280, 3, 1280], P(None, None, 'tp'), may hold values from -1 to 1
- output_weight: bfloat16 [1280, 1280], P('tp'), may hold values from -0.15625 to 0.15625
- mixer_gain: bfloat16 [1280], replicated, may hold values from 0.25 to 1.75
- expand_weight: bfloat16 [1280, 5120], P(None, 'tp'), may hold values from -0.15625 to 0.15625
- reduce_weight: bfloat16 [5120, 1280], P('tp'), may hold values from -0.078125 to 0.078125
- output_gain: bfloat16 [1280], replicated, may hold values from 0.25 to 1.75
- merge_weight: bfloat16 [5120, 1280], P(None, 'tp'), may hold values from -0.078125 to 0.078125
- merge_index: int32 [8192, 4], P('req'), may hold values from 0 to 32767, as said below
- owners: int32 [8192, 1], P('req'), may hold values from 0 to 31; in each aligned block of 256 rows (0 to 255, 256 to 511, ...) at most 16 rows name the same one
Outputs:
- owned: bfloat16 [32, 32, 16, 1280], P('req', None, None, 'tp')
The draws below stay inside these ranges and needn't reach their ends.
Inputs may be any that keep to these rules, and one draw needn't show every extreme that they name: segments never fall along the tokens; every image has at most 2048 tokens. `merge_index`: merged rows 256 * j to 256 * (j + 1) - 1 name the tokens 1024 * j to 1024 * (j + 1) - 1, each exactly once. `owners`: within the rows of one index of req each owner is named at most 16 times.
All inputs are finite; a program needn't handle non-finite values.
Results may differ from the reference program's by a relative error of at most 0.014.
Values may be sent and summed in bfloat16 or wider, within the bound.
A program may use at most 128 MiB of HBM per device.

```python
import math
import jax
import jax.numpy as jnp
import numpy as np
from jax import lax

D = 1280
HEADS = 16
HD = 80
FF = 5120
TOK_DEV = 1024
TOKENS = 32768
M_DEV = 256
MERGED = 8192
CAP = 16
N_REQ = 32
N_TP = 4


def draw_tokens(key, part):
    first = jax.random.fold_in(key, 0)
    values = jax.random.normal(first, (TOKENS, D), jnp.float32)
    return jnp.clip(values, -14.0, 14.0).astype(jnp.bfloat16)


def draw_attend_weight(key, part):
    first = jax.random.fold_in(key, 0)
    spread = jnp.clip(jax.random.normal(first, (D, 3, D), jnp.float32), -6.0, 6.0) / math.sqrt(D)
    values = 2.0 * spread
    return jnp.clip(values, -1.0, 1.0).astype(jnp.bfloat16)


def shuffle_block(stream):
    return jax.random.permutation(stream, TOK_DEV)


def draw_merge_index(key, part):
    blocks = TOKENS // TOK_DEV
    streams = jax.random.split(key, blocks)
    orders = jax.vmap(shuffle_block)(streams).astype(jnp.int32)
    starts = (jnp.arange(blocks, dtype=jnp.int32) * TOK_DEV)[:, None]
    return (orders + starts).reshape(MERGED, 4)


def shard_levels(own_key, dims, shards, low, high):
    loudness = 1.0
    for axis_at, shards_of in shards:
        heights = jax.random.uniform(jax.random.fold_in(jax.random.fold_in(own_key, 6), axis_at), (shards_of,), jnp.float32, low / len(shards), high / len(shards))
        loudness = loudness * jnp.repeat(jnp.exp(heights), dims[axis_at] // shards_of).reshape((-1,) + (1,) * (len(dims) - 1 - axis_at))
    return loudness


def length_profile(count, total, bound, slope):
    loads = [(1 << 20) // math.isqrt(standing ** slope) + 1 for standing in range(2, count + 1)]
    spare, holding = total - bound - (count - 1), [1] * (count - 1)
    while spare > 0:
        free = [i for i in range(count - 1) if holding[i] < bound]
        whole, remaining = sum([loads[i] for i in free]), spare
        for i in free:
            more = min(bound - holding[i], max(1, remaining * loads[i] // whole), spare)
            holding[i] = holding[i] + more
            spare = spare - more
    return np.array([bound] + holding)


def ragged(stream_key, number_of, total, limit, slope):
    if number_of == 2:
        one = jax.random.randint(stream_key, (), max(1, total - limit), min(limit, total - 1) + 1)
        return jnp.stack([one, total - one])
    lengths = jnp.asarray(length_profile(number_of, total, limit, slope), jnp.int32)
    couples = (number_of - 1) // 2
    giver, receiver = lengths[1:1 + 2 * couples:2], lengths[2:2 + 2 * couples:2]
    room = jnp.minimum(giver - 1, limit - receiver)
    moved = jax.random.randint(jax.random.fold_in(stream_key, 1), (couples,), 0, 1 << 20) % (room + 1)
    lengths = lengths.at[1:1 + 2 * couples:2].set(giver - moved).at[2:2 + 2 * couples:2].set(receiver + moved)
    return lengths[jax.random.permutation(jax.random.fold_in(stream_key, 2), number_of)]


def shared_out(key, own, number, rows, number_of, top, limit, skew):
    order = jax.random.permutation(key, number_of)
    packed, usual = portions_of(number_of, rows * top, limit, skew, True), portions_of(number_of, rows * top, limit, skew, False)
    places = jnp.arange(number_of)

    def named(sizes, turn):
        used = int((sizes > 0).sum())
        fixed = max(1, used // 4)
        moved = fixed + (places - fixed + turn * (used - fixed)) % max(1, number_of - fixed)
        return jnp.zeros((number_of,), jnp.int32).at[order[jnp.where(places < fixed, places, moved)]].set(jnp.asarray(sizes, jnp.int32))

    sizes = jnp.where(number % 4 == 0, named(packed, number // 4), named(usual, number - number // 4 - 1))
    mixed = jax.random.permutation(jax.random.fold_in(own, 3), number_of)
    donor, sink = mixed[0:number_of // 2 * 2:2], mixed[1:number_of // 2 * 2:2]
    slack = jnp.minimum(sizes[donor] - 1, limit - sizes[sink]) // 2
    slack = jnp.where((donor == order[0]) | (sink == order[0]) | (sizes[sink] == 0), 0, jnp.maximum(slack, 0))
    moved = jax.random.randint(jax.random.fold_in(own, 4), (number_of // 2,), 0, 1 << 20) % (slack + 1)
    sizes = sizes.at[donor].add(-moved).at[sink].add(moved)
    members = jnp.searchsorted(jnp.cumsum(sizes), jnp.arange(rows * top), side="right").astype(jnp.int32)
    listing = members.reshape(top, rows).T
    listing = listing[jax.random.permutation(jax.random.fold_in(own, 1), rows)]
    turn = jax.random.randint(jax.random.fold_in(own, 2), (rows, 1), 0, top)
    return jnp.take_along_axis(listing, (jnp.arange(top)[None, :] + turn) % top, axis=1)


def portions_of(amount, total, limit, skew, full):
    weights = [(1 << 20) // math.isqrt(grade ** skew) + 1 for grade in range(1, amount + 1)]
    largest = limit if full else min(limit, max(-(-total // amount), total * weights[0] // sum(weights)))
    least = 1 if total - largest >= amount - 1 else 0
    holding, surplus = [largest] + [least] * (amount - 1), total - largest - least * (amount - 1)
    while surplus > 0:
        free = [i for i in range(1, amount) if holding[i] < largest] or [i for i in range(1, amount) if holding[i] < limit]
        whole, left = sum([weights[i] for i in free]), surplus
        for i in free:
            addition = min(limit - holding[i], max(1, left * weights[i] // whole), surplus)
            holding[i] = holding[i] + addition
            surplus = surplus - addition
    return np.array(holding)


def noise(rng, dims, width, most, shards=(), kind=jnp.bfloat16):
    factor_of = shard_levels(rng, dims, shards, -0.22, 0.18) if shards else 1.0
    values = jax.random.normal(rng, dims, jnp.float32) * width * factor_of
    return jnp.minimum(jnp.maximum(values, -most), most).astype(kind)


def setup_inputs(seed: int = 0) -> dict:
    arg_keys = jax.random.split(jax.random.key(seed), 13)
    tokens = draw_tokens(jax.random.fold_in(arg_keys[12], 71), 0)
    segments = jnp.searchsorted(jnp.cumsum(ragged(arg_keys[1], N_REQ - 1, TOKENS, 2 * TOK_DEV, 2)), jnp.arange(TOKENS), side="right").astype(jnp.int32)
    attend_gain = jnp.clip(1.0 + 0.15 * jax.random.normal(arg_keys[2], (D,), jnp.float32), 0.25, 1.75).astype(jnp.bfloat16)
    attend_weight = draw_attend_weight(jax.random.fold_in(arg_keys[12], 71), 0)
    output_weight = noise(arg_keys[4], (D, D), D ** -0.5, 0.15625, ((0, 4),))
    mixer_gain = jnp.clip(1.0 + 0.15 * jax.random.normal(arg_keys[5], (D,), jnp.float32), 0.25, 1.75).astype(jnp.bfloat16)
    expand_weight = noise(arg_keys[6], (D, FF), D ** -0.5, 0.15625, ((1, 4),))
    reduce_weight = noise(arg_keys[7], (FF, D), FF ** -0.5, 0.078125, ((0, 4),))
    output_gain = jnp.clip(1.0 + 0.15 * jax.random.normal(arg_keys[8], (D,), jnp.float32), 0.25, 1.75).astype(jnp.bfloat16)
    merge_weight = noise(arg_keys[9], (4 * D, D), (4 * D) ** -0.5, 0.078125, ((1, 4),))
    merge_index = draw_merge_index(jax.random.fold_in(arg_keys[12], 71), 0)
    owners_keys = jax.random.split(jax.random.fold_in(arg_keys[11], 1), MERGED // M_DEV)
    owners_turns = jax.random.permutation(jax.random.fold_in(arg_keys[11], 3), MERGED // M_DEV)
    owners = jax.vmap(lambda own, number: shared_out(jax.random.fold_in(arg_keys[11], 2), own, number, M_DEV, N_REQ, 1, CAP, 2))(owners_keys, owners_turns).reshape((MERGED, 1))
    return dict(tokens=tokens, segments=segments, attend_gain=attend_gain, attend_weight=attend_weight, output_weight=output_weight, mixer_gain=mixer_gain, expand_weight=expand_weight, reduce_weight=reduce_weight, output_gain=output_gain, merge_weight=merge_weight, merge_index=merge_index, owners=owners)


def layer_norm(stream, gain):
    center = lax.optimization_barrier(jnp.mean(stream, axis=-1, keepdims=True))
    shifted = stream - center
    spread = lax.optimization_barrier(jnp.mean(shifted * shifted, axis=-1, keepdims=True))
    return shifted * lax.rsqrt(spread + 1e-06) * gain.astype(jnp.float32)

def round_trip(values):
    return lax.optimization_barrier(values.astype(jnp.bfloat16)).astype(jnp.float32)

def reference(tokens, segments, attend_gain, attend_weight, output_weight, mixer_gain, expand_weight, reduce_weight, output_gain, merge_weight, merge_index, owners):
    stream = tokens.astype(jnp.float32)
    attend_in = layer_norm(stream, attend_gain).astype(jnp.bfloat16)
    projected = jnp.dot(attend_in, attend_weight.reshape(D, 3 * D), preferred_element_type=jnp.float32).astype(jnp.bfloat16)
    queries = projected[:, :D].reshape(TOKENS, HEADS, HD)
    key_rows = projected[:, D:2 * D].reshape(TOKENS, HEADS, HD)
    value_rows = projected[:, 2 * D:].reshape(TOKENS, HEADS, HD)
    margin = 2 * TOK_DEV
    key_padded = jnp.pad(key_rows, ((margin, margin), (0, 0), (0, 0)))
    value_padded = jnp.pad(value_rows, ((margin, margin), (0, 0), (0, 0)))
    segment_padded = jnp.pad(segments, (margin, margin), constant_values=-1)
    factor = 1.0 / math.sqrt(HD)

    def block_context(block):
        start = (block * TOK_DEV).astype(jnp.int32)
        query_block = lax.dynamic_slice_in_dim(queries, start, TOK_DEV, 0).astype(jnp.float32)
        query_segment = lax.dynamic_slice_in_dim(segments, start, TOK_DEV, 0)
        key_block = lax.dynamic_slice_in_dim(key_padded, start, 5 * TOK_DEV, 0).astype(jnp.float32)
        value_block = lax.dynamic_slice_in_dim(value_padded, start, 5 * TOK_DEV, 0).astype(jnp.float32)
        key_segment = lax.dynamic_slice_in_dim(segment_padded, start, 5 * TOK_DEV, 0)
        scores = jnp.einsum('qhd,khd->hqk', query_block, key_block) * factor
        matches = (query_segment[:, None] == key_segment[None, :])[None]
        largest = lax.optimization_barrier(jnp.max(jnp.where(matches, scores, -1e+30), axis=-1, keepdims=True))
        probs = jnp.where(matches, jnp.exp(scores - largest), 0.0)
        norms = lax.optimization_barrier(jnp.sum(probs, axis=-1))
        weighted = jnp.einsum('hqk,khd->qhd', round_trip(probs), value_block)
        return (weighted / jnp.transpose(norms)[:, :, None]).astype(jnp.bfloat16)
    context = lax.map(block_context, jnp.arange(N_REQ, dtype=jnp.int32)).reshape(TOKENS, N_TP, D // N_TP)
    head_terms = jnp.einsum('tgc,gcd->gtd', context.astype(jnp.float32), output_weight.astype(jnp.float32).reshape(N_TP, D // N_TP, D))
    middle = stream + lax.optimization_barrier(jnp.sum(round_trip(head_terms), axis=0))
    mixer_in = layer_norm(middle, mixer_gain).astype(jnp.bfloat16)
    expanded = jax.nn.gelu(jnp.dot(mixer_in, expand_weight, preferred_element_type=jnp.float32), approximate=False).astype(jnp.bfloat16)
    hidden_terms = jnp.einsum('tgc,gcd->gtd', expanded.astype(jnp.float32).reshape(TOKENS, N_TP, FF // N_TP), reduce_weight.astype(jnp.float32).reshape(N_TP, FF // N_TP, D))
    final_stream = middle + lax.optimization_barrier(jnp.sum(round_trip(hidden_terms), axis=0))
    final_normed = layer_norm(final_stream, output_gain).astype(jnp.bfloat16)
    merged = jnp.take(final_normed, merge_index.reshape(-1), axis=0).reshape(MERGED, 4 * D)
    feature = jnp.dot(merged, merge_weight, preferred_element_type=jnp.float32).astype(jnp.bfloat16)
    target = owners[:, 0].reshape(N_REQ, M_DEV)
    choose = (target[:, :, None] == jnp.arange(N_REQ, dtype=jnp.int32)[None, None, :]).astype(jnp.int32)
    slot = lax.optimization_barrier(jnp.sum((jnp.cumsum(choose, axis=1) - 1) * choose, axis=2)).astype(jnp.int32)
    source = jnp.repeat(jnp.arange(N_REQ, dtype=jnp.int32), M_DEV)
    owned = jnp.zeros((N_REQ, N_REQ, CAP, D), jnp.bfloat16)
    owned = owned.at[target.reshape(-1), source, slot.reshape(-1)].set(feature)
    return owned
```

```python
import math

import jax
import jax.numpy as jnp
from jax import lax
from jax.sharding import PartitionSpec as P

HD = 80


def shifted_2(block, axis, distance):
    devices = range(lax.axis_size(axis))
    route = [(i - distance, i) for i in devices if i - distance in devices]
    return lax.ppermute(block, axis, route)


def layer_norm(stream, gain):
    center = jnp.mean(stream, axis=-1, keepdims=True)
    shifted = stream - center
    spread = jnp.mean(shifted * shifted, axis=-1, keepdims=True)
    return shifted * lax.rsqrt(spread + 1e-06) * gain.astype(jnp.float32)


def attention(queries, query_segment, key_value, head_count):
    token_rows = queries.shape[0]
    head_width = head_count * HD
    factor = 1.0 / math.sqrt(HD)
    lowest = jnp.min(query_segment)
    highest = jnp.max(query_segment)

    def absorb(state, piece, piece_segment):

        def update(current):
            running_max, running_sum, weighted = current
            key_block = piece[:, :head_width].reshape(token_rows, head_count, HD)
            value_block = piece[:, head_width:].reshape(token_rows, head_count, HD)
            scores = (
                jnp.einsum("qhd,khd->hqk", queries, key_block, preferred_element_type=jnp.float32)
                * factor
            )
            matches = (query_segment[:, None] == piece_segment[None, :])[None]
            new_max = jnp.maximum(running_max, jnp.max(jnp.where(matches, scores, -1e30), axis=-1))
            probs = jnp.where(matches, jnp.exp(scores - new_max[:, :, None]), 0.0)
            shrink = jnp.exp(running_max - new_max)
            new_sum = running_sum * shrink + jnp.sum(probs, axis=-1)
            update_term = jnp.einsum(
                "hqk,khd->qhd",
                probs.astype(jnp.bfloat16),
                value_block,
                preferred_element_type=jnp.float32,
            )
            new_weighted = weighted * jnp.transpose(shrink)[:, :, None] + update_term
            return (new_max, new_sum, new_weighted)

        def unchanged(current):
            return current

        present = jnp.where(piece_segment > 0, piece_segment, jnp.int32(1 << 30))
        touches = (jnp.max(piece_segment) >= lowest) & (jnp.min(present) <= highest)
        return lax.cond(touches, update, unchanged, state)

    state = (
        jnp.full((head_count, token_rows), -1e30, jnp.float32),
        jnp.zeros((head_count, token_rows), jnp.float32),
        jnp.zeros((token_rows, head_count, HD), jnp.float32),
    )
    state = absorb(state, key_value, query_segment)
    for distance in (1, -1, 2, -2):
        far_pieces, far_segment = shifted_2((key_value, query_segment), "req", distance)
        state = absorb(state, far_pieces, far_segment)
    running_max, running_sum, weighted = state
    context = weighted / jnp.transpose(running_sum)[:, :, None]
    return context.astype(jnp.bfloat16).reshape(token_rows, head_width)


def body(
    tokens,
    segments,
    attend_gain,
    attend_weight,
    output_weight,
    mixer_gain,
    expand_weight,
    reduce_weight,
    output_gain,
    merge_weight,
    merge_index,
    owners,
):
    token_rows = tokens.shape[0]
    head_width = attend_weight.shape[2]
    head_count = head_width // HD
    full_weight = lax.all_gather(output_weight, "tp", axis=0, tiled=True)
    stream = tokens.astype(jnp.float32)
    attend_in = layer_norm(stream, attend_gain).astype(jnp.bfloat16)
    projected = jnp.dot(
        attend_in,
        attend_weight.reshape(attend_weight.shape[0], 3 * head_width),
        preferred_element_type=jnp.float32,
    ).astype(jnp.bfloat16)
    queries = projected[:, :head_width].reshape(token_rows, head_count, HD)
    key_value = projected[:, head_width:]
    context = attention(queries, segments + 1, key_value, head_count)
    full_context = lax.all_gather(context, "tp", axis=1, tiled=True)
    groups = output_weight.shape[0]
    attend_out = jnp.zeros(stream.shape, jnp.float32)
    for g in range(full_weight.shape[0] // groups):
        part = slice(g * groups, (g + 1) * groups)
        term = jnp.dot(full_context[:, part], full_weight[part], preferred_element_type=jnp.float32)
        attend_out = attend_out + term.astype(jnp.bfloat16).astype(jnp.float32)
    middle = stream + attend_out
    mixer_in = layer_norm(middle, mixer_gain).astype(jnp.bfloat16)
    expanded = jax.nn.gelu(
        jnp.dot(mixer_in, expand_weight, preferred_element_type=jnp.float32), approximate=False
    ).astype(jnp.bfloat16)
    hidden_terms = jnp.dot(expanded, reduce_weight, preferred_element_type=jnp.float32)
    final_stream = middle + lax.psum(hidden_terms.astype(jnp.bfloat16), "tp").astype(jnp.float32)
    final_normed = layer_norm(final_stream, output_gain).astype(jnp.bfloat16)
    merged_rows = merge_index.shape[0]
    local_index = merge_index - lax.axis_index("req") * token_rows
    merged = jnp.take(final_normed, local_index.reshape(-1), axis=0).reshape(
        merged_rows, 4 * final_normed.shape[1]
    )
    feature = jnp.dot(merged, merge_weight, preferred_element_type=jnp.float32).astype(jnp.bfloat16)
    peers = lax.axis_size("req")
    capacity = 2 * merged_rows // peers
    target = owners[:, 0]
    choose = (target[:, None] == jnp.arange(peers, dtype=jnp.int32)[None, :]).astype(jnp.int32)
    slot = jnp.sum((jnp.cumsum(choose, axis=0) - 1) * choose, axis=1)
    position = target * capacity + slot
    placement = (
        position[:, None] == jnp.arange(peers * capacity, dtype=jnp.int32)[None, :]
    ).astype(jnp.bfloat16)
    outgoing = jnp.einsum(
        "ms,mc->sc", placement, feature, preferred_element_type=jnp.float32
    ).astype(jnp.bfloat16)
    outgoing = outgoing.reshape(peers, capacity, feature.shape[1])
    received = lax.all_to_all(outgoing, "req", split_axis=0, concat_axis=0, tiled=True)
    return received.reshape(1, peers, capacity, feature.shape[1])


def solution(mesh):
    placed = (
        P("req", None),
        P("req"),
        P(),
        P(None, None, "tp"),
        P("tp", None),
        P(),
        P(None, "tp"),
        P("tp", None),
        P(),
        P(None, "tp"),
        P("req", None),
        P("req", None),
    )
    return jax.shard_map(
        body, mesh=mesh, in_specs=placed, out_specs=P("req", None, None, "tp"), check_vma=False
    )
```

```python
import functools
import math

import jax
import jax.numpy as jnp
from jax import lax
from jax.experimental import pallas as pl
from jax.experimental.pallas import tpu as pltpu
from jax.sharding import PartitionSpec as P

HD = 80
MESH_IDS = pl.DeviceIdType.MESH


def project_kernel(order, ctx_ref, weight_ref, tokens_ref, out_ref, slots, send_sem, recv_sem):
    n = slots.shape[0]
    rows, width = ctx_ref.shape
    cols = out_ref.shape[1]
    me = lax.axis_index("tp")
    place = {"tp": me, "req": lax.axis_index("req")}

    def peer(k):
        where = dict(place, tp=lax.rem(me + k, n))
        return tuple(where[a] for a in order)

    barrier = pltpu.get_barrier_semaphore()
    for k in range(1, n):
        pl.semaphore_signal(barrier, inc=1, device_id=peer(k), device_id_type=MESH_IDS)
    pl.semaphore_wait(barrier, n - 1)
    copies = []
    for k in range(1, n):
        copy = pltpu.make_async_remote_copy(
            src_ref=ctx_ref,
            dst_ref=slots.at[k],
            send_sem=send_sem.at[k],
            recv_sem=recv_sem.at[k],
            device_id=peer(k),
            device_id_type=MESH_IDS,
        )
        copy.start()
        copies.append(copy)
    tile = 256

    def add_term(block, source, first):
        base = pl.multiple_of(source * width, 8)

        @pl.loop(0, rows // tile)
        def _(i):
            r = pl.ds(pl.multiple_of(i * tile, tile), tile)

            @pl.loop(0, cols // tile)
            def _(j):
                c = pl.ds(pl.multiple_of(j * tile, tile), tile)
                term = jnp.dot(
                    block[r, :], weight_ref[pl.ds(base, width), c], preferred_element_type=jnp.float32
                )
                term = term.astype(jnp.bfloat16).astype(jnp.float32)
                if first:
                    out_ref[r, c] = term
                else:
                    out_ref[r, c] = out_ref[r, c] + term

    add_term(ctx_ref, me, True)
    for k in range(1, n):
        copies[k - 1].wait_recv()
        add_term(slots.at[k], lax.rem(me - k + n, n), False)

    @pl.loop(0, rows // tile)
    def _(i):
        r = pl.ds(pl.multiple_of(i * tile, tile), tile)
        out_ref[r, :] = out_ref[r, :] + tokens_ref[r, :].astype(jnp.float32)

    for copy in copies:
        copy.wait_send()


def project(context, weight, tokens, order):
    n = weight.shape[0] // context.shape[1]
    rows, cols = tokens.shape
    return pl.pallas_call(
        functools.partial(project_kernel, order),
        out_shape=jax.ShapeDtypeStruct((rows, cols), jnp.float32),
        in_specs=[pl.BlockSpec(memory_space=pltpu.VMEM)] * 3,
        out_specs=pl.BlockSpec(memory_space=pltpu.VMEM),
        scratch_shapes=[
            pltpu.VMEM((n,) + context.shape, context.dtype),
            pltpu.SemaphoreType.DMA((n,)),
            pltpu.SemaphoreType.DMA((n,)),
        ],
        compiler_params=pltpu.CompilerParams(
            collective_id=0, has_side_effects=True, vmem_limit_bytes=48 * 1024 * 1024
        ),
        cost_estimate=pl.CostEstimate(
            flops=2 * rows * cols * weight.shape[0],
            bytes_accessed=4 * rows * cols + 2 * weight.size + 2 * rows * cols + 2 * n * context.size,
            transcendentals=0,
        ),
    )(context, weight, tokens)


def shifted_2(block, axis, distance):
    devices = range(lax.axis_size(axis))
    route = [(i - distance, i) for i in devices if i - distance in devices]
    return lax.ppermute(block, axis, route)


def layer_norm(stream, gain):
    center = jnp.mean(stream, axis=-1, keepdims=True)
    shifted = stream - center
    spread = jnp.mean(shifted * shifted, axis=-1, keepdims=True)
    return shifted * lax.rsqrt(spread + 1e-06) * gain.astype(jnp.float32)


def attention(queries, query_segment, key_value, head_count):
    token_rows = queries.shape[0]
    head_width = head_count * HD
    factor = 1.0 / math.sqrt(HD)
    lowest = jnp.min(query_segment)
    highest = jnp.max(query_segment)

    def absorb(state, piece, piece_segment):

        def update(current):
            running_max, running_sum, weighted = current
            key_block = piece[:, :head_width].reshape(token_rows, head_count, HD)
            value_block = piece[:, head_width:].reshape(token_rows, head_count, HD)
            scores = (
                jnp.einsum("qhd,khd->hqk", queries, key_block, preferred_element_type=jnp.float32)
                * factor
            )
            matches = (query_segment[:, None] == piece_segment[None, :])[None]
            new_max = jnp.maximum(running_max, jnp.max(jnp.where(matches, scores, -1e30), axis=-1))
            probs = jnp.where(matches, jnp.exp(scores - new_max[:, :, None]), 0.0)
            shrink = jnp.exp(running_max - new_max)
            new_sum = running_sum * shrink + jnp.sum(probs, axis=-1)
            update_term = jnp.einsum(
                "hqk,khd->qhd",
                probs.astype(jnp.bfloat16),
                value_block,
                preferred_element_type=jnp.float32,
            )
            new_weighted = weighted * jnp.transpose(shrink)[:, :, None] + update_term
            return (new_max, new_sum, new_weighted)

        def unchanged(current):
            return current

        present = jnp.where(piece_segment > 0, piece_segment, jnp.int32(1 << 30))
        touches = (jnp.max(piece_segment) >= lowest) & (jnp.min(present) <= highest)
        return lax.cond(touches, update, unchanged, state)

    state = (
        jnp.full((head_count, token_rows), -1e30, jnp.float32),
        jnp.zeros((head_count, token_rows), jnp.float32),
        jnp.zeros((token_rows, head_count, HD), jnp.float32),
    )
    state = absorb(state, key_value, query_segment)
    for distance in (1, -1, 2, -2):
        far_pieces, far_segment = shifted_2((key_value, query_segment), "req", distance)
        state = absorb(state, far_pieces, far_segment)
    running_max, running_sum, weighted = state
    context = weighted / jnp.transpose(running_sum)[:, :, None]
    return context.astype(jnp.bfloat16).reshape(token_rows, head_width)


def body(
    order,
    tokens,
    segments,
    attend_gain,
    attend_weight,
    output_weight,
    mixer_gain,
    expand_weight,
    reduce_weight,
    output_gain,
    merge_weight,
    merge_index,
    owners,
):
    token_rows = tokens.shape[0]
    head_width = attend_weight.shape[2]
    head_count = head_width // HD
    full_weight = lax.all_gather(output_weight, "tp", axis=0, tiled=True)
    stream = tokens.astype(jnp.float32)
    attend_in = layer_norm(stream, attend_gain).astype(jnp.bfloat16)
    projected = jnp.dot(
        attend_in,
        attend_weight.reshape(attend_weight.shape[0], 3 * head_width),
        preferred_element_type=jnp.float32,
    ).astype(jnp.bfloat16)
    queries = projected[:, :head_width].reshape(token_rows, head_count, HD)
    key_value = projected[:, head_width:]
    context = attention(queries, segments + 1, key_value, head_count)
    middle = project(context, full_weight, tokens, order)
    mixer_in = layer_norm(middle, mixer_gain).astype(jnp.bfloat16)
    expanded = jax.nn.gelu(
        jnp.dot(mixer_in, expand_weight, preferred_element_type=jnp.float32), approximate=False
    ).astype(jnp.bfloat16)
    hidden_terms = jnp.dot(expanded, reduce_weight, preferred_element_type=jnp.float32)
    final_stream = middle + lax.psum(hidden_terms.astype(jnp.bfloat16), "tp").astype(jnp.float32)
    final_normed = layer_norm(final_stream, output_gain).astype(jnp.bfloat16)
    merged_rows = merge_index.shape[0]
    local_index = merge_index - lax.axis_index("req") * token_rows
    merged = jnp.take(final_normed, local_index.reshape(-1), axis=0).reshape(
        merged_rows, 4 * final_normed.shape[1]
    )
    feature = jnp.dot(merged, merge_weight, preferred_element_type=jnp.float32).astype(jnp.bfloat16)
    peers = lax.axis_size("req")
    capacity = 2 * merged_rows // peers
    target = owners[:, 0]
    choose = (target[:, None] == jnp.arange(peers, dtype=jnp.int32)[None, :]).astype(jnp.int32)
    slot = jnp.sum((jnp.cumsum(choose, axis=0) - 1) * choose, axis=1)
    position = target * capacity + slot
    placement = (
        position[:, None] == jnp.arange(peers * capacity, dtype=jnp.int32)[None, :]
    ).astype(jnp.bfloat16)
    outgoing = jnp.einsum(
        "ms,mc->sc", placement, feature, preferred_element_type=jnp.float32
    ).astype(jnp.bfloat16)
    outgoing = outgoing.reshape(peers, capacity, feature.shape[1])
    received = lax.all_to_all(outgoing, "req", split_axis=0, concat_axis=0, tiled=True)
    return received.reshape(1, peers, capacity, feature.shape[1])


def solution(mesh):
    placed = (
        P("req", None),
        P("req"),
        P(),
        P(None, None, "tp"),
        P("tp", None),
        P(),
        P(None, "tp"),
        P("tp", None),
        P(),
        P(None, "tp"),
        P("req", None),
        P("req", None),
    )
    return jax.shard_map(
        functools.partial(body, tuple(mesh.axis_names)), mesh=mesh, in_specs=placed, out_specs=P("req", None, None, "tp"), check_vma=False
    )
```

```python
import functools
import math

import jax
import jax.numpy as jnp
from jax import lax
from jax.experimental import pallas as pl
from jax.experimental.pallas import tpu as pltpu
from jax.sharding import PartitionSpec as P

HD = 80
CHUNKS = 2
MESH_IDS = pl.DeviceIdType.MESH


def project_kernel(order, ctx_ref, weight_ref, tokens_ref, out_ref, slots, send_sem, recv_sem):
    n = slots.shape[0]
    rows, width = ctx_ref.shape
    cols = out_ref.shape[1]
    me = lax.axis_index("tp")
    place = {"tp": me, "req": lax.axis_index("req")}

    def peer(k):
        where = dict(place, tp=lax.rem(me + k, n))
        return tuple(where[a] for a in order)

    barrier = pltpu.get_barrier_semaphore()
    for k in range(1, n):
        pl.semaphore_signal(barrier, inc=1, device_id=peer(k), device_id_type=MESH_IDS)
    pl.semaphore_wait(barrier, n - 1)
    copies = []
    for k in range(1, n):
        copy = pltpu.make_async_remote_copy(
            src_ref=ctx_ref,
            dst_ref=slots.at[k],
            send_sem=send_sem.at[k],
            recv_sem=recv_sem.at[k],
            device_id=peer(k),
            device_id_type=MESH_IDS,
        )
        copy.start()
        copies.append(copy)
    tile = 256

    def add_term(block, source, first):
        base = pl.multiple_of(source * width, 8)

        @pl.loop(0, rows // tile)
        def _(i):
            r = pl.ds(pl.multiple_of(i * tile, tile), tile)

            @pl.loop(0, cols // tile)
            def _(j):
                c = pl.ds(pl.multiple_of(j * tile, tile), tile)
                term = jnp.dot(
                    block[r, :], weight_ref[pl.ds(base, width), c], preferred_element_type=jnp.float32
                )
                term = term.astype(jnp.bfloat16).astype(jnp.float32)
                if first:
                    out_ref[r, c] = term
                else:
                    out_ref[r, c] = out_ref[r, c] + term

    add_term(ctx_ref, me, True)
    for k in range(1, n):
        copies[k - 1].wait_recv()
        add_term(slots.at[k], lax.rem(me - k + n, n), False)

    @pl.loop(0, rows // tile)
    def _(i):
        r = pl.ds(pl.multiple_of(i * tile, tile), tile)
        out_ref[r, :] = out_ref[r, :] + tokens_ref[r, :].astype(jnp.float32)

    for copy in copies:
        copy.wait_send()


def project(context, weight, tokens, order, call):
    n = weight.shape[0] // context.shape[1]
    rows, cols = tokens.shape
    return pl.pallas_call(
        functools.partial(project_kernel, order),
        out_shape=jax.ShapeDtypeStruct((rows, cols), jnp.float32),
        in_specs=[pl.BlockSpec(memory_space=pltpu.VMEM)] * 3,
        out_specs=pl.BlockSpec(memory_space=pltpu.VMEM),
        scratch_shapes=[
            pltpu.VMEM((n,) + context.shape, context.dtype),
            pltpu.SemaphoreType.DMA((n,)),
            pltpu.SemaphoreType.DMA((n,)),
        ],
        compiler_params=pltpu.CompilerParams(
            collective_id=call, has_side_effects=True, vmem_limit_bytes=48 * 1024 * 1024
        ),
        cost_estimate=pl.CostEstimate(
            flops=2 * rows * cols * weight.shape[0],
            bytes_accessed=4 * rows * cols + 2 * weight.size + 2 * rows * cols + 2 * n * context.size,
            transcendentals=0,
        ),
    )(context, weight, tokens)


def shifted_2(block, axis, distance):
    devices = range(lax.axis_size(axis))
    route = [(i - distance, i) for i in devices if i - distance in devices]
    return lax.ppermute(block, axis, route)


def layer_norm(stream, gain):
    center = jnp.mean(stream, axis=-1, keepdims=True)
    shifted = stream - center
    spread = jnp.mean(shifted * shifted, axis=-1, keepdims=True)
    return shifted * lax.rsqrt(spread + 1e-06) * gain.astype(jnp.float32)


def attention(queries, query_segment, pieces, head_count):
    token_rows = queries.shape[0]
    head_width = head_count * HD
    factor = 1.0 / math.sqrt(HD)
    lowest = jnp.min(query_segment)
    highest = jnp.max(query_segment)

    def absorb(state, piece, piece_segment):

        def update(current):
            running_max, running_sum, weighted = current
            key_block = piece[:, :head_width].reshape(piece.shape[0], head_count, HD)
            value_block = piece[:, head_width:].reshape(piece.shape[0], head_count, HD)
            scores = (
                jnp.einsum("qhd,khd->hqk", queries, key_block, preferred_element_type=jnp.float32)
                * factor
            )
            matches = (query_segment[:, None] == piece_segment[None, :])[None]
            new_max = jnp.maximum(running_max, jnp.max(jnp.where(matches, scores, -1e30), axis=-1))
            probs = jnp.where(matches, jnp.exp(scores - new_max[:, :, None]), 0.0)
            shrink = jnp.exp(running_max - new_max)
            new_sum = running_sum * shrink + jnp.sum(probs, axis=-1)
            update_term = jnp.einsum(
                "hqk,khd->qhd",
                probs.astype(jnp.bfloat16),
                value_block,
                preferred_element_type=jnp.float32,
            )
            new_weighted = weighted * jnp.transpose(shrink)[:, :, None] + update_term
            return (new_max, new_sum, new_weighted)

        def unchanged(current):
            return current

        present = jnp.where(piece_segment > 0, piece_segment, jnp.int32(1 << 30))
        touches = (jnp.max(piece_segment) >= lowest) & (jnp.min(present) <= highest)
        return lax.cond(touches, update, unchanged, state)

    state = (
        jnp.full((head_count, token_rows), -1e30, jnp.float32),
        jnp.zeros((head_count, token_rows), jnp.float32),
        jnp.zeros((token_rows, head_count, HD), jnp.float32),
    )
    for piece, piece_segment in pieces:
        state = absorb(state, piece, piece_segment)
    running_max, running_sum, weighted = state
    context = weighted / jnp.transpose(running_sum)[:, :, None]
    return context.astype(jnp.bfloat16).reshape(token_rows, head_width)


def body(
    order,
    tokens,
    segments,
    attend_gain,
    attend_weight,
    output_weight,
    mixer_gain,
    expand_weight,
    reduce_weight,
    output_gain,
    merge_weight,
    merge_index,
    owners,
):
    token_rows = tokens.shape[0]
    head_width = attend_weight.shape[2]
    head_count = head_width // HD
    full_weight = lax.all_gather(output_weight, "tp", axis=0, tiled=True)
    stream = tokens.astype(jnp.float32)
    attend_in = layer_norm(stream, attend_gain).astype(jnp.bfloat16)
    projected = jnp.dot(
        attend_in,
        attend_weight.reshape(attend_weight.shape[0], 3 * head_width),
        preferred_element_type=jnp.float32,
    ).astype(jnp.bfloat16)
    queries = projected[:, :head_width].reshape(token_rows, head_count, HD)
    key_value = projected[:, head_width:]
    marks = segments + 1
    pieces = [(key_value, marks)]
    for distance in (1, -1, 2, -2):
        pieces.append(shifted_2((key_value, marks), "req", distance))
    finals = []
    span = token_rows // CHUNKS
    for c in range(CHUNKS):
        rows = slice(c * span, (c + 1) * span)
        chunk_queries, chunk_marks = queries[rows], marks[rows]
        if finals:
            chunk_queries, chunk_marks, _ = lax.optimization_barrier(
                (chunk_queries, chunk_marks, hidden_terms)
            )
        context = attention(chunk_queries, chunk_marks, pieces, head_count)
        middle = project(context, full_weight, tokens[rows], order, c)
        mixer_in = layer_norm(middle, mixer_gain).astype(jnp.bfloat16)
        expanded = jax.nn.gelu(
            jnp.dot(mixer_in, expand_weight, preferred_element_type=jnp.float32), approximate=False
        ).astype(jnp.bfloat16)
        hidden_terms = jnp.dot(expanded, reduce_weight, preferred_element_type=jnp.float32)
        hidden_terms = hidden_terms.astype(jnp.bfloat16)
        if finals:
            hidden_terms, _ = lax.optimization_barrier((hidden_terms, finals[-1]))
        finals.append(middle + lax.psum(hidden_terms, "tp").astype(jnp.float32))
    final_stream = jnp.concatenate(finals, axis=0)
    final_normed = layer_norm(final_stream, output_gain).astype(jnp.bfloat16)
    merged_rows = merge_index.shape[0]
    local_index = merge_index - lax.axis_index("req") * token_rows
    merged = jnp.take(final_normed, local_index.reshape(-1), axis=0).reshape(
        merged_rows, 4 * final_normed.shape[1]
    )
    feature = jnp.dot(merged, merge_weight, preferred_element_type=jnp.float32).astype(jnp.bfloat16)
    peers = lax.axis_size("req")
    capacity = 2 * merged_rows // peers
    target = owners[:, 0]
    choose = (target[:, None] == jnp.arange(peers, dtype=jnp.int32)[None, :]).astype(jnp.int32)
    slot = jnp.sum((jnp.cumsum(choose, axis=0) - 1) * choose, axis=1)
    position = target * capacity + slot
    placement = (
        position[:, None] == jnp.arange(peers * capacity, dtype=jnp.int32)[None, :]
    ).astype(jnp.bfloat16)
    outgoing = jnp.einsum(
        "ms,mc->sc", placement, feature, preferred_element_type=jnp.float32
    ).astype(jnp.bfloat16)
    outgoing = outgoing.reshape(peers, capacity, feature.shape[1])
    received = lax.all_to_all(outgoing, "req", split_axis=0, concat_axis=0, tiled=True)
    return received.reshape(1, peers, capacity, feature.shape[1])


def solution(mesh):
    placed = (
        P("req", None),
        P("req"),
        P(),
        P(None, None, "tp"),
        P("tp", None),
        P(),
        P(None, "tp"),
        P("tp", None),
        P(),
        P(None, "tp"),
        P("req", None),
        P("req", None),
    )
    return jax.shard_map(
        functools.partial(body, tuple(mesh.axis_names)), mesh=mesh, in_specs=placed, out_specs=P("req", None, None, "tp"), check_vma=False
    )
```

```python
import functools
import math

import jax
import jax.numpy as jnp
from jax import lax
from jax.experimental import pallas as pl
from jax.experimental.pallas import tpu as pltpu
from jax.sharding import PartitionSpec as P

HD = 80
TILE = 256
MESH_IDS = pl.DeviceIdType.MESH


def project_kernel(order, ctx_ref, weight_ref, tokens_ref, out_ref, slots, send_sem, recv_sem):
    n = slots.shape[0]
    rows, width = ctx_ref.shape
    cols = out_ref.shape[1]
    me = lax.axis_index("tp")
    place = {"tp": me, "req": lax.axis_index("req")}

    def peer(k):
        where = dict(place, tp=lax.rem(me + k, n))
        return tuple(where[a] for a in order)

    barrier = pltpu.get_barrier_semaphore()
    for k in range(1, n):
        pl.semaphore_signal(barrier, inc=1, device_id=peer(k), device_id_type=MESH_IDS)
    pl.semaphore_wait(barrier, n - 1)
    copies = []
    for k in range(1, n):
        copy = pltpu.make_async_remote_copy(
            src_ref=ctx_ref,
            dst_ref=slots.at[k],
            send_sem=send_sem.at[k],
            recv_sem=recv_sem.at[k],
            device_id=peer(k),
            device_id_type=MESH_IDS,
        )
        copy.start()
        copies.append(copy)
    tile = 256

    def add_term(block, source, first):
        base = pl.multiple_of(source * width, 8)

        @pl.loop(0, rows // tile)
        def _(i):
            r = pl.ds(pl.multiple_of(i * tile, tile), tile)

            @pl.loop(0, cols // tile)
            def _(j):
                c = pl.ds(pl.multiple_of(j * tile, tile), tile)
                term = jnp.dot(
                    block[r, :], weight_ref[pl.ds(base, width), c], preferred_element_type=jnp.float32
                )
                term = term.astype(jnp.bfloat16).astype(jnp.float32)
                if first:
                    out_ref[r, c] = term
                else:
                    out_ref[r, c] = out_ref[r, c] + term

    add_term(ctx_ref, me, True)
    for k in range(1, n):
        copies[k - 1].wait_recv()
        add_term(slots.at[k], lax.rem(me - k + n, n), False)

    @pl.loop(0, rows // tile)
    def _(i):
        r = pl.ds(pl.multiple_of(i * tile, tile), tile)
        out_ref[r, :] = out_ref[r, :] + tokens_ref[r, :].astype(jnp.float32)

    for copy in copies:
        copy.wait_send()


def project(context, weight, tokens, order):
    n = weight.shape[0] // context.shape[1]
    rows, cols = tokens.shape
    return pl.pallas_call(
        functools.partial(project_kernel, order),
        out_shape=jax.ShapeDtypeStruct((rows, cols), jnp.float32),
        in_specs=[pl.BlockSpec(memory_space=pltpu.VMEM)] * 3,
        out_specs=pl.BlockSpec(memory_space=pltpu.VMEM),
        scratch_shapes=[
            pltpu.VMEM((n,) + context.shape, context.dtype),
            pltpu.SemaphoreType.DMA((n,)),
            pltpu.SemaphoreType.DMA((n,)),
        ],
        compiler_params=pltpu.CompilerParams(
            collective_id=0, has_side_effects=True, vmem_limit_bytes=48 * 1024 * 1024
        ),
        cost_estimate=pl.CostEstimate(
            flops=2 * rows * cols * weight.shape[0],
            bytes_accessed=4 * rows * cols + 2 * weight.size + 2 * rows * cols + 2 * n * context.size,
            transcendentals=0,
        ),
    )(context, weight, tokens)


def shifted_2(block, axis, distance):
    devices = range(lax.axis_size(axis))
    route = [(i - distance, i) for i in devices if i - distance in devices]
    return lax.ppermute(block, axis, route)


def layer_norm(stream, gain):
    center = jnp.mean(stream, axis=-1, keepdims=True)
    shifted = stream - center
    spread = jnp.mean(shifted * shifted, axis=-1, keepdims=True)
    return shifted * lax.rsqrt(spread + 1e-06) * gain.astype(jnp.float32)


def flash_kernel(bounds, q_ref, qm_ref, k_ref, v_ref, km_ref, o_ref):
    i = pl.program_id(1)
    tile = TILE
    factor = 1.0 / math.sqrt(HD)
    q = q_ref[0]
    qm = qm_ref[...]

    def step(j, carry):
        running_max, running_sum, weighted = carry
        start = pl.multiple_of(j * tile, tile)
        keys = k_ref[0, pl.ds(start, tile), :]
        values = v_ref[0, pl.ds(start, tile), :]
        km = km_ref[:, pl.ds(start, tile)]
        scores = lax.dot_general(
            q, keys, (((1,), (1,)), ((), ())), preferred_element_type=jnp.float32
        ) * factor
        matches = qm == km
        new_max = jnp.maximum(
            running_max, jnp.max(jnp.where(matches, scores, -1e30), axis=1, keepdims=True)
        )
        probs = jnp.where(matches, jnp.exp(scores - new_max), 0.0)
        shrink = jnp.exp(running_max - new_max)
        new_sum = running_sum * shrink + jnp.sum(probs, axis=1, keepdims=True)
        new_weighted = weighted * shrink + jnp.dot(
            probs.astype(jnp.bfloat16), values, preferred_element_type=jnp.float32
        )
        return new_max, new_sum, new_weighted

    rows = q.shape[0]
    init = (
        jnp.full((rows, 1), -1e30, jnp.float32),
        jnp.zeros((rows, 1), jnp.float32),
        jnp.zeros((rows, q.shape[1]), jnp.float32),
    )
    _, total, weighted = lax.fori_loop(bounds[0, i], bounds[1, i], step, init)
    o_ref[0] = (weighted / total).astype(o_ref.dtype)


def attention(queries, query_marks, keys, values, key_marks):
    heads, rows, width = queries.shape
    key_rows = keys.shape[1]
    tiles = rows // TILE
    low = query_marks.reshape(tiles, TILE).min(axis=1)
    high = query_marks.reshape(tiles, TILE).max(axis=1)
    valid = (key_marks[None, :] >= low[:, None]) & (key_marks[None, :] <= high[:, None])
    first = jnp.argmax(valid, axis=1)
    last = key_rows - 1 - jnp.argmax(valid[:, ::-1], axis=1)
    bounds = jnp.stack([first // TILE, last // TILE + 1]).astype(jnp.int32)
    return pl.pallas_call(
        flash_kernel,
        out_shape=jax.ShapeDtypeStruct(queries.shape, queries.dtype),
        grid_spec=pltpu.PrefetchScalarGridSpec(
            num_scalar_prefetch=1,
            grid=(heads, tiles),
            in_specs=[
                pl.BlockSpec((1, TILE, width), lambda h, i, b: (h, i, 0)),
                pl.BlockSpec((TILE, 1), lambda h, i, b: (i, 0)),
                pl.BlockSpec((1, key_rows, width), lambda h, i, b: (h, 0, 0)),
                pl.BlockSpec((1, key_rows, width), lambda h, i, b: (h, 0, 0)),
                pl.BlockSpec((1, key_rows), lambda h, i, b: (0, 0)),
            ],
            out_specs=pl.BlockSpec((1, TILE, width), lambda h, i, b: (h, i, 0)),
        ),
        compiler_params=pltpu.CompilerParams(vmem_limit_bytes=48 * 1024 * 1024),
        cost_estimate=pl.CostEstimate(
            flops=4 * heads * rows * 2048 * width,
            bytes_accessed=2 * (queries.size * 2 + keys.size + values.size),
            transcendentals=heads * rows * 2048,
        ),
    )(bounds, queries, query_marks.reshape(rows, 1), keys, values, key_marks.reshape(1, key_rows))


def body(
    order,
    tokens,
    segments,
    attend_gain,
    attend_weight,
    output_weight,
    mixer_gain,
    expand_weight,
    reduce_weight,
    output_gain,
    merge_weight,
    merge_index,
    owners,
):
    token_rows = tokens.shape[0]
    head_width = attend_weight.shape[2]
    head_count = head_width // HD
    full_weight = lax.all_gather(output_weight, "tp", axis=0, tiled=True)
    stream = tokens.astype(jnp.float32)
    attend_in = layer_norm(stream, attend_gain).astype(jnp.bfloat16)
    projected = jnp.dot(
        attend_in,
        attend_weight.reshape(attend_weight.shape[0], 3 * head_width),
        preferred_element_type=jnp.float32,
    ).astype(jnp.bfloat16)
    key_value = projected[:, head_width:]
    marks = segments + 1
    near = {0: (key_value, marks)}
    for distance in (1, -1, 2, -2):
        near[distance] = shifted_2((key_value, marks), "req", distance)
    ordered = [near[d] for d in (2, 1, 0, -1, -2)]
    all_kv = jnp.concatenate([p for p, _ in ordered], axis=0)
    key_marks = jnp.concatenate([m for _, m in ordered], axis=0)

    def by_head(block):
        return jnp.transpose(block.reshape(block.shape[0], head_count, HD), (1, 0, 2))

    context = attention(
        by_head(projected[:, :head_width]),
        marks,
        by_head(all_kv[:, :head_width]),
        by_head(all_kv[:, head_width:]),
        key_marks,
    )
    context = jnp.transpose(context, (1, 0, 2)).reshape(token_rows, head_width)
    middle = project(context, full_weight, tokens, order)
    mixer_in = layer_norm(middle, mixer_gain).astype(jnp.bfloat16)
    expanded = jax.nn.gelu(
        jnp.dot(mixer_in, expand_weight, preferred_element_type=jnp.float32), approximate=False
    ).astype(jnp.bfloat16)
    hidden_terms = jnp.dot(expanded, reduce_weight, preferred_element_type=jnp.float32)
    final_stream = middle + lax.psum(hidden_terms.astype(jnp.bfloat16), "tp").astype(jnp.float32)
    final_normed = layer_norm(final_stream, output_gain).astype(jnp.bfloat16)
    merged_rows = merge_index.shape[0]
    local_index = merge_index - lax.axis_index("req") * token_rows
    merged = jnp.take(final_normed, local_index.reshape(-1), axis=0).reshape(
        merged_rows, 4 * final_normed.shape[1]
    )
    feature = jnp.dot(merged, merge_weight, preferred_element_type=jnp.float32).astype(jnp.bfloat16)
    peers = lax.axis_size("req")
    capacity = 2 * merged_rows // peers
    target = owners[:, 0]
    choose = (target[:, None] == jnp.arange(peers, dtype=jnp.int32)[None, :]).astype(jnp.int32)
    slot = jnp.sum((jnp.cumsum(choose, axis=0) - 1) * choose, axis=1)
    position = target * capacity + slot
    placement = (
        position[:, None] == jnp.arange(peers * capacity, dtype=jnp.int32)[None, :]
    ).astype(jnp.bfloat16)
    outgoing = jnp.einsum(
        "ms,mc->sc", placement, feature, preferred_element_type=jnp.float32
    ).astype(jnp.bfloat16)
    outgoing = outgoing.reshape(peers, capacity, feature.shape[1])
    received = lax.all_to_all(outgoing, "req", split_axis=0, concat_axis=0, tiled=True)
    return received.reshape(1, peers, capacity, feature.shape[1])


def solution(mesh):
    placed = (
        P("req", None),
        P("req"),
        P(),
        P(None, None, "tp"),
        P("tp", None),
        P(),
        P(None, "tp"),
        P("tp", None),
        P(),
        P(None, "tp"),
        P("req", None),
        P("req", None),
    )
    return jax.shard_map(
        functools.partial(body, tuple(mesh.axis_names)), mesh=mesh, in_specs=placed, out_specs=P("req", None, None, "tp"), check_vma=False
    )
```

```python
import functools
import math

import jax
import jax.numpy as jnp
from jax import lax
from jax.experimental import pallas as pl
from jax.experimental.pallas import tpu as pltpu
from jax.sharding import PartitionSpec as P

HD = 80
TILE = 256
MESH_IDS = pl.DeviceIdType.MESH


def project_kernel(order, ctx_ref, weight_ref, tokens_ref, out_ref, slots, send_sem, recv_sem):
    n = slots.shape[0]
    rows, width = ctx_ref.shape
    cols = out_ref.shape[1]
    me = lax.axis_index("tp")
    place = {"tp": me, "req": lax.axis_index("req")}

    def peer(k):
        where = dict(place, tp=lax.rem(me + k, n))
        return tuple(where[a] for a in order)

    barrier = pltpu.get_barrier_semaphore()
    for k in range(1, n):
        pl.semaphore_signal(barrier, inc=1, device_id=peer(k), device_id_type=MESH_IDS)
    pl.semaphore_wait(barrier, n - 1)
    copies = []
    for k in range(1, n):
        copy = pltpu.make_async_remote_copy(
            src_ref=ctx_ref,
            dst_ref=slots.at[k],
            send_sem=send_sem.at[k],
            recv_sem=recv_sem.at[k],
            device_id=peer(k),
            device_id_type=MESH_IDS,
        )
        copy.start()
        copies.append(copy)
    tile = 256

    def add_term(block, source, first):
        base = pl.multiple_of(source * width, 8)

        @pl.loop(0, rows // tile)
        def _(i):
            r = pl.ds(pl.multiple_of(i * tile, tile), tile)

            @pl.loop(0, cols // tile)
            def _(j):
                c = pl.ds(pl.multiple_of(j * tile, tile), tile)
                term = jnp.dot(
                    block[r, :], weight_ref[pl.ds(base, width), c], preferred_element_type=jnp.float32
                )
                term = term.astype(jnp.bfloat16).astype(jnp.float32)
                if first:
                    out_ref[r, c] = term
                else:
                    out_ref[r, c] = out_ref[r, c] + term

    add_term(ctx_ref, me, True)
    for k in range(1, n):
        copies[k - 1].wait_recv()
        add_term(slots.at[k], lax.rem(me - k + n, n), False)

    @pl.loop(0, rows // tile)
    def _(i):
        r = pl.ds(pl.multiple_of(i * tile, tile), tile)
        out_ref[r, :] = out_ref[r, :] + tokens_ref[r, :].astype(jnp.float32)

    for copy in copies:
        copy.wait_send()


def project(context, weight, tokens, order):
    n = weight.shape[0] // context.shape[1]
    rows, cols = tokens.shape
    return pl.pallas_call(
        functools.partial(project_kernel, order),
        out_shape=jax.ShapeDtypeStruct((rows, cols), jnp.float32),
        in_specs=[pl.BlockSpec(memory_space=pltpu.VMEM)] * 3,
        out_specs=pl.BlockSpec(memory_space=pltpu.VMEM),
        scratch_shapes=[
            pltpu.VMEM((n,) + context.shape, context.dtype),
            pltpu.SemaphoreType.DMA((n,)),
            pltpu.SemaphoreType.DMA((n,)),
        ],
        compiler_params=pltpu.CompilerParams(
            collective_id=0, has_side_effects=True, vmem_limit_bytes=48 * 1024 * 1024
        ),
        cost_estimate=pl.CostEstimate(
            flops=2 * rows * cols * weight.shape[0],
            bytes_accessed=4 * rows * cols + 2 * weight.size + 2 * rows * cols + 2 * n * context.size,
            transcendentals=0,
        ),
    )(context, weight, tokens)


def shifted_2(block, axis, distance):
    devices = range(lax.axis_size(axis))
    route = [(i - distance, i) for i in devices if i - distance in devices]
    return lax.ppermute(block, axis, route)


def layer_norm(stream, gain):
    center = jnp.mean(stream, axis=-1, keepdims=True)
    shifted = stream - center
    spread = jnp.mean(shifted * shifted, axis=-1, keepdims=True)
    return shifted * lax.rsqrt(spread + 1e-06) * gain.astype(jnp.float32)


def flash_kernel(bounds, q_ref, qm_ref, k_ref, v_ref, km_ref, o_ref):
    i = pl.program_id(0)
    tile = TILE
    factor = 1.0 / math.sqrt(HD)
    q = q_ref[...]
    qm = qm_ref[...]

    def step(j, carry):
        running_max, running_sum, weighted = carry
        start = pl.multiple_of(j * tile, tile)
        keys = k_ref[:, :, pl.ds(start, tile)]
        values = v_ref[:, pl.ds(start, tile), :]
        km = km_ref[:, pl.ds(start, tile)]
        scores = lax.dot_general(
            q, keys, (((2,), (1,)), ((0,), (0,))), preferred_element_type=jnp.float32
        ) * factor
        matches = (qm == km)[None]
        new_max = jnp.maximum(
            running_max, jnp.max(jnp.where(matches, scores, -1e30), axis=2, keepdims=True)
        )
        probs = jnp.where(matches, jnp.exp(scores - new_max), 0.0)
        shrink = jnp.exp(running_max - new_max)
        new_sum = running_sum * shrink + jnp.sum(probs, axis=2, keepdims=True)
        update = lax.dot_general(
            probs.astype(jnp.bfloat16), values, (((2,), (1,)), ((0,), (0,))),
            preferred_element_type=jnp.float32,
        )
        return new_max, new_sum, weighted * shrink + update

    heads, rows, width = q.shape
    init = (
        jnp.full((heads, rows, 1), -1e30, jnp.float32),
        jnp.zeros((heads, rows, 1), jnp.float32),
        jnp.zeros((heads, rows, width), jnp.float32),
    )
    _, total, weighted = lax.fori_loop(bounds[0, i], bounds[1, i], step, init)
    o_ref[...] = (weighted / total).astype(o_ref.dtype)


def attention(queries, query_marks, keys, values, key_marks):
    heads, rows, width = queries.shape
    key_rows = keys.shape[2]
    tiles = rows // TILE
    low = query_marks.reshape(tiles, TILE).min(axis=1)
    high = query_marks.reshape(tiles, TILE).max(axis=1)
    valid = (key_marks[None, :] >= low[:, None]) & (key_marks[None, :] <= high[:, None])
    first = jnp.argmax(valid, axis=1)
    last = key_rows - 1 - jnp.argmax(valid[:, ::-1], axis=1)
    bounds = jnp.stack([first // TILE, last // TILE + 1]).astype(jnp.int32)
    return pl.pallas_call(
        flash_kernel,
        out_shape=jax.ShapeDtypeStruct(queries.shape, queries.dtype),
        grid_spec=pltpu.PrefetchScalarGridSpec(
            num_scalar_prefetch=1,
            grid=(tiles,),
            in_specs=[
                pl.BlockSpec((heads, TILE, width), lambda i, b: (0, i, 0)),
                pl.BlockSpec((TILE, 1), lambda i, b: (i, 0)),
                pl.BlockSpec((heads, width, key_rows), lambda i, b: (0, 0, 0)),
                pl.BlockSpec((heads, key_rows, width), lambda i, b: (0, 0, 0)),
                pl.BlockSpec((1, key_rows), lambda i, b: (0, 0)),
            ],
            out_specs=pl.BlockSpec((heads, TILE, width), lambda i, b: (0, i, 0)),
        ),
        compiler_params=pltpu.CompilerParams(vmem_limit_bytes=48 * 1024 * 1024),
        cost_estimate=pl.CostEstimate(
            flops=4 * heads * rows * 2048 * width,
            bytes_accessed=2 * (queries.size * 2 + keys.size + values.size),
            transcendentals=heads * rows * 2048,
        ),
    )(bounds, queries, query_marks.reshape(rows, 1), keys, values, key_marks.reshape(1, key_rows))


def body(
    order,
    tokens,
    segments,
    attend_gain,
    attend_weight,
    output_weight,
    mixer_gain,
    expand_weight,
    reduce_weight,
    output_gain,
    merge_weight,
    merge_index,
    owners,
):
    token_rows = tokens.shape[0]
    head_width = attend_weight.shape[2]
    head_count = head_width // HD
    full_weight = lax.all_gather(output_weight, "tp", axis=0, tiled=True)
    stream = tokens.astype(jnp.float32)
    attend_in = layer_norm(stream, attend_gain).astype(jnp.bfloat16)
    projected = jnp.dot(
        attend_in,
        attend_weight.reshape(attend_weight.shape[0], 3 * head_width),
        preferred_element_type=jnp.float32,
    ).astype(jnp.bfloat16)
    key_value = projected[:, head_width:]
    marks = segments + 1
    near = {0: (key_value, marks)}
    for distance in (1, -1, 2, -2):
        near[distance] = shifted_2((key_value, marks), "req", distance)
    ordered = [near[d] for d in (2, 1, 0, -1, -2)]
    all_kv = jnp.concatenate([p for p, _ in ordered], axis=0)
    key_marks = jnp.concatenate([m for _, m in ordered], axis=0)

    def by_head(block):
        return jnp.transpose(block.reshape(block.shape[0], head_count, HD), (1, 0, 2))

    context = attention(
        by_head(projected[:, :head_width]),
        marks,
        jnp.transpose(all_kv[:, :head_width].reshape(-1, head_count, HD), (1, 2, 0)),
        by_head(all_kv[:, head_width:]),
        key_marks,
    )
    context = jnp.transpose(context, (1, 0, 2)).reshape(token_rows, head_width)
    middle = project(context, full_weight, tokens, order)
    mixer_in = layer_norm(middle, mixer_gain).astype(jnp.bfloat16)
    expanded = jax.nn.gelu(
        jnp.dot(mixer_in, expand_weight, preferred_element_type=jnp.float32), approximate=False
    ).astype(jnp.bfloat16)
    hidden_terms = jnp.dot(expanded, reduce_weight, preferred_element_type=jnp.float32)
    final_stream = middle + lax.psum(hidden_terms.astype(jnp.bfloat16), "tp").astype(jnp.float32)
    final_normed = layer_norm(final_stream, output_gain).astype(jnp.bfloat16)
    merged_rows = merge_index.shape[0]
    local_index = merge_index - lax.axis_index("req") * token_rows
    merged = jnp.take(final_normed, local_index.reshape(-1), axis=0).reshape(
        merged_rows, 4 * final_normed.shape[1]
    )
    feature = jnp.dot(merged, merge_weight, preferred_element_type=jnp.float32).astype(jnp.bfloat16)
    peers = lax.axis_size("req")
    capacity = 2 * merged_rows // peers
    target = owners[:, 0]
    choose = (target[:, None] == jnp.arange(peers, dtype=jnp.int32)[None, :]).astype(jnp.int32)
    slot = jnp.sum((jnp.cumsum(choose, axis=0) - 1) * choose, axis=1)
    position = target * capacity + slot
    placement = (
        position[:, None] == jnp.arange(peers * capacity, dtype=jnp.int32)[None, :]
    ).astype(jnp.bfloat16)
    outgoing = jnp.einsum(
        "ms,mc->sc", placement, feature, preferred_element_type=jnp.float32
    ).astype(jnp.bfloat16)
    outgoing = outgoing.reshape(peers, capacity, feature.shape[1])
    received = lax.all_to_all(outgoing, "req", split_axis=0, concat_axis=0, tiled=True)
    return received.reshape(1, peers, capacity, feature.shape[1])


def solution(mesh):
    placed = (
        P("req", None),
        P("req"),
        P(),
        P(None, None, "tp"),
        P("tp", None),
        P(),
        P(None, "tp"),
        P("tp", None),
        P(),
        P(None, "tp"),
        P("req", None),
        P("req", None),
    )
    return jax.shard_map(
        functools.partial(body, tuple(mesh.axis_names)), mesh=mesh, in_specs=placed, out_specs=P("req", None, None, "tp"), check_vma=False
    )
```

```python
import functools
import math

import jax
import jax.numpy as jnp
from jax import lax
from jax.experimental import pallas as pl
from jax.experimental.pallas import tpu as pltpu
from jax.sharding import PartitionSpec as P

HD = 80
TILE = 256
MESH_IDS = pl.DeviceIdType.MESH


def project_kernel(order, ctx_ref, weight_ref, tokens_ref, out_ref, slots, send_sem, recv_sem):
    n = slots.shape[0]
    rows, width = ctx_ref.shape
    cols = out_ref.shape[1]
    half = rows // 2
    me = lax.axis_index("tp")
    place = {"tp": me, "req": lax.axis_index("req")}

    def peer(k):
        where = dict(place, tp=lax.rem(me + k, n))
        return tuple(where[a] for a in order)

    def send(src, dst, sem, k):
        copy = pltpu.make_async_remote_copy(
            src_ref=src,
            dst_ref=dst,
            send_sem=send_sem.at[sem],
            recv_sem=recv_sem.at[sem],
            device_id=peer(k),
            device_id_type=MESH_IDS,
        )
        copy.start()
        return copy

    barrier = pltpu.get_barrier_semaphore()
    for k in (1, n - 1):
        pl.semaphore_signal(barrier, inc=1, device_id=peer(k), device_id_type=MESH_IDS)
    pl.semaphore_wait(barrier, 2)
    right = send(ctx_ref, slots.at[1], 1, 1)
    left = send(ctx_ref, slots.at[3], 3, n - 1)
    tile = 256

    def add_term(block, source, first):
        base = pl.multiple_of(source * width, 8)

        @pl.loop(0, rows // tile)
        def _(i):
            r = pl.ds(pl.multiple_of(i * tile, tile), tile)

            @pl.loop(0, cols // tile)
            def _(j):
                c = pl.ds(pl.multiple_of(j * tile, tile), tile)
                term = jnp.dot(
                    block[r, :], weight_ref[pl.ds(base, width), c], preferred_element_type=jnp.float32
                )
                term = term.astype(jnp.bfloat16).astype(jnp.float32)
                if first:
                    out_ref[r, c] = term
                else:
                    out_ref[r, c] = out_ref[r, c] + term

    add_term(ctx_ref, me, True)
    right.wait_recv()
    onward = send(slots.at[1, pl.ds(0, half)], slots.at[2, pl.ds(0, half)], 2, 1)
    add_term(slots.at[1], lax.rem(me + n - 1, n), False)
    left.wait_recv()
    backward = send(slots.at[3, pl.ds(half, half)], slots.at[2, pl.ds(half, half)], 0, n - 1)
    add_term(slots.at[3], lax.rem(me + 1, n), False)
    onward.wait_recv()
    backward.wait_recv()
    add_term(slots.at[2], lax.rem(me + 2, n), False)

    @pl.loop(0, rows // tile)
    def _(i):
        r = pl.ds(pl.multiple_of(i * tile, tile), tile)
        out_ref[r, :] = out_ref[r, :] + tokens_ref[r, :].astype(jnp.float32)

    for copy in (right, left, onward, backward):
        copy.wait_send()


def project(context, weight, tokens, order):
    n = weight.shape[0] // context.shape[1]
    rows, cols = tokens.shape
    return pl.pallas_call(
        functools.partial(project_kernel, order),
        out_shape=jax.ShapeDtypeStruct((rows, cols), jnp.float32),
        in_specs=[pl.BlockSpec(memory_space=pltpu.VMEM)] * 3,
        out_specs=pl.BlockSpec(memory_space=pltpu.VMEM),
        scratch_shapes=[
            pltpu.VMEM((n,) + context.shape, context.dtype),
            pltpu.SemaphoreType.DMA((n,)),
            pltpu.SemaphoreType.DMA((n,)),
        ],
        compiler_params=pltpu.CompilerParams(
            collective_id=0, has_side_effects=True, vmem_limit_bytes=48 * 1024 * 1024
        ),
        cost_estimate=pl.CostEstimate(
            flops=2 * rows * cols * weight.shape[0],
            bytes_accessed=4 * rows * cols + 2 * weight.size + 2 * rows * cols + 2 * n * context.size,
            transcendentals=0,
        ),
    )(context, weight, tokens)


def shifted_2(block, axis, distance):
    devices = range(lax.axis_size(axis))
    route = [(i - distance, i) for i in devices if i - distance in devices]
    return lax.ppermute(block, axis, route)


def layer_norm(stream, gain):
    center = jnp.mean(stream, axis=-1, keepdims=True)
    shifted = stream - center
    spread = jnp.mean(shifted * shifted, axis=-1, keepdims=True)
    return shifted * lax.rsqrt(spread + 1e-06) * gain.astype(jnp.float32)


def flash_kernel(bounds, q_ref, qm_ref, k_ref, v_ref, km_ref, o_ref):
    i = pl.program_id(0)
    tile = TILE
    factor = 1.0 / math.sqrt(HD)
    q = q_ref[...]
    qm = qm_ref[...]

    def step(j, carry):
        running_max, running_sum, weighted = carry
        start = pl.multiple_of(j * tile, tile)
        keys = k_ref[:, :, pl.ds(start, tile)]
        values = v_ref[:, pl.ds(start, tile), :]
        km = km_ref[:, pl.ds(start, tile)]
        scores = lax.dot_general(
            q, keys, (((2,), (1,)), ((0,), (0,))), preferred_element_type=jnp.float32
        ) * factor
        matches = (qm == km)[None]
        new_max = jnp.maximum(
            running_max, jnp.max(jnp.where(matches, scores, -1e30), axis=2, keepdims=True)
        )
        probs = jnp.where(matches, jnp.exp(scores - new_max), 0.0)
        shrink = jnp.exp(running_max - new_max)
        new_sum = running_sum * shrink + jnp.sum(probs, axis=2, keepdims=True)
        update = lax.dot_general(
            probs.astype(jnp.bfloat16), values, (((2,), (1,)), ((0,), (0,))),
            preferred_element_type=jnp.float32,
        )
        return new_max, new_sum, weighted * shrink + update

    heads, rows, width = q.shape
    init = (
        jnp.full((heads, rows, 1), -1e30, jnp.float32),
        jnp.zeros((heads, rows, 1), jnp.float32),
        jnp.zeros((heads, rows, width), jnp.float32),
    )
    _, total, weighted = lax.fori_loop(bounds[0, i], bounds[1, i], step, init)
    o_ref[...] = (weighted / total).astype(o_ref.dtype)


def attention(queries, query_marks, keys, values, key_marks):
    heads, rows, width = queries.shape
    key_rows = keys.shape[2]
    tiles = rows // TILE
    low = query_marks.reshape(tiles, TILE).min(axis=1)
    high = query_marks.reshape(tiles, TILE).max(axis=1)
    valid = (key_marks[None, :] >= low[:, None]) & (key_marks[None, :] <= high[:, None])
    first = jnp.argmax(valid, axis=1)
    last = key_rows - 1 - jnp.argmax(valid[:, ::-1], axis=1)
    bounds = jnp.stack([first // TILE, last // TILE + 1]).astype(jnp.int32)
    return pl.pallas_call(
        flash_kernel,
        out_shape=jax.ShapeDtypeStruct(queries.shape, queries.dtype),
        grid_spec=pltpu.PrefetchScalarGridSpec(
            num_scalar_prefetch=1,
            grid=(tiles,),
            in_specs=[
                pl.BlockSpec((heads, TILE, width), lambda i, b: (0, i, 0)),
                pl.BlockSpec((TILE, 1), lambda i, b: (i, 0)),
                pl.BlockSpec((heads, width, key_rows), lambda i, b: (0, 0, 0)),
                pl.BlockSpec((heads, key_rows, width), lambda i, b: (0, 0, 0)),
                pl.BlockSpec((1, key_rows), lambda i, b: (0, 0)),
            ],
            out_specs=pl.BlockSpec((heads, TILE, width), lambda i, b: (0, i, 0)),
        ),
        compiler_params=pltpu.CompilerParams(vmem_limit_bytes=48 * 1024 * 1024),
        cost_estimate=pl.CostEstimate(
            flops=4 * heads * rows * 2048 * width,
            bytes_accessed=2 * (queries.size * 2 + keys.size + values.size),
            transcendentals=heads * rows * 2048,
        ),
    )(bounds, queries, query_marks.reshape(rows, 1), keys, values, key_marks.reshape(1, key_rows))


def body(
    order,
    tokens,
    segments,
    attend_gain,
    attend_weight,
    output_weight,
    mixer_gain,
    expand_weight,
    reduce_weight,
    output_gain,
    merge_weight,
    merge_index,
    owners,
):
    token_rows = tokens.shape[0]
    head_width = attend_weight.shape[2]
    head_count = head_width // HD
    full_weight = lax.all_gather(output_weight, "tp", axis=0, tiled=True)
    stream = tokens.astype(jnp.float32)
    attend_in = layer_norm(stream, attend_gain).astype(jnp.bfloat16)
    projected = jnp.dot(
        attend_in,
        attend_weight.reshape(attend_weight.shape[0], 3 * head_width),
        preferred_element_type=jnp.float32,
    ).astype(jnp.bfloat16)
    key_value = projected[:, head_width:]
    marks = segments + 1
    near = {0: (key_value, marks)}
    for distance in (1, -1, 2, -2):
        near[distance] = shifted_2((key_value, marks), "req", distance)
    ordered = [near[d] for d in (2, 1, 0, -1, -2)]
    all_kv = jnp.concatenate([p for p, _ in ordered], axis=0)
    key_marks = jnp.concatenate([m for _, m in ordered], axis=0)

    def by_head(block):
        return jnp.transpose(block.reshape(block.shape[0], head_count, HD), (1, 0, 2))

    context = attention(
        by_head(projected[:, :head_width]),
        marks,
        jnp.transpose(all_kv[:, :head_width].reshape(-1, head_count, HD), (1, 2, 0)),
        by_head(all_kv[:, head_width:]),
        key_marks,
    )
    context = jnp.transpose(context, (1, 0, 2)).reshape(token_rows, head_width)
    middle = project(context, full_weight, tokens, order)
    mixer_in = layer_norm(middle, mixer_gain).astype(jnp.bfloat16)
    expanded = jax.nn.gelu(
        jnp.dot(mixer_in, expand_weight, preferred_element_type=jnp.float32), approximate=False
    ).astype(jnp.bfloat16)
    hidden_terms = jnp.dot(expanded, reduce_weight, preferred_element_type=jnp.float32)
    final_stream = middle + lax.psum(hidden_terms.astype(jnp.bfloat16), "tp").astype(jnp.float32)
    final_normed = layer_norm(final_stream, output_gain).astype(jnp.bfloat16)
    merged_rows = merge_index.shape[0]
    local_index = merge_index - lax.axis_index("req") * token_rows
    merged = jnp.take(final_normed, local_index.reshape(-1), axis=0).reshape(
        merged_rows, 4 * final_normed.shape[1]
    )
    feature = jnp.dot(merged, merge_weight, preferred_element_type=jnp.float32).astype(jnp.bfloat16)
    peers = lax.axis_size("req")
    capacity = 2 * merged_rows // peers
    target = owners[:, 0]
    choose = (target[:, None] == jnp.arange(peers, dtype=jnp.int32)[None, :]).astype(jnp.int32)
    slot = jnp.sum((jnp.cumsum(choose, axis=0) - 1) * choose, axis=1)
    position = target * capacity + slot
    placement = (
        position[:, None] == jnp.arange(peers * capacity, dtype=jnp.int32)[None, :]
    ).astype(jnp.bfloat16)
    outgoing = jnp.einsum(
        "ms,mc->sc", placement, feature, preferred_element_type=jnp.float32
    ).astype(jnp.bfloat16)
    outgoing = outgoing.reshape(peers, capacity, feature.shape[1])
    received = lax.all_to_all(outgoing, "req", split_axis=0, concat_axis=0, tiled=True)
    return received.reshape(1, peers, capacity, feature.shape[1])


def solution(mesh):
    placed = (
        P("req", None),
        P("req"),
        P(),
        P(None, None, "tp"),
        P("tp", None),
        P(),
        P(None, "tp"),
        P("tp", None),
        P(),
        P(None, "tp"),
        P("req", None),
        P("req", None),
    )
    return jax.shard_map(
        functools.partial(body, tuple(mesh.axis_names)), mesh=mesh, in_specs=placed, out_specs=P("req", None, None, "tp"), check_vma=False
    )
```

```python
import functools
import math

import jax
import jax.numpy as jnp
from jax import lax
from jax.experimental import pallas as pl
from jax.experimental.pallas import tpu as pltpu
from jax.sharding import PartitionSpec as P

HD = 80
TILE = 256
NEAR = (1, -1, 2, -2)
MESH_IDS = pl.DeviceIdType.MESH


def project_kernel(order, ctx_ref, weight_ref, tokens_ref, out_ref, slots, send_sem, recv_sem):
    n = slots.shape[0]
    rows, width = ctx_ref.shape
    cols = out_ref.shape[1]
    half = rows // 2
    me = lax.axis_index("tp")
    place = {"tp": me, "req": lax.axis_index("req")}

    def peer(k):
        where = dict(place, tp=lax.rem(me + k, n))
        return tuple(where[a] for a in order)

    def send(src, dst, sem, k):
        copy = pltpu.make_async_remote_copy(
            src_ref=src,
            dst_ref=dst,
            send_sem=send_sem.at[sem],
            recv_sem=recv_sem.at[sem],
            device_id=peer(k),
            device_id_type=MESH_IDS,
        )
        copy.start()
        return copy

    barrier = pltpu.get_barrier_semaphore()
    for k in (1, n - 1):
        pl.semaphore_signal(barrier, inc=1, device_id=peer(k), device_id_type=MESH_IDS)
    pl.semaphore_wait(barrier, 2)
    right = send(ctx_ref, slots.at[1], 1, 1)
    left = send(ctx_ref, slots.at[3], 3, n - 1)
    tile = 256

    def add_term(block, source, first):
        base = pl.multiple_of(source * width, 8)

        @pl.loop(0, rows // tile)
        def _(i):
            r = pl.ds(pl.multiple_of(i * tile, tile), tile)

            @pl.loop(0, cols // tile)
            def _(j):
                c = pl.ds(pl.multiple_of(j * tile, tile), tile)
                term = jnp.dot(
                    block[r, :], weight_ref[pl.ds(base, width), c], preferred_element_type=jnp.float32
                )
                term = term.astype(jnp.bfloat16).astype(jnp.float32)
                if first:
                    out_ref[r, c] = term
                else:
                    out_ref[r, c] = out_ref[r, c] + term

    add_term(ctx_ref, me, True)
    right.wait_recv()
    onward = send(slots.at[1, pl.ds(0, half)], slots.at[2, pl.ds(0, half)], 2, 1)
    add_term(slots.at[1], lax.rem(me + n - 1, n), False)
    left.wait_recv()
    backward = send(slots.at[3, pl.ds(half, half)], slots.at[2, pl.ds(half, half)], 0, n - 1)
    add_term(slots.at[3], lax.rem(me + 1, n), False)
    onward.wait_recv()
    backward.wait_recv()
    add_term(slots.at[2], lax.rem(me + 2, n), False)

    @pl.loop(0, rows // tile)
    def _(i):
        r = pl.ds(pl.multiple_of(i * tile, tile), tile)
        out_ref[r, :] = out_ref[r, :] + tokens_ref[r, :].astype(jnp.float32)

    for copy in (right, left, onward, backward):
        copy.wait_send()


def exchange_kernel(order, n, keys_ref, values_ref, marks_ref, keys_out, values_out, marks_out,
                    send_sem, recv_sem, local_sem):
    me = lax.axis_index("req")
    place = {"req": me, "tp": lax.axis_index("tp")}
    span = marks_ref.shape[1]

    def peer(d):
        where = dict(place, req=lax.rem(me + d + n, n))
        return tuple(where[a] for a in order)

    def windows(slot):
        part = pl.ds(slot * span, span)
        return (keys_out.at[:, :, part], values_out.at[:, part, :], marks_out.at[:, part])

    sources = (keys_ref, values_ref, marks_ref)
    barrier = pltpu.get_barrier_semaphore()
    for d in NEAR:
        pl.semaphore_signal(barrier, inc=1, device_id=peer(d), device_id_type=MESH_IDS)
    pl.semaphore_wait(barrier, len(NEAR))
    copies = []
    for index, d in enumerate(NEAR):
        for a, (src, dst) in enumerate(zip(sources, windows(2 - d))):
            copy = pltpu.make_async_remote_copy(
                src_ref=src,
                dst_ref=dst,
                send_sem=send_sem.at[3 * index + a],
                recv_sem=recv_sem.at[3 * index + a],
                device_id=peer(d),
                device_id_type=MESH_IDS,
            )
            copy.start()
            copies.append(copy)
    local = []
    for a, (src, dst) in enumerate(zip(sources, windows(2))):
        copy = pltpu.make_async_copy(src, dst, local_sem.at[a])
        copy.start()
        local.append(copy)
    for copy in local:
        copy.wait()
    for copy in copies:
        copy.wait()


def exchange(keys, values, marks, order):
    n = lax.axis_size("req")
    slots = 2 * max(NEAR) + 1
    heads, width, span = keys.shape
    any_spec = pl.BlockSpec(memory_space=pl.ANY)
    keys_all, values_all, marks_all = pl.pallas_call(
        functools.partial(exchange_kernel, order, n),
        out_shape=(
            jax.ShapeDtypeStruct((heads, width, slots * span), keys.dtype),
            jax.ShapeDtypeStruct((heads, slots * span, width), values.dtype),
            jax.ShapeDtypeStruct((1, slots * span), marks.dtype),
        ),
        in_specs=[any_spec] * 3,
        out_specs=(any_spec, any_spec, any_spec),
        scratch_shapes=[
            pltpu.SemaphoreType.DMA((3 * len(NEAR),)),
            pltpu.SemaphoreType.DMA((3 * len(NEAR),)),
            pltpu.SemaphoreType.DMA((3,)),
        ],
        compiler_params=pltpu.CompilerParams(collective_id=1, has_side_effects=True),
    )(keys, values, marks.reshape(1, span))
    source = lax.axis_index("req") + jnp.arange(slots * span, dtype=jnp.int32) // span - max(NEAR)
    present = (source >= 0) & (source < n)
    return keys_all, values_all, jnp.where(present, marks_all[0], 0)


def project(context, weight, tokens, order):
    n = weight.shape[0] // context.shape[1]
    rows, cols = tokens.shape
    return pl.pallas_call(
        functools.partial(project_kernel, order),
        out_shape=jax.ShapeDtypeStruct((rows, cols), jnp.float32),
        in_specs=[pl.BlockSpec(memory_space=pltpu.VMEM)] * 3,
        out_specs=pl.BlockSpec(memory_space=pltpu.VMEM),
        scratch_shapes=[
            pltpu.VMEM((n,) + context.shape, context.dtype),
            pltpu.SemaphoreType.DMA((n,)),
            pltpu.SemaphoreType.DMA((n,)),
        ],
        compiler_params=pltpu.CompilerParams(
            collective_id=0, has_side_effects=True, vmem_limit_bytes=48 * 1024 * 1024
        ),
        cost_estimate=pl.CostEstimate(
            flops=2 * rows * cols * weight.shape[0],
            bytes_accessed=4 * rows * cols + 2 * weight.size + 2 * rows * cols + 2 * n * context.size,
            transcendentals=0,
        ),
    )(context, weight, tokens)


def shifted_2(block, axis, distance):
    devices = range(lax.axis_size(axis))
    route = [(i - distance, i) for i in devices if i - distance in devices]
    return lax.ppermute(block, axis, route)


def layer_norm(stream, gain):
    center = jnp.mean(stream, axis=-1, keepdims=True)
    shifted = stream - center
    spread = jnp.mean(shifted * shifted, axis=-1, keepdims=True)
    return shifted * lax.rsqrt(spread + 1e-06) * gain.astype(jnp.float32)


def flash_kernel(bounds, q_ref, qm_ref, k_ref, v_ref, km_ref, o_ref):
    i = pl.program_id(0)
    tile = TILE
    factor = 1.0 / math.sqrt(HD)
    q = q_ref[...]
    qm = qm_ref[...]

    def step(j, carry):
        running_max, running_sum, weighted = carry
        start = pl.multiple_of(j * tile, tile)
        keys = k_ref[:, :, pl.ds(start, tile)]
        values = v_ref[:, pl.ds(start, tile), :]
        km = km_ref[:, pl.ds(start, tile)]
        scores = lax.dot_general(
            q, keys, (((2,), (1,)), ((0,), (0,))), preferred_element_type=jnp.float32
        ) * factor
        matches = (qm == km)[None]
        new_max = jnp.maximum(
            running_max, jnp.max(jnp.where(matches, scores, -1e30), axis=2, keepdims=True)
        )
        probs = jnp.where(matches, jnp.exp(scores - new_max), 0.0)
        shrink = jnp.exp(running_max - new_max)
        new_sum = running_sum * shrink + jnp.sum(probs, axis=2, keepdims=True)
        update = lax.dot_general(
            probs.astype(jnp.bfloat16), values, (((2,), (1,)), ((0,), (0,))),
            preferred_element_type=jnp.float32,
        )
        return new_max, new_sum, weighted * shrink + update

    heads, rows, width = q.shape
    init = (
        jnp.full((heads, rows, 1), -1e30, jnp.float32),
        jnp.zeros((heads, rows, 1), jnp.float32),
        jnp.zeros((heads, rows, width), jnp.float32),
    )
    _, total, weighted = lax.fori_loop(bounds[0, i], bounds[1, i], step, init)
    o_ref[...] = (weighted / total).astype(o_ref.dtype)


def attention(queries, query_marks, keys, values, key_marks):
    heads, rows, width = queries.shape
    key_rows = keys.shape[2]
    tiles = rows // TILE
    low = query_marks.reshape(tiles, TILE).min(axis=1)
    high = query_marks.reshape(tiles, TILE).max(axis=1)
    valid = (key_marks[None, :] >= low[:, None]) & (key_marks[None, :] <= high[:, None])
    first = jnp.argmax(valid, axis=1)
    last = key_rows - 1 - jnp.argmax(valid[:, ::-1], axis=1)
    bounds = jnp.stack([first // TILE, last // TILE + 1]).astype(jnp.int32)
    return pl.pallas_call(
        flash_kernel,
        out_shape=jax.ShapeDtypeStruct(queries.shape, queries.dtype),
        grid_spec=pltpu.PrefetchScalarGridSpec(
            num_scalar_prefetch=1,
            grid=(tiles,),
            in_specs=[
                pl.BlockSpec((heads, TILE, width), lambda i, b: (0, i, 0)),
                pl.BlockSpec((TILE, 1), lambda i, b: (i, 0)),
                pl.BlockSpec((heads, width, key_rows), lambda i, b: (0, 0, 0)),
                pl.BlockSpec((heads, key_rows, width), lambda i, b: (0, 0, 0)),
                pl.BlockSpec((1, key_rows), lambda i, b: (0, 0)),
            ],
            out_specs=pl.BlockSpec((heads, TILE, width), lambda i, b: (0, i, 0)),
        ),
        compiler_params=pltpu.CompilerParams(vmem_limit_bytes=48 * 1024 * 1024),
        cost_estimate=pl.CostEstimate(
            flops=4 * heads * rows * 2048 * width,
            bytes_accessed=2 * (queries.size * 2 + keys.size + values.size),
            transcendentals=heads * rows * 2048,
        ),
    )(bounds, queries, query_marks.reshape(rows, 1), keys, values, key_marks.reshape(1, key_rows))


def body(
    order,
    tokens,
    segments,
    attend_gain,
    attend_weight,
    output_weight,
    mixer_gain,
    expand_weight,
    reduce_weight,
    output_gain,
    merge_weight,
    merge_index,
    owners,
):
    token_rows = tokens.shape[0]
    head_width = attend_weight.shape[2]
    head_count = head_width // HD
    full_weight = lax.all_gather(output_weight, "tp", axis=0, tiled=True)
    stream = tokens.astype(jnp.float32)
    attend_in = layer_norm(stream, attend_gain).astype(jnp.bfloat16)
    projected = jnp.dot(
        attend_in,
        attend_weight.reshape(attend_weight.shape[0], 3 * head_width),
        preferred_element_type=jnp.float32,
    ).astype(jnp.bfloat16)
    marks = segments + 1

    def by_head(block):
        return jnp.transpose(block.reshape(block.shape[0], head_count, HD), (1, 0, 2))

    keys_all, values_all, key_marks = exchange(
        jnp.transpose(projected[:, head_width : 2 * head_width].reshape(-1, head_count, HD), (1, 2, 0)),
        by_head(projected[:, 2 * head_width :]),
        marks,
        order,
    )
    context = attention(by_head(projected[:, :head_width]), marks, keys_all, values_all, key_marks)
    context = jnp.transpose(context, (1, 0, 2)).reshape(token_rows, head_width)
    middle = project(context, full_weight, tokens, order)
    mixer_in = layer_norm(middle, mixer_gain).astype(jnp.bfloat16)
    expanded = jax.nn.gelu(
        jnp.dot(mixer_in, expand_weight, preferred_element_type=jnp.float32), approximate=False
    ).astype(jnp.bfloat16)
    hidden_terms = jnp.dot(expanded, reduce_weight, preferred_element_type=jnp.float32)
    final_stream = middle + lax.psum(hidden_terms.astype(jnp.bfloat16), "tp").astype(jnp.float32)
    final_normed = layer_norm(final_stream, output_gain).astype(jnp.bfloat16)
    merged_rows = merge_index.shape[0]
    local_index = merge_index - lax.axis_index("req") * token_rows
    merged = jnp.take(final_normed, local_index.reshape(-1), axis=0).reshape(
        merged_rows, 4 * final_normed.shape[1]
    )
    feature = jnp.dot(merged, merge_weight, preferred_element_type=jnp.float32).astype(jnp.bfloat16)
    peers = lax.axis_size("req")
    capacity = 2 * merged_rows // peers
    target = owners[:, 0]
    choose = (target[:, None] == jnp.arange(peers, dtype=jnp.int32)[None, :]).astype(jnp.int32)
    slot = jnp.sum((jnp.cumsum(choose, axis=0) - 1) * choose, axis=1)
    position = target * capacity + slot
    placement = (
        position[:, None] == jnp.arange(peers * capacity, dtype=jnp.int32)[None, :]
    ).astype(jnp.bfloat16)
    outgoing = jnp.einsum(
        "ms,mc->sc", placement, feature, preferred_element_type=jnp.float32
    ).astype(jnp.bfloat16)
    outgoing = outgoing.reshape(peers, capacity, feature.shape[1])
    received = lax.all_to_all(outgoing, "req", split_axis=0, concat_axis=0, tiled=True)
    return received.reshape(1, peers, capacity, feature.shape[1])


def solution(mesh):
    placed = (
        P("req", None),
        P("req"),
        P(),
        P(None, None, "tp"),
        P("tp", None),
        P(),
        P(None, "tp"),
        P("tp", None),
        P(),
        P(None, "tp"),
        P("req", None),
        P("req", None),
    )
    return jax.shard_map(
        functools.partial(body, tuple(mesh.axis_names)), mesh=mesh, in_specs=placed, out_specs=P("req", None, None, "tp"), check_vma=False
    )
```

```python
import functools
import math

import jax
import jax.numpy as jnp
from jax import lax
from jax.experimental import pallas as pl
from jax.experimental.pallas import tpu as pltpu
from jax.sharding import PartitionSpec as P

HD = 80
TILE = 256
NEAR = (1, -1, 2, -2)
MESH_IDS = pl.DeviceIdType.MESH


def project_kernel(order, ctx_ref, weight_ref, tokens_ref, out_ref, slots, send_sem, recv_sem):
    n = slots.shape[0]
    rows, width = ctx_ref.shape
    cols = out_ref.shape[1]
    half = rows // 2
    me = lax.axis_index("tp")
    place = {"tp": me, "req": lax.axis_index("req")}

    def peer(k):
        where = dict(place, tp=lax.rem(me + k, n))
        return tuple(where[a] for a in order)

    def send(src, dst, sem, k):
        copy = pltpu.make_async_remote_copy(
            src_ref=src,
            dst_ref=dst,
            send_sem=send_sem.at[sem],
            recv_sem=recv_sem.at[sem],
            device_id=peer(k),
            device_id_type=MESH_IDS,
        )
        copy.start()
        return copy

    barrier = pltpu.get_barrier_semaphore()
    for k in (1, n - 1):
        pl.semaphore_signal(barrier, inc=1, device_id=peer(k), device_id_type=MESH_IDS)
    pl.semaphore_wait(barrier, 2)
    right = send(ctx_ref, slots.at[1], 1, 1)
    left = send(ctx_ref, slots.at[3], 3, n - 1)
    tile = 256

    def add_term(block, source, first):
        base = pl.multiple_of(source * width, 8)

        @pl.loop(0, rows // tile)
        def _(i):
            r = pl.ds(pl.multiple_of(i * tile, tile), tile)

            @pl.loop(0, cols // tile)
            def _(j):
                c = pl.ds(pl.multiple_of(j * tile, tile), tile)
                term = jnp.dot(
                    block[r, :], weight_ref[pl.ds(base, width), c], preferred_element_type=jnp.float32
                )
                term = term.astype(jnp.bfloat16).astype(jnp.float32)
                if first:
                    out_ref[r, c] = term
                else:
                    out_ref[r, c] = out_ref[r, c] + term

    add_term(ctx_ref, me, True)
    right.wait_recv()
    onward = send(slots.at[1, pl.ds(0, half)], slots.at[2, pl.ds(0, half)], 2, 1)
    add_term(slots.at[1], lax.rem(me + n - 1, n), False)
    left.wait_recv()
    backward = send(slots.at[3, pl.ds(half, half)], slots.at[2, pl.ds(half, half)], 0, n - 1)
    add_term(slots.at[3], lax.rem(me + 1, n), False)
    onward.wait_recv()
    backward.wait_recv()
    add_term(slots.at[2], lax.rem(me + 2, n), False)

    @pl.loop(0, rows // tile)
    def _(i):
        r = pl.ds(pl.multiple_of(i * tile, tile), tile)
        out_ref[r, :] = out_ref[r, :] + tokens_ref[r, :].astype(jnp.float32)

    for copy in (right, left, onward, backward):
        copy.wait_send()


def exchange_kernel(order, n, keys_ref, values_ref, marks_ref, keys_out, values_out, marks_out,
                    send_sem, recv_sem, local_sem):
    me = lax.axis_index("req")
    place = {"req": me, "tp": lax.axis_index("tp")}
    span = marks_ref.shape[1]

    def peer(d):
        where = dict(place, req=lax.rem(me + d + n, n))
        return tuple(where[a] for a in order)

    def windows(slot):
        part = pl.ds(slot * span, span)
        return (keys_out.at[:, :, part], values_out.at[:, part, :], marks_out.at[:, part])

    sources = (keys_ref, values_ref, marks_ref)
    barrier = pltpu.get_barrier_semaphore()
    for d in NEAR:
        pl.semaphore_signal(barrier, inc=1, device_id=peer(d), device_id_type=MESH_IDS)
    pl.semaphore_wait(barrier, len(NEAR))
    odd = lax.rem(me, 2)

    def send(kind, slices, targets, d):
        out = []
        for a, (src, dst) in enumerate(zip(slices, targets)):
            copy = pltpu.make_async_remote_copy(
                src_ref=src,
                dst_ref=dst,
                send_sem=send_sem.at[3 * kind + a],
                recv_sem=recv_sem.at[3 * kind + a],
                device_id=peer(d),
                device_id_type=MESH_IDS,
            )
            copy.start()
            out.append(copy)
        return out

    right = send(0, sources, windows(1), 1)
    left = send(1, sources, windows(3), -1)
    far = send(2, sources, windows(4 * odd), 2 - 4 * odd)
    local = []
    for a, (src, dst) in enumerate(zip(sources, windows(2))):
        copy = pltpu.make_async_copy(src, dst, local_sem.at[a])
        copy.start()
        local.append(copy)
    for a in range(3):
        right[a].wait_recv()
        left[a].wait_recv()
    relay = send(3, windows(1 + 2 * odd), windows(4 * odd), 1 - 2 * odd)
    for copy in local:
        copy.wait()
    for copy in right + left:
        copy.wait_send()
    for copy in far + relay:
        copy.wait()


def exchange(keys, values, marks, order):
    n = lax.axis_size("req")
    slots = 2 * max(NEAR) + 1
    heads, width, span = keys.shape
    any_spec = pl.BlockSpec(memory_space=pl.ANY)
    keys_all, values_all, marks_all = pl.pallas_call(
        functools.partial(exchange_kernel, order, n),
        out_shape=(
            jax.ShapeDtypeStruct((heads, width, slots * span), keys.dtype),
            jax.ShapeDtypeStruct((heads, slots * span, width), values.dtype),
            jax.ShapeDtypeStruct((1, slots * span), marks.dtype),
        ),
        in_specs=[any_spec] * 3,
        out_specs=(any_spec, any_spec, any_spec),
        scratch_shapes=[
            pltpu.SemaphoreType.DMA((12,)),
            pltpu.SemaphoreType.DMA((12,)),
            pltpu.SemaphoreType.DMA((3,)),
        ],
        compiler_params=pltpu.CompilerParams(collective_id=1, has_side_effects=True),
    )(keys, values, marks.reshape(1, span))
    source = lax.axis_index("req") + jnp.arange(slots * span, dtype=jnp.int32) // span - max(NEAR)
    present = (source >= 0) & (source < n)
    return keys_all, values_all, jnp.where(present, marks_all[0], 0)


def project(context, weight, tokens, order):
    n = weight.shape[0] // context.shape[1]
    rows, cols = tokens.shape
    return pl.pallas_call(
        functools.partial(project_kernel, order),
        out_shape=jax.ShapeDtypeStruct((rows, cols), jnp.float32),
        in_specs=[pl.BlockSpec(memory_space=pltpu.VMEM)] * 3,
        out_specs=pl.BlockSpec(memory_space=pltpu.VMEM),
        scratch_shapes=[
            pltpu.VMEM((n,) + context.shape, context.dtype),
            pltpu.SemaphoreType.DMA((n,)),
            pltpu.SemaphoreType.DMA((n,)),
        ],
        compiler_params=pltpu.CompilerParams(
            collective_id=0, has_side_effects=True, vmem_limit_bytes=48 * 1024 * 1024
        ),
        cost_estimate=pl.CostEstimate(
            flops=2 * rows * cols * weight.shape[0],
            bytes_accessed=4 * rows * cols + 2 * weight.size + 2 * rows * cols + 2 * n * context.size,
            transcendentals=0,
        ),
    )(context, weight, tokens)


def shifted_2(block, axis, distance):
    devices = range(lax.axis_size(axis))
    route = [(i - distance, i) for i in devices if i - distance in devices]
    return lax.ppermute(block, axis, route)


def layer_norm(stream, gain):
    center = jnp.mean(stream, axis=-1, keepdims=True)
    shifted = stream - center
    spread = jnp.mean(shifted * shifted, axis=-1, keepdims=True)
    return shifted * lax.rsqrt(spread + 1e-06) * gain.astype(jnp.float32)


def flash_kernel(bounds, q_ref, qm_ref, k_ref, v_ref, km_ref, o_ref):
    i = pl.program_id(0)
    tile = TILE
    factor = 1.0 / math.sqrt(HD)
    q = q_ref[...]
    qm = qm_ref[...]

    def step(j, carry):
        running_max, running_sum, weighted = carry
        start = pl.multiple_of(j * tile, tile)
        keys = k_ref[:, :, pl.ds(start, tile)]
        values = v_ref[:, pl.ds(start, tile), :]
        km = km_ref[:, pl.ds(start, tile)]
        scores = lax.dot_general(
            q, keys, (((2,), (1,)), ((0,), (0,))), preferred_element_type=jnp.float32
        ) * factor
        matches = (qm == km)[None]
        new_max = jnp.maximum(
            running_max, jnp.max(jnp.where(matches, scores, -1e30), axis=2, keepdims=True)
        )
        probs = jnp.where(matches, jnp.exp(scores - new_max), 0.0)
        shrink = jnp.exp(running_max - new_max)
        new_sum = running_sum * shrink + jnp.sum(probs, axis=2, keepdims=True)
        update = lax.dot_general(
            probs.astype(jnp.bfloat16), values, (((2,), (1,)), ((0,), (0,))),
            preferred_element_type=jnp.float32,
        )
        return new_max, new_sum, weighted * shrink + update

    heads, rows, width = q.shape
    init = (
        jnp.full((heads, rows, 1), -1e30, jnp.float32),
        jnp.zeros((heads, rows, 1), jnp.float32),
        jnp.zeros((heads, rows, width), jnp.float32),
    )
    _, total, weighted = lax.fori_loop(bounds[0, i], bounds[1, i], step, init)
    o_ref[...] = (weighted / total).astype(o_ref.dtype)


def attention(queries, query_marks, keys, values, key_marks):
    heads, rows, width = queries.shape
    key_rows = keys.shape[2]
    tiles = rows // TILE
    low = query_marks.reshape(tiles, TILE).min(axis=1)
    high = query_marks.reshape(tiles, TILE).max(axis=1)
    valid = (key_marks[None, :] >= low[:, None]) & (key_marks[None, :] <= high[:, None])
    first = jnp.argmax(valid, axis=1)
    last = key_rows - 1 - jnp.argmax(valid[:, ::-1], axis=1)
    bounds = jnp.stack([first // TILE, last // TILE + 1]).astype(jnp.int32)
    return pl.pallas_call(
        flash_kernel,
        out_shape=jax.ShapeDtypeStruct(queries.shape, queries.dtype),
        grid_spec=pltpu.PrefetchScalarGridSpec(
            num_scalar_prefetch=1,
            grid=(tiles,),
            in_specs=[
                pl.BlockSpec((heads, TILE, width), lambda i, b: (0, i, 0)),
                pl.BlockSpec((TILE, 1), lambda i, b: (i, 0)),
                pl.BlockSpec((heads, width, key_rows), lambda i, b: (0, 0, 0)),
                pl.BlockSpec((heads, key_rows, width), lambda i, b: (0, 0, 0)),
                pl.BlockSpec((1, key_rows), lambda i, b: (0, 0)),
            ],
            out_specs=pl.BlockSpec((heads, TILE, width), lambda i, b: (0, i, 0)),
        ),
        compiler_params=pltpu.CompilerParams(vmem_limit_bytes=48 * 1024 * 1024),
        cost_estimate=pl.CostEstimate(
            flops=4 * heads * rows * 2048 * width,
            bytes_accessed=2 * (queries.size * 2 + keys.size + values.size),
            transcendentals=heads * rows * 2048,
        ),
    )(bounds, queries, query_marks.reshape(rows, 1), keys, values, key_marks.reshape(1, key_rows))


def body(
    order,
    tokens,
    segments,
    attend_gain,
    attend_weight,
    output_weight,
    mixer_gain,
    expand_weight,
    reduce_weight,
    output_gain,
    merge_weight,
    merge_index,
    owners,
):
    token_rows = tokens.shape[0]
    head_width = attend_weight.shape[2]
    head_count = head_width // HD
    full_weight = lax.all_gather(output_weight, "tp", axis=0, tiled=True)
    stream = tokens.astype(jnp.float32)
    attend_in = layer_norm(stream, attend_gain).astype(jnp.bfloat16)
    projected = jnp.dot(
        attend_in,
        attend_weight.reshape(attend_weight.shape[0], 3 * head_width),
        preferred_element_type=jnp.float32,
    ).astype(jnp.bfloat16)
    marks = segments + 1

    def by_head(block):
        return jnp.transpose(block.reshape(block.shape[0], head_count, HD), (1, 0, 2))

    keys_all, values_all, key_marks = exchange(
        jnp.transpose(projected[:, head_width : 2 * head_width].reshape(-1, head_count, HD), (1, 2, 0)),
        by_head(projected[:, 2 * head_width :]),
        marks,
        order,
    )
    context = attention(by_head(projected[:, :head_width]), marks, keys_all, values_all, key_marks)
    context = jnp.transpose(context, (1, 0, 2)).reshape(token_rows, head_width)
    middle = project(context, full_weight, tokens, order)
    mixer_in = layer_norm(middle, mixer_gain).astype(jnp.bfloat16)
    expanded = jax.nn.gelu(
        jnp.dot(mixer_in, expand_weight, preferred_element_type=jnp.float32), approximate=False
    ).astype(jnp.bfloat16)
    hidden_terms = jnp.dot(expanded, reduce_weight, preferred_element_type=jnp.float32)
    final_stream = middle + lax.psum(hidden_terms.astype(jnp.bfloat16), "tp").astype(jnp.float32)
    final_normed = layer_norm(final_stream, output_gain).astype(jnp.bfloat16)
    merged_rows = merge_index.shape[0]
    local_index = merge_index - lax.axis_index("req") * token_rows
    merged = jnp.take(final_normed, local_index.reshape(-1), axis=0).reshape(
        merged_rows, 4 * final_normed.shape[1]
    )
    feature = jnp.dot(merged, merge_weight, preferred_element_type=jnp.float32).astype(jnp.bfloat16)
    peers = lax.axis_size("req")
    capacity = 2 * merged_rows // peers
    target = owners[:, 0]
    choose = (target[:, None] == jnp.arange(peers, dtype=jnp.int32)[None, :]).astype(jnp.int32)
    slot = jnp.sum((jnp.cumsum(choose, axis=0) - 1) * choose, axis=1)
    position = target * capacity + slot
    placement = (
        position[:, None] == jnp.arange(peers * capacity, dtype=jnp.int32)[None, :]
    ).astype(jnp.bfloat16)
    outgoing = jnp.einsum(
        "ms,mc->sc", placement, feature, preferred_element_type=jnp.float32
    ).astype(jnp.bfloat16)
    outgoing = outgoing.reshape(peers, capacity, feature.shape[1])
    received = lax.all_to_all(outgoing, "req", split_axis=0, concat_axis=0, tiled=True)
    return received.reshape(1, peers, capacity, feature.shape[1])


def solution(mesh):
    placed = (
        P("req", None),
        P("req"),
        P(),
        P(None, None, "tp"),
        P("tp", None),
        P(),
        P(None, "tp"),
        P("tp", None),
        P(),
        P(None, "tp"),
        P("req", None),
        P("req", None),
    )
    return jax.shard_map(
        functools.partial(body, tuple(mesh.axis_names)), mesh=mesh, in_specs=placed, out_specs=P("req", None, None, "tp"), check_vma=False
    )
```

```python
import functools
import math

import jax
import jax.numpy as jnp
from jax import lax
from jax.experimental import pallas as pl
from jax.experimental.pallas import tpu as pltpu
from jax.sharding import PartitionSpec as P

HD = 80
TILE = 256
NEAR = (1, -1, 2, -2)
MESH_IDS = pl.DeviceIdType.MESH


def project_kernel(order, ctx_ref, weight_ref, tokens_ref, out_ref, slots, send_sem, recv_sem):
    n = slots.shape[0]
    rows, width = ctx_ref.shape
    cols = out_ref.shape[1]
    half = rows // 2
    me = lax.axis_index("tp")
    place = {"tp": me, "req": lax.axis_index("req")}

    def peer(k):
        where = dict(place, tp=lax.rem(me + k, n))
        return tuple(where[a] for a in order)

    def send(src, dst, sem, k):
        copy = pltpu.make_async_remote_copy(
            src_ref=src,
            dst_ref=dst,
            send_sem=send_sem.at[sem],
            recv_sem=recv_sem.at[sem],
            device_id=peer(k),
            device_id_type=MESH_IDS,
        )
        copy.start()
        return copy

    barrier = pltpu.get_barrier_semaphore()
    for k in (1, n - 1):
        pl.semaphore_signal(barrier, inc=1, device_id=peer(k), device_id_type=MESH_IDS)
    pl.semaphore_wait(barrier, 2)
    right = send(ctx_ref, slots.at[1], 1, 1)
    left = send(ctx_ref, slots.at[3], 3, n - 1)
    tile = 256

    def add_term(block, source, first):
        base = pl.multiple_of(source * width, 8)

        @pl.loop(0, rows // tile)
        def _(i):
            r = pl.ds(pl.multiple_of(i * tile, tile), tile)

            @pl.loop(0, cols // tile)
            def _(j):
                c = pl.ds(pl.multiple_of(j * tile, tile), tile)
                term = jnp.dot(
                    block[r, :], weight_ref[pl.ds(base, width), c], preferred_element_type=jnp.float32
                )
                term = term.astype(jnp.bfloat16).astype(jnp.float32)
                if first:
                    out_ref[r, c] = term
                else:
                    out_ref[r, c] = out_ref[r, c] + term

    add_term(ctx_ref, me, True)
    right.wait_recv()
    onward = send(slots.at[1, pl.ds(0, half)], slots.at[2, pl.ds(0, half)], 2, 1)
    add_term(slots.at[1], lax.rem(me + n - 1, n), False)
    left.wait_recv()
    backward = send(slots.at[3, pl.ds(half, half)], slots.at[2, pl.ds(half, half)], 0, n - 1)
    add_term(slots.at[3], lax.rem(me + 1, n), False)
    onward.wait_recv()
    backward.wait_recv()
    add_term(slots.at[2], lax.rem(me + 2, n), False)

    @pl.loop(0, rows // tile)
    def _(i):
        r = pl.ds(pl.multiple_of(i * tile, tile), tile)
        out_ref[r, :] = out_ref[r, :] + tokens_ref[r, :].astype(jnp.float32)

    for copy in (right, left, onward, backward):
        copy.wait_send()


def exchange_kernel(order, n, keys_ref, values_ref, marks_ref, keys_out, values_out, marks_out,
                    send_sem, recv_sem, local_sem):
    me = lax.axis_index("req")
    place = {"req": me, "tp": lax.axis_index("tp")}
    span = marks_ref.shape[1]

    def peer(d):
        where = dict(place, req=lax.rem(me + d + n, n))
        return tuple(where[a] for a in order)

    def windows(slot):
        part = pl.ds(slot * span, span)
        return (keys_out.at[:, :, part], values_out.at[:, part, :], marks_out.at[:, part])

    sources = (keys_ref, values_ref, marks_ref)
    barrier = pltpu.get_barrier_semaphore()
    for d in NEAR:
        pl.semaphore_signal(barrier, inc=1, device_id=peer(d), device_id_type=MESH_IDS)
    pl.semaphore_wait(barrier, len(NEAR))
    odd = lax.rem(me, 2)

    def send(kind, slices, targets, d):
        out = []
        for a, (src, dst) in enumerate(zip(slices, targets)):
            copy = pltpu.make_async_remote_copy(
                src_ref=src,
                dst_ref=dst,
                send_sem=send_sem.at[3 * kind + a],
                recv_sem=recv_sem.at[3 * kind + a],
                device_id=peer(d),
                device_id_type=MESH_IDS,
            )
            copy.start()
            out.append(copy)
        return out

    right = send(0, sources, windows(1), 1)
    left = send(1, sources, windows(3), -1)
    far = send(2, sources, windows(4 * odd), 2 - 4 * odd)
    local = []
    for a, (src, dst) in enumerate(zip(sources, windows(2))):
        copy = pltpu.make_async_copy(src, dst, local_sem.at[a])
        copy.start()
        local.append(copy)
    for a in range(3):
        right[a].wait_recv()
        left[a].wait_recv()
    relay = send(3, windows(1 + 2 * odd), windows(4 * odd), 1 - 2 * odd)
    for copy in local:
        copy.wait()
    for copy in right + left:
        copy.wait_send()
    for copy in far + relay:
        copy.wait()


def exchange(keys, values, marks, order):
    n = lax.axis_size("req")
    slots = 2 * max(NEAR) + 1
    heads, width, span = keys.shape
    any_spec = pl.BlockSpec(memory_space=pl.ANY)
    keys_all, values_all, marks_all = pl.pallas_call(
        functools.partial(exchange_kernel, order, n),
        out_shape=(
            jax.ShapeDtypeStruct((heads, width, slots * span), keys.dtype),
            jax.ShapeDtypeStruct((heads, slots * span, width), values.dtype),
            jax.ShapeDtypeStruct((1, slots * span), marks.dtype),
        ),
        in_specs=[any_spec] * 3,
        out_specs=(any_spec, any_spec, any_spec),
        scratch_shapes=[
            pltpu.SemaphoreType.DMA((12,)),
            pltpu.SemaphoreType.DMA((12,)),
            pltpu.SemaphoreType.DMA((3,)),
        ],
        compiler_params=pltpu.CompilerParams(collective_id=1, has_side_effects=True),
    )(keys, values, marks.reshape(1, span))
    source = lax.axis_index("req") + jnp.arange(slots * span, dtype=jnp.int32) // span - max(NEAR)
    present = (source >= 0) & (source < n)
    return keys_all, values_all, jnp.where(present, marks_all[0], 0)


def project(context, weight, tokens, order):
    n = weight.shape[0] // context.shape[1]
    rows, cols = tokens.shape
    return pl.pallas_call(
        functools.partial(project_kernel, order),
        out_shape=jax.ShapeDtypeStruct((rows, cols), jnp.float32),
        in_specs=[pl.BlockSpec(memory_space=pltpu.VMEM)] * 3,
        out_specs=pl.BlockSpec(memory_space=pltpu.VMEM),
        scratch_shapes=[
            pltpu.VMEM((n,) + context.shape, context.dtype),
            pltpu.SemaphoreType.DMA((n,)),
            pltpu.SemaphoreType.DMA((n,)),
        ],
        compiler_params=pltpu.CompilerParams(
            collective_id=0, has_side_effects=True, vmem_limit_bytes=48 * 1024 * 1024
        ),
        cost_estimate=pl.CostEstimate(
            flops=2 * rows * cols * weight.shape[0],
            bytes_accessed=4 * rows * cols + 2 * weight.size + 2 * rows * cols + 2 * n * context.size,
            transcendentals=0,
        ),
    )(context, weight, tokens)


def shifted_2(block, axis, distance):
    devices = range(lax.axis_size(axis))
    route = [(i - distance, i) for i in devices if i - distance in devices]
    return lax.ppermute(block, axis, route)


def layer_norm(stream, gain):
    center = jnp.mean(stream, axis=-1, keepdims=True)
    shifted = stream - center
    spread = jnp.mean(shifted * shifted, axis=-1, keepdims=True)
    return shifted * lax.rsqrt(spread + 1e-06) * gain.astype(jnp.float32)


def flash_kernel(bounds, q_ref, qm_ref, k_ref, v_ref, km_ref, o_ref):
    i = pl.program_id(0)
    tile = TILE
    factor = 1.0 / math.sqrt(HD)
    q = q_ref[...]
    qm = qm_ref[...]

    def step(j, carry):
        running_max, running_sum, weighted = carry
        start = pl.multiple_of(j * tile, tile)
        keys = k_ref[:, :, pl.ds(start, tile)]
        values = v_ref[:, pl.ds(start, tile), :]
        km = km_ref[:, pl.ds(start, tile)]
        scores = lax.dot_general(
            q, keys, (((2,), (1,)), ((0,), (0,))), preferred_element_type=jnp.float32
        ) * factor
        matches = (qm == km)[None]
        new_max = jnp.maximum(
            running_max, jnp.max(jnp.where(matches, scores, -1e30), axis=2, keepdims=True)
        )
        probs = jnp.where(matches, jnp.exp(scores - new_max), 0.0)
        shrink = jnp.exp(running_max - new_max)
        new_sum = running_sum * shrink + jnp.sum(probs, axis=2, keepdims=True)
        update = lax.dot_general(
            probs.astype(jnp.bfloat16), values, (((2,), (1,)), ((0,), (0,))),
            preferred_element_type=jnp.float32,
        )
        return new_max, new_sum, weighted * shrink + update

    heads, rows, width = q.shape
    init = (
        jnp.full((heads, rows, 1), -1e30, jnp.float32),
        jnp.zeros((heads, rows, 1), jnp.float32),
        jnp.zeros((heads, rows, width), jnp.float32),
    )
    _, total, weighted = lax.fori_loop(bounds[0, i], bounds[1, i], step, init)
    o_ref[...] = (weighted / total).astype(o_ref.dtype)


def attention(queries, query_marks, keys, values, key_marks):
    heads, rows, width = queries.shape
    key_rows = keys.shape[2]
    tiles = rows // TILE
    low = query_marks.reshape(tiles, TILE).min(axis=1)
    high = query_marks.reshape(tiles, TILE).max(axis=1)
    valid = (key_marks[None, :] >= low[:, None]) & (key_marks[None, :] <= high[:, None])
    place = jnp.arange(key_rows, dtype=jnp.int32)[None, :]
    first = jnp.min(jnp.where(valid, place, key_rows), axis=1)
    last = jnp.max(jnp.where(valid, place, -1), axis=1)
    bounds = jnp.stack([first // TILE, last // TILE + 1]).astype(jnp.int32)
    return pl.pallas_call(
        flash_kernel,
        out_shape=jax.ShapeDtypeStruct(queries.shape, queries.dtype),
        grid_spec=pltpu.PrefetchScalarGridSpec(
            num_scalar_prefetch=1,
            grid=(tiles,),
            in_specs=[
                pl.BlockSpec((heads, TILE, width), lambda i, b: (0, i, 0)),
                pl.BlockSpec((TILE, 1), lambda i, b: (i, 0)),
                pl.BlockSpec((heads, width, key_rows), lambda i, b: (0, 0, 0)),
                pl.BlockSpec((heads, key_rows, width), lambda i, b: (0, 0, 0)),
                pl.BlockSpec((1, key_rows), lambda i, b: (0, 0)),
            ],
            out_specs=pl.BlockSpec((heads, TILE, width), lambda i, b: (0, i, 0)),
        ),
        compiler_params=pltpu.CompilerParams(vmem_limit_bytes=48 * 1024 * 1024),
        cost_estimate=pl.CostEstimate(
            flops=4 * heads * rows * 2048 * width,
            bytes_accessed=2 * (queries.size * 2 + keys.size + values.size),
            transcendentals=heads * rows * 2048,
        ),
    )(bounds, queries, query_marks.reshape(rows, 1), keys, values, key_marks.reshape(1, key_rows))


def body(
    order,
    tokens,
    segments,
    attend_gain,
    attend_weight,
    output_weight,
    mixer_gain,
    expand_weight,
    reduce_weight,
    output_gain,
    merge_weight,
    merge_index,
    owners,
):
    token_rows = tokens.shape[0]
    head_width = attend_weight.shape[2]
    head_count = head_width // HD
    full_weight = lax.all_gather(output_weight, "tp", axis=0, tiled=True)
    stream = tokens.astype(jnp.float32)
    attend_in = layer_norm(stream, attend_gain).astype(jnp.bfloat16)
    projected = jnp.dot(
        attend_in,
        attend_weight.reshape(attend_weight.shape[0], 3 * head_width),
        preferred_element_type=jnp.float32,
    ).astype(jnp.bfloat16)
    marks = segments + 1

    def by_head(block):
        return jnp.transpose(block.reshape(block.shape[0], head_count, HD), (1, 0, 2))

    keys_all, values_all, key_marks = exchange(
        jnp.transpose(projected[:, head_width : 2 * head_width].reshape(-1, head_count, HD), (1, 2, 0)),
        by_head(projected[:, 2 * head_width :]),
        marks,
        order,
    )
    context = attention(by_head(projected[:, :head_width]), marks, keys_all, values_all, key_marks)
    context = jnp.transpose(context, (1, 0, 2)).reshape(token_rows, head_width)
    middle = project(context, full_weight, tokens, order)
    mixer_in = layer_norm(middle, mixer_gain).astype(jnp.bfloat16)
    expanded = jax.nn.gelu(
        jnp.dot(mixer_in, expand_weight, preferred_element_type=jnp.float32), approximate=False
    ).astype(jnp.bfloat16)
    hidden_terms = jnp.dot(expanded, reduce_weight, preferred_element_type=jnp.float32)
    final_stream = middle + lax.psum(hidden_terms.astype(jnp.bfloat16), "tp").astype(jnp.float32)
    final_normed = layer_norm(final_stream, output_gain).astype(jnp.bfloat16)
    merged_rows = merge_index.shape[0]
    local_index = merge_index - lax.axis_index("req") * token_rows
    picks = (local_index[:, :, None] == jnp.arange(token_rows, dtype=jnp.int32)).astype(jnp.bfloat16)
    merged = jnp.einsum(
        "mkt,tc->mkc", picks, final_normed, preferred_element_type=jnp.float32
    ).astype(jnp.bfloat16).reshape(merged_rows, 4 * final_normed.shape[1])
    feature = jnp.dot(merged, merge_weight, preferred_element_type=jnp.float32).astype(jnp.bfloat16)
    peers = lax.axis_size("req")
    capacity = 2 * merged_rows // peers
    target = owners[:, 0]
    choose = (target[:, None] == jnp.arange(peers, dtype=jnp.int32)[None, :]).astype(jnp.int32)
    slot = jnp.sum((jnp.cumsum(choose, axis=0) - 1) * choose, axis=1)
    position = target * capacity + slot
    placement = (
        position[:, None] == jnp.arange(peers * capacity, dtype=jnp.int32)[None, :]
    ).astype(jnp.bfloat16)
    outgoing = jnp.einsum(
        "ms,mc->sc", placement, feature, preferred_element_type=jnp.float32
    ).astype(jnp.bfloat16)
    outgoing = outgoing.reshape(peers, capacity, feature.shape[1])
    received = lax.all_to_all(outgoing, "req", split_axis=0, concat_axis=0, tiled=True)
    return received.reshape(1, peers, capacity, feature.shape[1])


def solution(mesh):
    placed = (
        P("req", None),
        P("req"),
        P(),
        P(None, None, "tp"),
        P("tp", None),
        P(),
        P(None, "tp"),
        P("tp", None),
        P(),
        P(None, "tp"),
        P("req", None),
        P("req", None),
    )
    return jax.shard_map(
        functools.partial(body, tuple(mesh.axis_names)), mesh=mesh, in_specs=placed, out_specs=P("req", None, None, "tp"), check_vma=False
    )
```

```python
import functools
import math

import jax
import jax.numpy as jnp
from jax import lax
from jax.experimental import pallas as pl
from jax.experimental.pallas import tpu as pltpu
from jax.sharding import PartitionSpec as P

HD = 80
TILE = 256
NEAR = (1, -1, 2, -2)
MESH_IDS = pl.DeviceIdType.MESH


def project_kernel(order, ctx_ref, weight_ref, tokens_ref, out_ref, slots, send_sem, recv_sem):
    n = slots.shape[0]
    rows, width = ctx_ref.shape
    cols = out_ref.shape[1]
    half = rows // 2
    me = lax.axis_index("tp")
    place = {"tp": me, "req": lax.axis_index("req")}

    def peer(k):
        where = dict(place, tp=lax.rem(me + k, n))
        return tuple(where[a] for a in order)

    def send(src, dst, sem, k):
        copy = pltpu.make_async_remote_copy(
            src_ref=src,
            dst_ref=dst,
            send_sem=send_sem.at[sem],
            recv_sem=recv_sem.at[sem],
            device_id=peer(k),
            device_id_type=MESH_IDS,
        )
        copy.start()
        return copy

    barrier = pltpu.get_barrier_semaphore()
    for k in (1, n - 1):
        pl.semaphore_signal(barrier, inc=1, device_id=peer(k), device_id_type=MESH_IDS)
    pl.semaphore_wait(barrier, 2)
    right = send(ctx_ref, slots.at[1], 1, 1)
    left = send(ctx_ref, slots.at[3], 3, n - 1)
    tile = 256

    def add_term(block, source, first):
        base = pl.multiple_of(source * width, 8)

        @pl.loop(0, rows // tile)
        def _(i):
            r = pl.ds(pl.multiple_of(i * tile, tile), tile)

            @pl.loop(0, cols // tile)
            def _(j):
                c = pl.ds(pl.multiple_of(j * tile, tile), tile)
                term = jnp.dot(
                    block[r, :], weight_ref[pl.ds(base, width), c], preferred_element_type=jnp.float32
                )
                term = term.astype(jnp.bfloat16).astype(jnp.float32)
                if first:
                    out_ref[r, c] = term
                else:
                    out_ref[r, c] = out_ref[r, c] + term

    add_term(ctx_ref, me, True)
    right.wait_recv()
    onward = send(slots.at[1, pl.ds(0, half)], slots.at[2, pl.ds(0, half)], 2, 1)
    add_term(slots.at[1], lax.rem(me + n - 1, n), False)
    left.wait_recv()
    backward = send(slots.at[3, pl.ds(half, half)], slots.at[2, pl.ds(half, half)], 0, n - 1)
    add_term(slots.at[3], lax.rem(me + 1, n), False)
    onward.wait_recv()
    backward.wait_recv()
    add_term(slots.at[2], lax.rem(me + 2, n), False)

    @pl.loop(0, rows // tile)
    def _(i):
        r = pl.ds(pl.multiple_of(i * tile, tile), tile)
        out_ref[r, :] = out_ref[r, :] + tokens_ref[r, :].astype(jnp.float32)

    for copy in (right, left, onward, backward):
        copy.wait_send()


def exchange_kernel(order, n, keys_ref, values_ref, marks_ref, keys_out, values_out, marks_out,
                    send_sem, recv_sem, local_sem):
    me = lax.axis_index("req")
    place = {"req": me, "tp": lax.axis_index("tp")}
    span = marks_ref.shape[1]

    def peer(d):
        where = dict(place, req=lax.rem(me + d + n, n))
        return tuple(where[a] for a in order)

    def windows(slot):
        part = pl.ds(slot * span, span)
        return (keys_out.at[:, :, part], values_out.at[:, part, :], marks_out.at[:, part])

    sources = (keys_ref, values_ref, marks_ref)
    barrier = pltpu.get_barrier_semaphore()
    for d in NEAR:
        pl.semaphore_signal(barrier, inc=1, device_id=peer(d), device_id_type=MESH_IDS)
    pl.semaphore_wait(barrier, len(NEAR))
    odd = lax.rem(me, 2)

    def send(kind, slices, targets, d):
        out = []
        for a, (src, dst) in enumerate(zip(slices, targets)):
            copy = pltpu.make_async_remote_copy(
                src_ref=src,
                dst_ref=dst,
                send_sem=send_sem.at[3 * kind + a],
                recv_sem=recv_sem.at[3 * kind + a],
                device_id=peer(d),
                device_id_type=MESH_IDS,
            )
            copy.start()
            out.append(copy)
        return out

    right = send(0, sources, windows(1), 1)
    left = send(1, sources, windows(3), -1)
    far = send(2, sources, windows(4 * odd), 2 - 4 * odd)
    local = []
    for a, (src, dst) in enumerate(zip(sources, windows(2))):
        copy = pltpu.make_async_copy(src, dst, local_sem.at[a])
        copy.start()
        local.append(copy)
    for a in range(3):
        right[a].wait_recv()
        left[a].wait_recv()
    relay = send(3, windows(1 + 2 * odd), windows(4 * odd), 1 - 2 * odd)
    for copy in local:
        copy.wait()
    for copy in right + left:
        copy.wait_send()
    for copy in far + relay:
        copy.wait()


def exchange(keys, values, marks, order):
    n = lax.axis_size("req")
    slots = 2 * max(NEAR) + 1
    heads, width, span = keys.shape
    any_spec = pl.BlockSpec(memory_space=pl.ANY)
    keys_all, values_all, marks_all = pl.pallas_call(
        functools.partial(exchange_kernel, order, n),
        out_shape=(
            jax.ShapeDtypeStruct((heads, width, slots * span), keys.dtype),
            jax.ShapeDtypeStruct((heads, slots * span, width), values.dtype),
            jax.ShapeDtypeStruct((1, slots * span), marks.dtype),
        ),
        in_specs=[any_spec] * 3,
        out_specs=(any_spec, any_spec, any_spec),
        scratch_shapes=[
            pltpu.SemaphoreType.DMA((12,)),
            pltpu.SemaphoreType.DMA((12,)),
            pltpu.SemaphoreType.DMA((3,)),
        ],
        compiler_params=pltpu.CompilerParams(collective_id=1, has_side_effects=True),
    )(keys, values, marks.reshape(1, span))
    source = lax.axis_index("req") + jnp.arange(slots * span, dtype=jnp.int32) // span - max(NEAR)
    present = (source >= 0) & (source < n)
    return keys_all, values_all, jnp.where(present, marks_all[0], 0)


def deliver_kernel(order, n, outgoing_ref, received_ref, send_sem, recv_sem, local_sem):
    me = lax.axis_index("req")
    place = {"req": me, "tp": lax.axis_index("tp")}

    def peer(k):
        where = dict(place, req=lax.rem(me + k, n))
        return tuple(where[a] for a in order)

    barrier = pltpu.get_barrier_semaphore()
    for k in range(1, n):
        pl.semaphore_signal(barrier, inc=1, device_id=peer(k), device_id_type=MESH_IDS)
    pl.semaphore_wait(barrier, n - 1)
    copies = []
    for k in range(1, n):
        copy = pltpu.make_async_remote_copy(
            src_ref=outgoing_ref.at[lax.rem(me + k, n)],
            dst_ref=received_ref.at[me],
            send_sem=send_sem.at[k],
            recv_sem=recv_sem.at[k],
            device_id=peer(k),
            device_id_type=MESH_IDS,
        )
        copy.start()
        copies.append(copy)
    own = pltpu.make_async_copy(outgoing_ref.at[me], received_ref.at[me], local_sem.at[0])
    own.start()
    own.wait()
    for copy in copies:
        copy.wait()


def deliver(outgoing, order):
    n = lax.axis_size("req")
    return pl.pallas_call(
        functools.partial(deliver_kernel, order, n),
        out_shape=jax.ShapeDtypeStruct(outgoing.shape, outgoing.dtype),
        in_specs=[pl.BlockSpec(memory_space=pltpu.VMEM)],
        out_specs=pl.BlockSpec(memory_space=pltpu.VMEM),
        scratch_shapes=[
            pltpu.SemaphoreType.DMA((n,)),
            pltpu.SemaphoreType.DMA((n,)),
            pltpu.SemaphoreType.DMA((1,)),
        ],
        compiler_params=pltpu.CompilerParams(collective_id=2, has_side_effects=True),
    )(outgoing)


def project(context, weight, tokens, order):
    n = weight.shape[0] // context.shape[1]
    rows, cols = tokens.shape
    return pl.pallas_call(
        functools.partial(project_kernel, order),
        out_shape=jax.ShapeDtypeStruct((rows, cols), jnp.float32),
        in_specs=[pl.BlockSpec(memory_space=pltpu.VMEM)] * 3,
        out_specs=pl.BlockSpec(memory_space=pltpu.VMEM),
        scratch_shapes=[
            pltpu.VMEM((n,) + context.shape, context.dtype),
            pltpu.SemaphoreType.DMA((n,)),
            pltpu.SemaphoreType.DMA((n,)),
        ],
        compiler_params=pltpu.CompilerParams(
            collective_id=0, has_side_effects=True, vmem_limit_bytes=48 * 1024 * 1024
        ),
        cost_estimate=pl.CostEstimate(
            flops=2 * rows * cols * weight.shape[0],
            bytes_accessed=4 * rows * cols + 2 * weight.size + 2 * rows * cols + 2 * n * context.size,
            transcendentals=0,
        ),
    )(context, weight, tokens)


def shifted_2(block, axis, distance):
    devices = range(lax.axis_size(axis))
    route = [(i - distance, i) for i in devices if i - distance in devices]
    return lax.ppermute(block, axis, route)


def layer_norm(stream, gain):
    center = jnp.mean(stream, axis=-1, keepdims=True)
    shifted = stream - center
    spread = jnp.mean(shifted * shifted, axis=-1, keepdims=True)
    return shifted * lax.rsqrt(spread + 1e-06) * gain.astype(jnp.float32)


def flash_kernel(bounds, q_ref, qm_ref, k_ref, v_ref, km_ref, o_ref):
    i = pl.program_id(0)
    tile = TILE
    factor = 1.0 / math.sqrt(HD)
    q = q_ref[...]
    qm = qm_ref[...]

    def step(j, carry):
        running_max, running_sum, weighted = carry
        start = pl.multiple_of(j * tile, tile)
        keys = k_ref[:, :, pl.ds(start, tile)]
        values = v_ref[:, pl.ds(start, tile), :]
        km = km_ref[:, pl.ds(start, tile)]
        scores = lax.dot_general(
            q, keys, (((2,), (1,)), ((0,), (0,))), preferred_element_type=jnp.float32
        ) * factor
        matches = (qm == km)[None]
        new_max = jnp.maximum(
            running_max, jnp.max(jnp.where(matches, scores, -1e30), axis=2, keepdims=True)
        )
        probs = jnp.where(matches, jnp.exp(scores - new_max), 0.0)
        shrink = jnp.exp(running_max - new_max)
        new_sum = running_sum * shrink + jnp.sum(probs, axis=2, keepdims=True)
        update = lax.dot_general(
            probs.astype(jnp.bfloat16), values, (((2,), (1,)), ((0,), (0,))),
            preferred_element_type=jnp.float32,
        )
        return new_max, new_sum, weighted * shrink + update

    heads, rows, width = q.shape
    init = (
        jnp.full((heads, rows, 1), -1e30, jnp.float32),
        jnp.zeros((heads, rows, 1), jnp.float32),
        jnp.zeros((heads, rows, width), jnp.float32),
    )
    _, total, weighted = lax.fori_loop(bounds[0, i], bounds[1, i], step, init)
    o_ref[...] = (weighted / total).astype(o_ref.dtype)


def attention(queries, query_marks, keys, values, key_marks):
    heads, rows, width = queries.shape
    key_rows = keys.shape[2]
    tiles = rows // TILE
    low = query_marks.reshape(tiles, TILE).min(axis=1)
    high = query_marks.reshape(tiles, TILE).max(axis=1)
    valid = (key_marks[None, :] >= low[:, None]) & (key_marks[None, :] <= high[:, None])
    place = jnp.arange(key_rows, dtype=jnp.int32)[None, :]
    first = jnp.min(jnp.where(valid, place, key_rows), axis=1)
    last = jnp.max(jnp.where(valid, place, -1), axis=1)
    bounds = jnp.stack([first // TILE, last // TILE + 1]).astype(jnp.int32)
    return pl.pallas_call(
        flash_kernel,
        out_shape=jax.ShapeDtypeStruct(queries.shape, queries.dtype),
        grid_spec=pltpu.PrefetchScalarGridSpec(
            num_scalar_prefetch=1,
            grid=(tiles,),
            in_specs=[
                pl.BlockSpec((heads, TILE, width), lambda i, b: (0, i, 0)),
                pl.BlockSpec((TILE, 1), lambda i, b: (i, 0)),
                pl.BlockSpec((heads, width, key_rows), lambda i, b: (0, 0, 0)),
                pl.BlockSpec((heads, key_rows, width), lambda i, b: (0, 0, 0)),
                pl.BlockSpec((1, key_rows), lambda i, b: (0, 0)),
            ],
            out_specs=pl.BlockSpec((heads, TILE, width), lambda i, b: (0, i, 0)),
        ),
        compiler_params=pltpu.CompilerParams(vmem_limit_bytes=48 * 1024 * 1024),
        cost_estimate=pl.CostEstimate(
            flops=4 * heads * rows * 2048 * width,
            bytes_accessed=2 * (queries.size * 2 + keys.size + values.size),
            transcendentals=heads * rows * 2048,
        ),
    )(bounds, queries, query_marks.reshape(rows, 1), keys, values, key_marks.reshape(1, key_rows))


def body(
    order,
    tokens,
    segments,
    attend_gain,
    attend_weight,
    output_weight,
    mixer_gain,
    expand_weight,
    reduce_weight,
    output_gain,
    merge_weight,
    merge_index,
    owners,
):
    token_rows = tokens.shape[0]
    head_width = attend_weight.shape[2]
    head_count = head_width // HD
    full_weight = lax.all_gather(output_weight, "tp", axis=0, tiled=True)
    stream = tokens.astype(jnp.float32)
    attend_in = layer_norm(stream, attend_gain).astype(jnp.bfloat16)
    projected = jnp.dot(
        attend_in,
        attend_weight.reshape(attend_weight.shape[0], 3 * head_width),
        preferred_element_type=jnp.float32,
    ).astype(jnp.bfloat16)
    marks = segments + 1

    def by_head(block):
        return jnp.transpose(block.reshape(block.shape[0], head_count, HD), (1, 0, 2))

    keys_all, values_all, key_marks = exchange(
        jnp.transpose(projected[:, head_width : 2 * head_width].reshape(-1, head_count, HD), (1, 2, 0)),
        by_head(projected[:, 2 * head_width :]),
        marks,
        order,
    )
    context = attention(by_head(projected[:, :head_width]), marks, keys_all, values_all, key_marks)
    context = jnp.transpose(context, (1, 0, 2)).reshape(token_rows, head_width)
    middle = project(context, full_weight, tokens, order)
    mixer_in = layer_norm(middle, mixer_gain).astype(jnp.bfloat16)
    expanded = jax.nn.gelu(
        jnp.dot(mixer_in, expand_weight, preferred_element_type=jnp.float32), approximate=False
    ).astype(jnp.bfloat16)
    hidden_terms = jnp.dot(expanded, reduce_weight, preferred_element_type=jnp.float32)
    final_stream = middle + lax.psum(hidden_terms.astype(jnp.bfloat16), "tp").astype(jnp.float32)
    final_normed = layer_norm(final_stream, output_gain).astype(jnp.bfloat16)
    merged_rows = merge_index.shape[0]
    local_index = merge_index - lax.axis_index("req") * token_rows
    picks = (local_index[:, :, None] == jnp.arange(token_rows, dtype=jnp.int32)).astype(jnp.bfloat16)
    merged = jnp.einsum(
        "mkt,tc->mkc", picks, final_normed, preferred_element_type=jnp.float32
    ).astype(jnp.bfloat16).reshape(merged_rows, 4 * final_normed.shape[1])
    feature = jnp.dot(merged, merge_weight, preferred_element_type=jnp.float32).astype(jnp.bfloat16)
    peers = lax.axis_size("req")
    capacity = 2 * merged_rows // peers
    target = owners[:, 0]
    choose = (target[:, None] == jnp.arange(peers, dtype=jnp.int32)[None, :]).astype(jnp.int32)
    slot = jnp.sum((jnp.cumsum(choose, axis=0) - 1) * choose, axis=1)
    position = target * capacity + slot
    placement = (
        position[:, None] == jnp.arange(peers * capacity, dtype=jnp.int32)[None, :]
    ).astype(jnp.bfloat16)
    outgoing = jnp.einsum(
        "ms,mc->sc", placement, feature, preferred_element_type=jnp.float32
    ).astype(jnp.bfloat16)
    outgoing = outgoing.reshape(peers, capacity, feature.shape[1])
    received = deliver(outgoing, order)
    return received.reshape(1, peers, capacity, feature.shape[1])


def solution(mesh):
    placed = (
        P("req", None),
        P("req"),
        P(),
        P(None, None, "tp"),
        P("tp", None),
        P(),
        P(None, "tp"),
        P("tp", None),
        P(),
        P(None, "tp"),
        P("req", None),
        P("req", None),
    )
    return jax.shard_map(
        functools.partial(body, tuple(mesh.axis_names)), mesh=mesh, in_specs=placed, out_specs=P("req", None, None, "tp"), check_vma=False
    )
```

```python
import functools
import math

import jax
import jax.numpy as jnp
from jax import lax
from jax.experimental import pallas as pl
from jax.experimental.pallas import tpu as pltpu
from jax.sharding import PartitionSpec as P

HD = 80
TILE = 256
NEAR = (1, -1, 2, -2)
MESH_IDS = pl.DeviceIdType.MESH


def project_kernel(order, ctx_ref, weight_ref, tokens_ref, out_ref, slots, send_sem, recv_sem):
    n = slots.shape[0]
    rows, width = ctx_ref.shape
    cols = out_ref.shape[1]
    half = rows // 2
    me = lax.axis_index("tp")
    place = {"tp": me, "req": lax.axis_index("req")}

    def peer(k):
        where = dict(place, tp=lax.rem(me + k, n))
        return tuple(where[a] for a in order)

    def send(src, dst, sem, k):
        copy = pltpu.make_async_remote_copy(
            src_ref=src,
            dst_ref=dst,
            send_sem=send_sem.at[sem],
            recv_sem=recv_sem.at[sem],
            device_id=peer(k),
            device_id_type=MESH_IDS,
        )
        copy.start()
        return copy

    barrier = pltpu.get_barrier_semaphore()
    for k in (1, n - 1):
        pl.semaphore_signal(barrier, inc=1, device_id=peer(k), device_id_type=MESH_IDS)
    pl.semaphore_wait(barrier, 2)
    right = send(ctx_ref, slots.at[1], 1, 1)
    left = send(ctx_ref, slots.at[3], 3, n - 1)
    tile = 256

    def add_term(block, source, first):
        base = pl.multiple_of(source * width, 8)

        @pl.loop(0, rows // tile)
        def _(i):
            r = pl.ds(pl.multiple_of(i * tile, tile), tile)

            @pl.loop(0, cols // tile)
            def _(j):
                c = pl.ds(pl.multiple_of(j * tile, tile), tile)
                term = jnp.dot(
                    block[r, :], weight_ref[pl.ds(base, width), c], preferred_element_type=jnp.float32
                )
                term = term.astype(jnp.bfloat16).astype(jnp.float32)
                if first:
                    out_ref[r, c] = term
                else:
                    out_ref[r, c] = out_ref[r, c] + term

    add_term(ctx_ref, me, True)
    right.wait_recv()
    onward = send(slots.at[1, pl.ds(0, half)], slots.at[2, pl.ds(0, half)], 2, 1)
    add_term(slots.at[1], lax.rem(me + n - 1, n), False)
    left.wait_recv()
    backward = send(slots.at[3, pl.ds(half, half)], slots.at[2, pl.ds(half, half)], 0, n - 1)
    add_term(slots.at[3], lax.rem(me + 1, n), False)
    onward.wait_recv()
    backward.wait_recv()
    add_term(slots.at[2], lax.rem(me + 2, n), False)

    @pl.loop(0, rows // tile)
    def _(i):
        r = pl.ds(pl.multiple_of(i * tile, tile), tile)
        out_ref[r, :] = out_ref[r, :] + tokens_ref[r, :].astype(jnp.float32)

    for copy in (right, left, onward, backward):
        copy.wait_send()


def exchange_kernel(order, n, keys_ref, values_ref, marks_ref, keys_out, values_out, marks_out,
                    send_sem, recv_sem, local_sem):
    me = lax.axis_index("req")
    place = {"req": me, "tp": lax.axis_index("tp")}
    span = marks_ref.shape[1]

    def peer(d):
        where = dict(place, req=lax.rem(me + d + n, n))
        return tuple(where[a] for a in order)

    def windows(slot):
        part = pl.ds(slot * span, span)
        return (keys_out.at[:, :, part], values_out.at[:, part, :], marks_out.at[:, part])

    sources = (keys_ref, values_ref, marks_ref)
    barrier = pltpu.get_barrier_semaphore()
    for d in NEAR:
        pl.semaphore_signal(barrier, inc=1, device_id=peer(d), device_id_type=MESH_IDS)
    pl.semaphore_wait(barrier, len(NEAR))
    odd = lax.rem(me, 2)

    def send(kind, slices, targets, d):
        out = []
        for a, (src, dst) in enumerate(zip(slices, targets)):
            copy = pltpu.make_async_remote_copy(
                src_ref=src,
                dst_ref=dst,
                send_sem=send_sem.at[3 * kind + a],
                recv_sem=recv_sem.at[3 * kind + a],
                device_id=peer(d),
                device_id_type=MESH_IDS,
            )
            copy.start()
            out.append(copy)
        return out

    right = send(0, sources, windows(1), 1)
    left = send(1, sources, windows(3), -1)
    far = send(2, sources, windows(4 * odd), 2 - 4 * odd)
    local = []
    for a, (src, dst) in enumerate(zip(sources, windows(2))):
        copy = pltpu.make_async_copy(src, dst, local_sem.at[a])
        copy.start()
        local.append(copy)
    for a in range(3):
        right[a].wait_recv()
        left[a].wait_recv()
    relay = send(3, windows(1 + 2 * odd), windows(4 * odd), 1 - 2 * odd)
    for copy in local:
        copy.wait()
    for copy in right + left:
        copy.wait_send()
    for copy in far + relay:
        copy.wait()


def exchange(keys, values, marks, order):
    n = lax.axis_size("req")
    slots = 2 * max(NEAR) + 1
    heads, width, span = keys.shape
    any_spec = pl.BlockSpec(memory_space=pl.ANY)
    keys_all, values_all, marks_all = pl.pallas_call(
        functools.partial(exchange_kernel, order, n),
        out_shape=(
            jax.ShapeDtypeStruct((heads, width, slots * span), keys.dtype),
            jax.ShapeDtypeStruct((heads, slots * span, width), values.dtype),
            jax.ShapeDtypeStruct((1, slots * span), marks.dtype),
        ),
        in_specs=[any_spec] * 3,
        out_specs=(any_spec, any_spec, any_spec),
        scratch_shapes=[
            pltpu.SemaphoreType.DMA((12,)),
            pltpu.SemaphoreType.DMA((12,)),
            pltpu.SemaphoreType.DMA((3,)),
        ],
        compiler_params=pltpu.CompilerParams(collective_id=1, has_side_effects=True),
    )(keys, values, marks.reshape(1, span))
    source = lax.axis_index("req") + jnp.arange(slots * span, dtype=jnp.int32) // span - max(NEAR)
    present = (source >= 0) & (source < n)
    return keys_all, values_all, jnp.where(present, marks_all[0], 0)


def deliver_kernel(order, n, outgoing_ref, received_ref, send_sem, recv_sem, local_sem):
    me = lax.axis_index("req")
    place = {"req": me, "tp": lax.axis_index("tp")}

    def peer(k):
        where = dict(place, req=lax.rem(me + k, n))
        return tuple(where[a] for a in order)

    barrier = pltpu.get_barrier_semaphore()
    for k in range(1, n):
        pl.semaphore_signal(barrier, inc=1, device_id=peer(k), device_id_type=MESH_IDS)
    pl.semaphore_wait(barrier, n - 1)
    copies = []
    for k in range(1, n):
        copy = pltpu.make_async_remote_copy(
            src_ref=outgoing_ref.at[lax.rem(me + k, n)],
            dst_ref=received_ref.at[me],
            send_sem=send_sem.at[k],
            recv_sem=recv_sem.at[k],
            device_id=peer(k),
            device_id_type=MESH_IDS,
        )
        copy.start()
        copies.append(copy)
    own = pltpu.make_async_copy(outgoing_ref.at[me], received_ref.at[me], local_sem.at[0])
    own.start()
    own.wait()
    for copy in copies:
        copy.wait()


def deliver(outgoing, order):
    n = lax.axis_size("req")
    return pl.pallas_call(
        functools.partial(deliver_kernel, order, n),
        out_shape=jax.ShapeDtypeStruct(outgoing.shape, outgoing.dtype),
        in_specs=[pl.BlockSpec(memory_space=pltpu.VMEM)],
        out_specs=pl.BlockSpec(memory_space=pltpu.VMEM),
        scratch_shapes=[
            pltpu.SemaphoreType.DMA((n,)),
            pltpu.SemaphoreType.DMA((n,)),
            pltpu.SemaphoreType.DMA((1,)),
        ],
        compiler_params=pltpu.CompilerParams(collective_id=2, has_side_effects=True),
    )(outgoing)


def project(context, weight, tokens, order):
    n = weight.shape[0] // context.shape[1]
    rows, cols = tokens.shape
    return pl.pallas_call(
        functools.partial(project_kernel, order),
        out_shape=jax.ShapeDtypeStruct((rows, cols), jnp.float32),
        in_specs=[pl.BlockSpec(memory_space=pltpu.VMEM)] * 3,
        out_specs=pl.BlockSpec(memory_space=pltpu.VMEM),
        scratch_shapes=[
            pltpu.VMEM((n,) + context.shape, context.dtype),
            pltpu.SemaphoreType.DMA((n,)),
            pltpu.SemaphoreType.DMA((n,)),
        ],
        compiler_params=pltpu.CompilerParams(
            collective_id=0, has_side_effects=True, vmem_limit_bytes=48 * 1024 * 1024
        ),
        cost_estimate=pl.CostEstimate(
            flops=2 * rows * cols * weight.shape[0],
            bytes_accessed=4 * rows * cols + 2 * weight.size + 2 * rows * cols + 2 * n * context.size,
            transcendentals=0,
        ),
    )(context, weight, tokens)


def shifted_2(block, axis, distance):
    devices = range(lax.axis_size(axis))
    route = [(i - distance, i) for i in devices if i - distance in devices]
    return lax.ppermute(block, axis, route)


def layer_norm(stream, gain):
    center = jnp.mean(stream, axis=-1, keepdims=True)
    shifted = stream - center
    spread = jnp.mean(shifted * shifted, axis=-1, keepdims=True)
    return shifted * lax.rsqrt(spread + 1e-06) * gain.astype(jnp.float32)


def flash_kernel(bounds, q_ref, qm_ref, k_ref, v_ref, km_ref, o_ref):
    i = pl.program_id(0)
    tile = TILE
    factor = 1.0 / math.sqrt(HD)
    q = q_ref[...]
    qm = qm_ref[...]

    def step(j, carry):
        running_max, running_sum, weighted = carry
        start = pl.multiple_of(j * tile, tile)
        keys = k_ref[:, :, pl.ds(start, tile)]
        values = v_ref[:, pl.ds(start, tile), :]
        km = km_ref[:, pl.ds(start, tile)]
        scores = lax.dot_general(
            q, keys, (((2,), (1,)), ((0,), (0,))), preferred_element_type=jnp.float32
        ) * factor
        masked = jnp.where((qm == km)[None], scores, -1e30)
        new_max = jnp.maximum(running_max, jnp.max(masked, axis=2, keepdims=True))
        probs = jnp.exp(masked - new_max)
        shrink = jnp.exp(running_max - new_max)
        new_sum = running_sum * shrink + jnp.sum(probs, axis=2, keepdims=True)
        update = lax.dot_general(
            probs.astype(jnp.bfloat16), values, (((2,), (1,)), ((0,), (0,))),
            preferred_element_type=jnp.float32,
        )
        return new_max, new_sum, weighted * shrink + update

    heads, rows, width = q.shape
    init = (
        jnp.full((heads, rows, 1), -1e30, jnp.float32),
        jnp.zeros((heads, rows, 1), jnp.float32),
        jnp.zeros((heads, rows, width), jnp.float32),
    )
    _, total, weighted = lax.fori_loop(bounds[0, i], bounds[1, i], step, init)
    o_ref[...] = (weighted / total).astype(o_ref.dtype)


def attention(queries, query_marks, keys, values, key_marks):
    heads, rows, width = queries.shape
    key_rows = keys.shape[2]
    tiles = rows // TILE
    low = query_marks.reshape(tiles, TILE).min(axis=1)
    high = query_marks.reshape(tiles, TILE).max(axis=1)
    valid = (key_marks[None, :] >= low[:, None]) & (key_marks[None, :] <= high[:, None])
    place = jnp.arange(key_rows, dtype=jnp.int32)[None, :]
    first = jnp.min(jnp.where(valid, place, key_rows), axis=1)
    last = jnp.max(jnp.where(valid, place, -1), axis=1)
    bounds = jnp.stack([first // TILE, last // TILE + 1]).astype(jnp.int32)
    return pl.pallas_call(
        flash_kernel,
        out_shape=jax.ShapeDtypeStruct(queries.shape, queries.dtype),
        grid_spec=pltpu.PrefetchScalarGridSpec(
            num_scalar_prefetch=1,
            grid=(tiles,),
            in_specs=[
                pl.BlockSpec((heads, TILE, width), lambda i, b: (0, i, 0)),
                pl.BlockSpec((TILE, 1), lambda i, b: (i, 0)),
                pl.BlockSpec((heads, width, key_rows), lambda i, b: (0, 0, 0)),
                pl.BlockSpec((heads, key_rows, width), lambda i, b: (0, 0, 0)),
                pl.BlockSpec((1, key_rows), lambda i, b: (0, 0)),
            ],
            out_specs=pl.BlockSpec((heads, TILE, width), lambda i, b: (0, i, 0)),
        ),
        compiler_params=pltpu.CompilerParams(vmem_limit_bytes=48 * 1024 * 1024),
        cost_estimate=pl.CostEstimate(
            flops=4 * heads * rows * 2048 * width,
            bytes_accessed=2 * (queries.size * 2 + keys.size + values.size),
            transcendentals=heads * rows * 2048,
        ),
    )(bounds, queries, query_marks.reshape(rows, 1), keys, values, key_marks.reshape(1, key_rows))


def body(
    order,
    tokens,
    segments,
    attend_gain,
    attend_weight,
    output_weight,
    mixer_gain,
    expand_weight,
    reduce_weight,
    output_gain,
    merge_weight,
    merge_index,
    owners,
):
    token_rows = tokens.shape[0]
    head_width = attend_weight.shape[2]
    head_count = head_width // HD
    full_weight = lax.all_gather(output_weight, "tp", axis=0, tiled=True)
    stream = tokens.astype(jnp.float32)
    attend_in = layer_norm(stream, attend_gain).astype(jnp.bfloat16)
    projected = jnp.dot(
        attend_in,
        attend_weight.reshape(attend_weight.shape[0], 3 * head_width),
        preferred_element_type=jnp.float32,
    ).astype(jnp.bfloat16)
    marks = segments + 1

    def by_head(block):
        return jnp.transpose(block.reshape(block.shape[0], head_count, HD), (1, 0, 2))

    keys_all, values_all, key_marks = exchange(
        jnp.transpose(projected[:, head_width : 2 * head_width].reshape(-1, head_count, HD), (1, 2, 0)),
        by_head(projected[:, 2 * head_width :]),
        marks,
        order,
    )
    context = attention(by_head(projected[:, :head_width]), marks, keys_all, values_all, key_marks)
    context = jnp.transpose(context, (1, 0, 2)).reshape(token_rows, head_width)
    middle = project(context, full_weight, tokens, order)
    mixer_in = layer_norm(middle, mixer_gain).astype(jnp.bfloat16)
    expanded = jax.nn.gelu(
        jnp.dot(mixer_in, expand_weight, preferred_element_type=jnp.float32), approximate=False
    ).astype(jnp.bfloat16)
    hidden_terms = jnp.dot(expanded, reduce_weight, preferred_element_type=jnp.float32)
    final_stream = middle + lax.psum(hidden_terms.astype(jnp.bfloat16), "tp").astype(jnp.float32)
    final_normed = layer_norm(final_stream, output_gain).astype(jnp.bfloat16)
    merged_rows = merge_index.shape[0]
    local_index = merge_index - lax.axis_index("req") * token_rows
    picks = (local_index[:, :, None] == jnp.arange(token_rows, dtype=jnp.int32)).astype(jnp.bfloat16)
    merged = jnp.einsum(
        "mkt,tc->mkc", picks, final_normed, preferred_element_type=jnp.float32
    ).astype(jnp.bfloat16)
    feature = jnp.einsum(
        "mkc,kcd->md",
        merged,
        merge_weight.reshape(4, final_normed.shape[1], merge_weight.shape[1]),
        preferred_element_type=jnp.float32,
    ).astype(jnp.bfloat16)
    peers = lax.axis_size("req")
    capacity = 2 * merged_rows // peers
    target = owners[:, 0]
    choose = (target[:, None] == jnp.arange(peers, dtype=jnp.int32)[None, :]).astype(jnp.int32)
    slot = jnp.sum((jnp.cumsum(choose, axis=0) - 1) * choose, axis=1)
    position = target * capacity + slot
    placement = (
        position[:, None] == jnp.arange(peers * capacity, dtype=jnp.int32)[None, :]
    ).astype(jnp.bfloat16)
    outgoing = jnp.einsum(
        "ms,mc->sc", placement, feature, preferred_element_type=jnp.float32
    ).astype(jnp.bfloat16)
    outgoing = outgoing.reshape(peers, capacity, feature.shape[1])
    received = deliver(outgoing, order)
    return received.reshape(1, peers, capacity, feature.shape[1])


def solution(mesh):
    placed = (
        P("req", None),
        P("req"),
        P(),
        P(None, None, "tp"),
        P("tp", None),
        P(),
        P(None, "tp"),
        P("tp", None),
        P(),
        P(None, "tp"),
        P("req", None),
        P("req", None),
    )
    return jax.shard_map(
        functools.partial(body, tuple(mesh.axis_names)), mesh=mesh, in_specs=placed, out_specs=P("req", None, None, "tp"), check_vma=False
    )
```

```python
import functools
import math

import jax
import jax.numpy as jnp
from jax import lax
from jax.experimental import pallas as pl
from jax.experimental.pallas import tpu as pltpu
from jax.sharding import PartitionSpec as P

HD = 80
TILE = 256
NEAR = (1, -1, 2, -2)
MESH_IDS = pl.DeviceIdType.MESH


def project_kernel(order, ctx_ref, weight_ref, tokens_ref, gain_ref, out_ref, norm_ref, slots, send_sem,
                   recv_sem):
    n = slots.shape[0]
    rows, width = ctx_ref.shape
    cols = out_ref.shape[1]
    half = rows // 2
    me = lax.axis_index("tp")
    place = {"tp": me, "req": lax.axis_index("req")}

    def peer(k):
        where = dict(place, tp=lax.rem(me + k, n))
        return tuple(where[a] for a in order)

    def send(src, dst, sem, k):
        copy = pltpu.make_async_remote_copy(
            src_ref=src,
            dst_ref=dst,
            send_sem=send_sem.at[sem],
            recv_sem=recv_sem.at[sem],
            device_id=peer(k),
            device_id_type=MESH_IDS,
        )
        copy.start()
        return copy

    barrier = pltpu.get_barrier_semaphore()
    for k in (1, n - 1):
        pl.semaphore_signal(barrier, inc=1, device_id=peer(k), device_id_type=MESH_IDS)
    pl.semaphore_wait(barrier, 2)
    right = send(ctx_ref, slots.at[1], 1, 1)
    left = send(ctx_ref, slots.at[3], 3, n - 1)
    tile = 256

    def add_term(block, source, first):
        base = pl.multiple_of(source * width, 8)

        @pl.loop(0, rows // tile)
        def _(i):
            r = pl.ds(pl.multiple_of(i * tile, tile), tile)

            @pl.loop(0, cols // tile)
            def _(j):
                c = pl.ds(pl.multiple_of(j * tile, tile), tile)
                term = jnp.dot(
                    block[r, :], weight_ref[pl.ds(base, width), c], preferred_element_type=jnp.float32
                )
                term = term.astype(jnp.bfloat16).astype(jnp.float32)
                if first:
                    out_ref[r, c] = term
                else:
                    out_ref[r, c] = out_ref[r, c] + term

    add_term(ctx_ref, me, True)
    right.wait_recv()
    onward = send(slots.at[1, pl.ds(0, half)], slots.at[2, pl.ds(0, half)], 2, 1)
    add_term(slots.at[1], lax.rem(me + n - 1, n), False)
    left.wait_recv()
    backward = send(slots.at[3, pl.ds(half, half)], slots.at[2, pl.ds(half, half)], 0, n - 1)
    add_term(slots.at[3], lax.rem(me + 1, n), False)
    onward.wait_recv()
    backward.wait_recv()
    add_term(slots.at[2], lax.rem(me + 2, n), False)

    @pl.loop(0, rows // tile)
    def _(i):
        r = pl.ds(pl.multiple_of(i * tile, tile), tile)
        middle = out_ref[r, :] + tokens_ref[r, :].astype(jnp.float32)
        out_ref[r, :] = middle
        norm_ref[r, :] = layer_norm(middle, gain_ref[...]).astype(norm_ref.dtype)

    for copy in (right, left, onward, backward):
        copy.wait_send()


def exchange_kernel(order, n, keys_ref, values_ref, marks_ref, keys_out, values_out, marks_out,
                    send_sem, recv_sem, local_sem):
    me = lax.axis_index("req")
    place = {"req": me, "tp": lax.axis_index("tp")}
    span = marks_ref.shape[1]

    def peer(d):
        where = dict(place, req=lax.rem(me + d + n, n))
        return tuple(where[a] for a in order)

    def windows(slot):
        part = pl.ds(slot * span, span)
        return (keys_out.at[:, :, part], values_out.at[:, part, :], marks_out.at[:, part])

    sources = (keys_ref, values_ref, marks_ref)
    barrier = pltpu.get_barrier_semaphore()
    for d in NEAR:
        pl.semaphore_signal(barrier, inc=1, device_id=peer(d), device_id_type=MESH_IDS)
    pl.semaphore_wait(barrier, len(NEAR))
    odd = lax.rem(me, 2)

    def send(kind, slices, targets, d):
        out = []
        for a, (src, dst) in enumerate(zip(slices, targets)):
            copy = pltpu.make_async_remote_copy(
                src_ref=src,
                dst_ref=dst,
                send_sem=send_sem.at[3 * kind + a],
                recv_sem=recv_sem.at[3 * kind + a],
                device_id=peer(d),
                device_id_type=MESH_IDS,
            )
            copy.start()
            out.append(copy)
        return out

    right = send(0, sources, windows(1), 1)
    left = send(1, sources, windows(3), -1)
    far = send(2, sources, windows(4 * odd), 2 - 4 * odd)
    local = []
    for a, (src, dst) in enumerate(zip(sources, windows(2))):
        copy = pltpu.make_async_copy(src, dst, local_sem.at[a])
        copy.start()
        local.append(copy)
    for a in range(3):
        right[a].wait_recv()
        left[a].wait_recv()
    relay = send(3, windows(1 + 2 * odd), windows(4 * odd), 1 - 2 * odd)
    for copy in local:
        copy.wait()
    for copy in right + left:
        copy.wait_send()
    for copy in far + relay:
        copy.wait()


def exchange(keys, values, marks, order):
    n = lax.axis_size("req")
    slots = 2 * max(NEAR) + 1
    heads, width, span = keys.shape
    any_spec = pl.BlockSpec(memory_space=pl.ANY)
    keys_all, values_all, marks_all = pl.pallas_call(
        functools.partial(exchange_kernel, order, n),
        out_shape=(
            jax.ShapeDtypeStruct((heads, width, slots * span), keys.dtype),
            jax.ShapeDtypeStruct((heads, slots * span, width), values.dtype),
            jax.ShapeDtypeStruct((1, slots * span), marks.dtype),
        ),
        in_specs=[any_spec] * 3,
        out_specs=(any_spec, any_spec, any_spec),
        scratch_shapes=[
            pltpu.SemaphoreType.DMA((12,)),
            pltpu.SemaphoreType.DMA((12,)),
            pltpu.SemaphoreType.DMA((3,)),
        ],
        compiler_params=pltpu.CompilerParams(collective_id=1, has_side_effects=True),
    )(keys, values, marks.reshape(1, span))
    source = lax.axis_index("req") + jnp.arange(slots * span, dtype=jnp.int32) // span - max(NEAR)
    present = (source >= 0) & (source < n)
    return keys_all, values_all, jnp.where(present, marks_all[0], 0)


def deliver_kernel(order, n, outgoing_ref, received_ref, send_sem, recv_sem, local_sem):
    me = lax.axis_index("req")
    place = {"req": me, "tp": lax.axis_index("tp")}

    def peer(k):
        where = dict(place, req=lax.rem(me + k, n))
        return tuple(where[a] for a in order)

    barrier = pltpu.get_barrier_semaphore()
    for k in range(1, n):
        pl.semaphore_signal(barrier, inc=1, device_id=peer(k), device_id_type=MESH_IDS)
    pl.semaphore_wait(barrier, n - 1)
    copies = []
    for k in range(1, n):
        copy = pltpu.make_async_remote_copy(
            src_ref=outgoing_ref.at[lax.rem(me + k, n)],
            dst_ref=received_ref.at[me],
            send_sem=send_sem.at[k],
            recv_sem=recv_sem.at[k],
            device_id=peer(k),
            device_id_type=MESH_IDS,
        )
        copy.start()
        copies.append(copy)
    own = pltpu.make_async_copy(outgoing_ref.at[me], received_ref.at[me], local_sem.at[0])
    own.start()
    own.wait()
    for copy in copies:
        copy.wait()


def deliver(outgoing, order):
    n = lax.axis_size("req")
    return pl.pallas_call(
        functools.partial(deliver_kernel, order, n),
        out_shape=jax.ShapeDtypeStruct(outgoing.shape, outgoing.dtype),
        in_specs=[pl.BlockSpec(memory_space=pltpu.VMEM)],
        out_specs=pl.BlockSpec(memory_space=pltpu.VMEM),
        scratch_shapes=[
            pltpu.SemaphoreType.DMA((n,)),
            pltpu.SemaphoreType.DMA((n,)),
            pltpu.SemaphoreType.DMA((1,)),
        ],
        compiler_params=pltpu.CompilerParams(collective_id=2, has_side_effects=True),
    )(outgoing)


def project(context, weight, tokens, gain, order):
    n = weight.shape[0] // context.shape[1]
    rows, cols = tokens.shape
    return pl.pallas_call(
        functools.partial(project_kernel, order),
        out_shape=(
            jax.ShapeDtypeStruct((rows, cols), jnp.float32),
            jax.ShapeDtypeStruct((rows, cols), jnp.bfloat16),
        ),
        in_specs=[pl.BlockSpec(memory_space=pltpu.VMEM)] * 4,
        out_specs=(pl.BlockSpec(memory_space=pltpu.VMEM), pl.BlockSpec(memory_space=pltpu.VMEM)),
        scratch_shapes=[
            pltpu.VMEM((n,) + context.shape, context.dtype),
            pltpu.SemaphoreType.DMA((n,)),
            pltpu.SemaphoreType.DMA((n,)),
        ],
        compiler_params=pltpu.CompilerParams(
            collective_id=0, has_side_effects=True, vmem_limit_bytes=48 * 1024 * 1024
        ),
        cost_estimate=pl.CostEstimate(
            flops=2 * rows * cols * weight.shape[0],
            bytes_accessed=4 * rows * cols + 2 * weight.size + 2 * rows * cols + 2 * n * context.size,
            transcendentals=0,
        ),
    )(context, weight, tokens, gain.reshape(1, cols))


def shifted_2(block, axis, distance):
    devices = range(lax.axis_size(axis))
    route = [(i - distance, i) for i in devices if i - distance in devices]
    return lax.ppermute(block, axis, route)


def layer_norm(stream, gain):
    center = jnp.mean(stream, axis=-1, keepdims=True)
    shifted = stream - center
    spread = jnp.mean(shifted * shifted, axis=-1, keepdims=True)
    return shifted * lax.rsqrt(spread + 1e-06) * gain.astype(jnp.float32)


def flash_kernel(bounds, q_ref, qm_ref, k_ref, v_ref, km_ref, o_ref):
    i = pl.program_id(0)
    tile = TILE
    factor = 1.0 / math.sqrt(HD)
    q = q_ref[...]
    qm = qm_ref[...]

    def step(j, carry):
        running_max, running_sum, weighted = carry
        start = pl.multiple_of(j * tile, tile)
        keys = k_ref[:, :, pl.ds(start, tile)]
        values = v_ref[:, pl.ds(start, tile), :]
        km = km_ref[:, pl.ds(start, tile)]
        scores = lax.dot_general(
            q, keys, (((2,), (1,)), ((0,), (0,))), preferred_element_type=jnp.float32
        ) * factor
        masked = jnp.where((qm == km)[None], scores, -1e30)
        new_max = jnp.maximum(running_max, jnp.max(masked, axis=2, keepdims=True))
        probs = jnp.exp(masked - new_max)
        shrink = jnp.exp(running_max - new_max)
        new_sum = running_sum * shrink + jnp.sum(probs, axis=2, keepdims=True)
        update = lax.dot_general(
            probs.astype(jnp.bfloat16), values, (((2,), (1,)), ((0,), (0,))),
            preferred_element_type=jnp.float32,
        )
        return new_max, new_sum, weighted * shrink + update

    heads, rows, width = q.shape
    init = (
        jnp.full((heads, rows, 1), -1e30, jnp.float32),
        jnp.zeros((heads, rows, 1), jnp.float32),
        jnp.zeros((heads, rows, width), jnp.float32),
    )
    _, total, weighted = lax.fori_loop(bounds[0, i], bounds[1, i], step, init)
    o_ref[...] = (weighted / total).astype(o_ref.dtype)


def attention(queries, query_marks, keys, values, key_marks):
    heads, rows, width = queries.shape
    key_rows = keys.shape[2]
    tiles = rows // TILE
    low = query_marks.reshape(tiles, TILE).min(axis=1)
    high = query_marks.reshape(tiles, TILE).max(axis=1)
    valid = (key_marks[None, :] >= low[:, None]) & (key_marks[None, :] <= high[:, None])
    place = jnp.arange(key_rows, dtype=jnp.int32)[None, :]
    first = jnp.min(jnp.where(valid, place, key_rows), axis=1)
    last = jnp.max(jnp.where(valid, place, -1), axis=1)
    bounds = jnp.stack([first // TILE, last // TILE + 1]).astype(jnp.int32)
    return pl.pallas_call(
        flash_kernel,
        out_shape=jax.ShapeDtypeStruct(queries.shape, queries.dtype),
        grid_spec=pltpu.PrefetchScalarGridSpec(
            num_scalar_prefetch=1,
            grid=(tiles,),
            in_specs=[
                pl.BlockSpec((heads, TILE, width), lambda i, b: (0, i, 0)),
                pl.BlockSpec((TILE, 1), lambda i, b: (i, 0)),
                pl.BlockSpec((heads, width, key_rows), lambda i, b: (0, 0, 0)),
                pl.BlockSpec((heads, key_rows, width), lambda i, b: (0, 0, 0)),
                pl.BlockSpec((1, key_rows), lambda i, b: (0, 0)),
            ],
            out_specs=pl.BlockSpec((heads, TILE, width), lambda i, b: (0, i, 0)),
        ),
        compiler_params=pltpu.CompilerParams(vmem_limit_bytes=48 * 1024 * 1024),
        cost_estimate=pl.CostEstimate(
            flops=4 * heads * rows * 2048 * width,
            bytes_accessed=2 * (queries.size * 2 + keys.size + values.size),
            transcendentals=heads * rows * 2048,
        ),
    )(bounds, queries, query_marks.reshape(rows, 1), keys, values, key_marks.reshape(1, key_rows))


def body(
    order,
    tokens,
    segments,
    attend_gain,
    attend_weight,
    output_weight,
    mixer_gain,
    expand_weight,
    reduce_weight,
    output_gain,
    merge_weight,
    merge_index,
    owners,
):
    token_rows = tokens.shape[0]
    head_width = attend_weight.shape[2]
    head_count = head_width // HD
    full_weight = lax.all_gather(output_weight, "tp", axis=0, tiled=True)
    stream = tokens.astype(jnp.float32)
    attend_in = layer_norm(stream, attend_gain).astype(jnp.bfloat16)
    projected = jnp.dot(
        attend_in,
        attend_weight.reshape(attend_weight.shape[0], 3 * head_width),
        preferred_element_type=jnp.float32,
    ).astype(jnp.bfloat16)
    marks = segments + 1

    def by_head(block):
        return jnp.transpose(block.reshape(block.shape[0], head_count, HD), (1, 0, 2))

    keys_all, values_all, key_marks = exchange(
        jnp.transpose(projected[:, head_width : 2 * head_width].reshape(-1, head_count, HD), (1, 2, 0)),
        by_head(projected[:, 2 * head_width :]),
        marks,
        order,
    )
    context = attention(by_head(projected[:, :head_width]), marks, keys_all, values_all, key_marks)
    context = jnp.transpose(context, (1, 0, 2)).reshape(token_rows, head_width)
    middle, mixer_in = project(context, full_weight, tokens, mixer_gain, order)
    expanded = jax.nn.gelu(
        jnp.dot(mixer_in, expand_weight, preferred_element_type=jnp.float32), approximate=False
    ).astype(jnp.bfloat16)
    hidden_terms = jnp.dot(expanded, reduce_weight, preferred_element_type=jnp.float32)
    final_stream = middle + lax.psum(hidden_terms.astype(jnp.bfloat16), "tp").astype(jnp.float32)
    final_normed = layer_norm(final_stream, output_gain).astype(jnp.bfloat16)
    merged_rows = merge_index.shape[0]
    local_index = merge_index - lax.axis_index("req") * token_rows
    picks = (local_index[:, :, None] == jnp.arange(token_rows, dtype=jnp.int32)).astype(jnp.bfloat16)
    merged = jnp.einsum(
        "mkt,tc->mkc", picks, final_normed, preferred_element_type=jnp.float32
    ).astype(jnp.bfloat16)
    feature = jnp.einsum(
        "mkc,kcd->md",
        merged,
        merge_weight.reshape(4, final_normed.shape[1], merge_weight.shape[1]),
        preferred_element_type=jnp.float32,
    ).astype(jnp.bfloat16)
    peers = lax.axis_size("req")
    capacity = 2 * merged_rows // peers
    target = owners[:, 0]
    choose = (target[:, None] == jnp.arange(peers, dtype=jnp.int32)[None, :]).astype(jnp.int32)
    slot = jnp.sum((jnp.cumsum(choose, axis=0) - 1) * choose, axis=1)
    position = target * capacity + slot
    placement = (
        position[:, None] == jnp.arange(peers * capacity, dtype=jnp.int32)[None, :]
    ).astype(jnp.bfloat16)
    outgoing = jnp.einsum(
        "ms,mc->sc", placement, feature, preferred_element_type=jnp.float32
    ).astype(jnp.bfloat16)
    outgoing = outgoing.reshape(peers, capacity, feature.shape[1])
    received = deliver(outgoing, order)
    return received.reshape(1, peers, capacity, feature.shape[1])


def solution(mesh):
    placed = (
        P("req", None),
        P("req"),
        P(),
        P(None, None, "tp"),
        P("tp", None),
        P(),
        P(None, "tp"),
        P("tp", None),
        P(),
        P(None, "tp"),
        P("req", None),
        P("req", None),
    )
    return jax.shard_map(
        functools.partial(body, tuple(mesh.axis_names)), mesh=mesh, in_specs=placed, out_specs=P("req", None, None, "tp"), check_vma=False
    )
```

```python
import functools
import math

import jax
import jax.numpy as jnp
from jax import lax
from jax.experimental import pallas as pl
from jax.experimental.pallas import tpu as pltpu
from jax.sharding import PartitionSpec as P

HD = 80
TILE = 256
NEAR = (1, -1, 2, -2)
MESH_IDS = pl.DeviceIdType.MESH


def project_kernel(order, ctx_ref, weight_ref, tokens_ref, gain_ref, out_ref, norm_ref, slots, send_sem,
                   recv_sem):
    n = slots.shape[0]
    rows, width = ctx_ref.shape
    cols = out_ref.shape[1]
    half = rows // 2
    me = lax.axis_index("tp")
    place = {"tp": me, "req": lax.axis_index("req")}

    def peer(k):
        where = dict(place, tp=lax.rem(me + k, n))
        return tuple(where[a] for a in order)

    def send(src, dst, sem, k):
        copy = pltpu.make_async_remote_copy(
            src_ref=src,
            dst_ref=dst,
            send_sem=send_sem.at[sem],
            recv_sem=recv_sem.at[sem],
            device_id=peer(k),
            device_id_type=MESH_IDS,
        )
        copy.start()
        return copy

    barrier = pltpu.get_barrier_semaphore()
    for k in (1, n - 1):
        pl.semaphore_signal(barrier, inc=1, device_id=peer(k), device_id_type=MESH_IDS)
    pl.semaphore_wait(barrier, 2)
    right = send(ctx_ref, slots.at[1], 1, 1)
    left = send(ctx_ref, slots.at[3], 3, n - 1)
    tile = 256

    def add_term(block, source, first):
        base = pl.multiple_of(source * width, 8)

        @pl.loop(0, rows // tile)
        def _(i):
            r = pl.ds(pl.multiple_of(i * tile, tile), tile)

            @pl.loop(0, cols // tile)
            def _(j):
                c = pl.ds(pl.multiple_of(j * tile, tile), tile)
                term = jnp.dot(
                    block[r, :], weight_ref[pl.ds(base, width), c], preferred_element_type=jnp.float32
                )
                term = term.astype(jnp.bfloat16).astype(jnp.float32)
                if first:
                    out_ref[r, c] = term
                else:
                    out_ref[r, c] = out_ref[r, c] + term

    add_term(ctx_ref, me, True)
    right.wait_recv()
    onward = send(slots.at[1, pl.ds(0, half)], slots.at[2, pl.ds(0, half)], 2, 1)
    add_term(slots.at[1], lax.rem(me + n - 1, n), False)
    left.wait_recv()
    backward = send(slots.at[3, pl.ds(half, half)], slots.at[2, pl.ds(half, half)], 0, n - 1)
    add_term(slots.at[3], lax.rem(me + 1, n), False)
    onward.wait_recv()
    backward.wait_recv()
    add_term(slots.at[2], lax.rem(me + 2, n), False)

    @pl.loop(0, rows // tile)
    def _(i):
        r = pl.ds(pl.multiple_of(i * tile, tile), tile)
        middle = out_ref[r, :] + tokens_ref[r, :].astype(jnp.float32)
        out_ref[r, :] = middle
        norm_ref[r, :] = layer_norm(middle, gain_ref[...]).astype(norm_ref.dtype)

    for copy in (right, left, onward, backward):
        copy.wait_send()


def exchange_kernel(order, n, keys_ref, values_ref, marks_ref, keys_out, values_out, marks_out,
                    send_sem, recv_sem, local_sem):
    me = lax.axis_index("req")
    place = {"req": me, "tp": lax.axis_index("tp")}
    span = marks_ref.shape[1]

    def peer(d):
        where = dict(place, req=lax.rem(me + d + n, n))
        return tuple(where[a] for a in order)

    def windows(slot):
        part = pl.ds(slot * span, span)
        return (keys_out.at[:, :, part], values_out.at[:, part, :], marks_out.at[:, part])

    sources = (keys_ref, values_ref, marks_ref)
    barrier = pltpu.get_barrier_semaphore()
    for d in NEAR:
        pl.semaphore_signal(barrier, inc=1, device_id=peer(d), device_id_type=MESH_IDS)
    pl.semaphore_wait(barrier, len(NEAR))
    odd = lax.rem(me, 2)

    def send(kind, slices, targets, d):
        out = []
        for a, (src, dst) in enumerate(zip(slices, targets)):
            copy = pltpu.make_async_remote_copy(
                src_ref=src,
                dst_ref=dst,
                send_sem=send_sem.at[3 * kind + a],
                recv_sem=recv_sem.at[3 * kind + a],
                device_id=peer(d),
                device_id_type=MESH_IDS,
            )
            copy.start()
            out.append(copy)
        return out

    right = send(0, sources, windows(1), 1)
    left = send(1, sources, windows(3), -1)
    far = send(2, sources, windows(4 * odd), 2 - 4 * odd)
    local = []
    for a, (src, dst) in enumerate(zip(sources, windows(2))):
        copy = pltpu.make_async_copy(src, dst, local_sem.at[a])
        copy.start()
        local.append(copy)
    for a in range(3):
        right[a].wait_recv()
        left[a].wait_recv()
    relay = send(3, windows(1 + 2 * odd), windows(4 * odd), 1 - 2 * odd)
    for copy in local:
        copy.wait()
    for copy in right + left:
        copy.wait_send()
    for copy in far + relay:
        copy.wait()


def exchange(keys, values, marks, order):
    n = lax.axis_size("req")
    slots = 2 * max(NEAR) + 1
    heads, width, span = keys.shape
    any_spec = pl.BlockSpec(memory_space=pl.ANY)
    keys_all, values_all, marks_all = pl.pallas_call(
        functools.partial(exchange_kernel, order, n),
        out_shape=(
            jax.ShapeDtypeStruct((heads, width, slots * span), keys.dtype),
            jax.ShapeDtypeStruct((heads, slots * span, width), values.dtype),
            jax.ShapeDtypeStruct((1, slots * span), marks.dtype),
        ),
        in_specs=[any_spec] * 3,
        out_specs=(any_spec, any_spec, any_spec),
        scratch_shapes=[
            pltpu.SemaphoreType.DMA((12,)),
            pltpu.SemaphoreType.DMA((12,)),
            pltpu.SemaphoreType.DMA((3,)),
        ],
        compiler_params=pltpu.CompilerParams(collective_id=1, has_side_effects=True),
    )(keys, values, marks.reshape(1, span))
    source = lax.axis_index("req") + jnp.arange(slots * span, dtype=jnp.int32) // span - max(NEAR)
    present = (source >= 0) & (source < n)
    return keys_all, values_all, jnp.where(present, marks_all[0], 0)


def deliver_kernel(order, n, outgoing_ref, received_ref, send_sem, recv_sem, local_sem):
    me = lax.axis_index("req")
    place = {"req": me, "tp": lax.axis_index("tp")}

    def peer(k):
        where = dict(place, req=lax.rem(me + k, n))
        return tuple(where[a] for a in order)

    barrier = pltpu.get_barrier_semaphore()
    for k in range(1, n):
        pl.semaphore_signal(barrier, inc=1, device_id=peer(k), device_id_type=MESH_IDS)
    pl.semaphore_wait(barrier, n - 1)
    copies = []
    for k in range(1, n):
        copy = pltpu.make_async_remote_copy(
            src_ref=outgoing_ref.at[lax.rem(me + k, n)],
            dst_ref=received_ref.at[me],
            send_sem=send_sem.at[k],
            recv_sem=recv_sem.at[k],
            device_id=peer(k),
            device_id_type=MESH_IDS,
        )
        copy.start()
        copies.append(copy)
    own = pltpu.make_async_copy(outgoing_ref.at[me], received_ref.at[me], local_sem.at[0])
    own.start()
    own.wait()
    for copy in copies:
        copy.wait()


def deliver(outgoing, order):
    n = lax.axis_size("req")
    return pl.pallas_call(
        functools.partial(deliver_kernel, order, n),
        out_shape=jax.ShapeDtypeStruct(outgoing.shape, outgoing.dtype),
        in_specs=[pl.BlockSpec(memory_space=pltpu.VMEM)],
        out_specs=pl.BlockSpec(memory_space=pltpu.VMEM),
        scratch_shapes=[
            pltpu.SemaphoreType.DMA((n,)),
            pltpu.SemaphoreType.DMA((n,)),
            pltpu.SemaphoreType.DMA((1,)),
        ],
        compiler_params=pltpu.CompilerParams(collective_id=2, has_side_effects=True),
    )(outgoing)


def norm_kernel(*refs):
    *inputs, gain_ref, out_ref = refs
    stream = inputs[0][...].astype(jnp.float32)
    for extra in inputs[1:]:
        stream = stream + extra[...].astype(jnp.float32)
    out_ref[...] = layer_norm(stream, gain_ref[...]).astype(out_ref.dtype)


def norm_rows(inputs, gain):
    rows, cols = inputs[0].shape
    block = pl.BlockSpec((TILE, cols), lambda i: (i, 0))
    return pl.pallas_call(
        norm_kernel,
        out_shape=jax.ShapeDtypeStruct((rows, cols), jnp.bfloat16),
        grid=(rows // TILE,),
        in_specs=[block] * len(inputs) + [pl.BlockSpec((1, cols), lambda i: (0, 0))],
        out_specs=block,
    )(*inputs, gain.reshape(1, cols))


def project(context, weight, tokens, gain, order):
    n = weight.shape[0] // context.shape[1]
    rows, cols = tokens.shape
    return pl.pallas_call(
        functools.partial(project_kernel, order),
        out_shape=(
            jax.ShapeDtypeStruct((rows, cols), jnp.float32),
            jax.ShapeDtypeStruct((rows, cols), jnp.bfloat16),
        ),
        in_specs=[pl.BlockSpec(memory_space=pltpu.VMEM)] * 4,
        out_specs=(pl.BlockSpec(memory_space=pltpu.VMEM), pl.BlockSpec(memory_space=pltpu.VMEM)),
        scratch_shapes=[
            pltpu.VMEM((n,) + context.shape, context.dtype),
            pltpu.SemaphoreType.DMA((n,)),
            pltpu.SemaphoreType.DMA((n,)),
        ],
        compiler_params=pltpu.CompilerParams(
            collective_id=0, has_side_effects=True, vmem_limit_bytes=48 * 1024 * 1024
        ),
        cost_estimate=pl.CostEstimate(
            flops=2 * rows * cols * weight.shape[0],
            bytes_accessed=4 * rows * cols + 2 * weight.size + 2 * rows * cols + 2 * n * context.size,
            transcendentals=0,
        ),
    )(context, weight, tokens, gain.reshape(1, cols))


def shifted_2(block, axis, distance):
    devices = range(lax.axis_size(axis))
    route = [(i - distance, i) for i in devices if i - distance in devices]
    return lax.ppermute(block, axis, route)


def layer_norm(stream, gain):
    center = jnp.mean(stream, axis=-1, keepdims=True)
    shifted = stream - center
    spread = jnp.mean(shifted * shifted, axis=-1, keepdims=True)
    return shifted * lax.rsqrt(spread + 1e-06) * gain.astype(jnp.float32)


def flash_kernel(bounds, q_ref, qm_ref, k_ref, v_ref, km_ref, o_ref):
    i = pl.program_id(0)
    tile = TILE
    factor = 1.0 / math.sqrt(HD)
    q = q_ref[...]
    qm = qm_ref[...]

    def step(j, carry):
        running_max, running_sum, weighted = carry
        start = pl.multiple_of(j * tile, tile)
        keys = k_ref[:, :, pl.ds(start, tile)]
        values = v_ref[:, pl.ds(start, tile), :]
        km = km_ref[:, pl.ds(start, tile)]
        scores = lax.dot_general(
            q, keys, (((2,), (1,)), ((0,), (0,))), preferred_element_type=jnp.float32
        ) * factor
        masked = jnp.where((qm == km)[None], scores, -1e30)
        new_max = jnp.maximum(running_max, jnp.max(masked, axis=2, keepdims=True))
        probs = jnp.exp(masked - new_max)
        shrink = jnp.exp(running_max - new_max)
        new_sum = running_sum * shrink + jnp.sum(probs, axis=2, keepdims=True)
        update = lax.dot_general(
            probs.astype(jnp.bfloat16), values, (((2,), (1,)), ((0,), (0,))),
            preferred_element_type=jnp.float32,
        )
        return new_max, new_sum, weighted * shrink + update

    heads, rows, width = q.shape
    init = (
        jnp.full((heads, rows, 1), -1e30, jnp.float32),
        jnp.zeros((heads, rows, 1), jnp.float32),
        jnp.zeros((heads, rows, width), jnp.float32),
    )
    _, total, weighted = lax.fori_loop(bounds[0, i], bounds[1, i], step, init)
    o_ref[...] = (weighted / total).astype(o_ref.dtype)


def attention(queries, query_marks, keys, values, key_marks):
    heads, rows, width = queries.shape
    key_rows = keys.shape[2]
    tiles = rows // TILE
    low = query_marks.reshape(tiles, TILE).min(axis=1)
    high = query_marks.reshape(tiles, TILE).max(axis=1)
    valid = (key_marks[None, :] >= low[:, None]) & (key_marks[None, :] <= high[:, None])
    place = jnp.arange(key_rows, dtype=jnp.int32)[None, :]
    first = jnp.min(jnp.where(valid, place, key_rows), axis=1)
    last = jnp.max(jnp.where(valid, place, -1), axis=1)
    bounds = jnp.stack([first // TILE, last // TILE + 1]).astype(jnp.int32)
    return pl.pallas_call(
        flash_kernel,
        out_shape=jax.ShapeDtypeStruct(queries.shape, queries.dtype),
        grid_spec=pltpu.PrefetchScalarGridSpec(
            num_scalar_prefetch=1,
            grid=(tiles,),
            in_specs=[
                pl.BlockSpec((heads, TILE, width), lambda i, b: (0, i, 0)),
                pl.BlockSpec((TILE, 1), lambda i, b: (i, 0)),
                pl.BlockSpec((heads, width, key_rows), lambda i, b: (0, 0, 0)),
                pl.BlockSpec((heads, key_rows, width), lambda i, b: (0, 0, 0)),
                pl.BlockSpec((1, key_rows), lambda i, b: (0, 0)),
            ],
            out_specs=pl.BlockSpec((heads, TILE, width), lambda i, b: (0, i, 0)),
        ),
        compiler_params=pltpu.CompilerParams(vmem_limit_bytes=48 * 1024 * 1024),
        cost_estimate=pl.CostEstimate(
            flops=4 * heads * rows * 2048 * width,
            bytes_accessed=2 * (queries.size * 2 + keys.size + values.size),
            transcendentals=heads * rows * 2048,
        ),
    )(bounds, queries, query_marks.reshape(rows, 1), keys, values, key_marks.reshape(1, key_rows))


def body(
    order,
    tokens,
    segments,
    attend_gain,
    attend_weight,
    output_weight,
    mixer_gain,
    expand_weight,
    reduce_weight,
    output_gain,
    merge_weight,
    merge_index,
    owners,
):
    token_rows = tokens.shape[0]
    head_width = attend_weight.shape[2]
    head_count = head_width // HD
    full_weight = lax.all_gather(output_weight, "tp", axis=0, tiled=True)
    attend_in = norm_rows([tokens], attend_gain)
    projected = jnp.dot(
        attend_in,
        attend_weight.reshape(attend_weight.shape[0], 3 * head_width),
        preferred_element_type=jnp.float32,
    ).astype(jnp.bfloat16)
    marks = segments + 1

    def by_head(block):
        return jnp.transpose(block.reshape(block.shape[0], head_count, HD), (1, 0, 2))

    keys_all, values_all, key_marks = exchange(
        jnp.transpose(projected[:, head_width : 2 * head_width].reshape(-1, head_count, HD), (1, 2, 0)),
        by_head(projected[:, 2 * head_width :]),
        marks,
        order,
    )
    context = attention(by_head(projected[:, :head_width]), marks, keys_all, values_all, key_marks)
    context = jnp.transpose(context, (1, 0, 2)).reshape(token_rows, head_width)
    middle, mixer_in = project(context, full_weight, tokens, mixer_gain, order)
    expanded = jax.nn.gelu(
        jnp.dot(mixer_in, expand_weight, preferred_element_type=jnp.float32), approximate=False
    ).astype(jnp.bfloat16)
    hidden_terms = jnp.dot(expanded, reduce_weight, preferred_element_type=jnp.float32)
    final_normed = norm_rows([middle, lax.psum(hidden_terms.astype(jnp.bfloat16), "tp")], output_gain)
    merged_rows = merge_index.shape[0]
    local_index = merge_index - lax.axis_index("req") * token_rows
    picks = (local_index[:, :, None] == jnp.arange(token_rows, dtype=jnp.int32)).astype(jnp.bfloat16)
    merged = jnp.einsum(
        "mkt,tc->mkc", picks, final_normed, preferred_element_type=jnp.float32
    ).astype(jnp.bfloat16)
    feature = jnp.einsum(
        "mkc,kcd->md",
        merged,
        merge_weight.reshape(4, final_normed.shape[1], merge_weight.shape[1]),
        preferred_element_type=jnp.float32,
    ).astype(jnp.bfloat16)
    peers = lax.axis_size("req")
    capacity = 2 * merged_rows // peers
    target = owners[:, 0]
    choose = (target[:, None] == jnp.arange(peers, dtype=jnp.int32)[None, :]).astype(jnp.int32)
    slot = jnp.sum((jnp.cumsum(choose, axis=0) - 1) * choose, axis=1)
    position = target * capacity + slot
    placement = (
        position[:, None] == jnp.arange(peers * capacity, dtype=jnp.int32)[None, :]
    ).astype(jnp.bfloat16)
    outgoing = jnp.einsum(
        "ms,mc->sc", placement, feature, preferred_element_type=jnp.float32
    ).astype(jnp.bfloat16)
    outgoing = outgoing.reshape(peers, capacity, feature.shape[1])
    received = deliver(outgoing, order)
    return received.reshape(1, peers, capacity, feature.shape[1])


def solution(mesh):
    placed = (
        P("req", None),
        P("req"),
        P(),
        P(None, None, "tp"),
        P("tp", None),
        P(),
        P(None, "tp"),
        P("tp", None),
        P(),
        P(None, "tp"),
        P("req", None),
        P("req", None),
    )
    return jax.shard_map(
        functools.partial(body, tuple(mesh.axis_names)), mesh=mesh, in_specs=placed, out_specs=P("req", None, None, "tp"), check_vma=False
    )
```

```python
import functools
import math

import jax
import jax.numpy as jnp
from jax import lax
from jax.experimental import pallas as pl
from jax.experimental.pallas import tpu as pltpu
from jax.sharding import PartitionSpec as P

HD = 80
TILE = 256
QTILE = 128
NEAR = (1, -1, 2, -2)
MESH_IDS = pl.DeviceIdType.MESH


def project_kernel(order, ctx_ref, weight_ref, tokens_ref, gain_ref, out_ref, norm_ref, slots, send_sem,
                   recv_sem):
    n = slots.shape[0]
    rows, width = ctx_ref.shape
    cols = out_ref.shape[1]
    half = rows // 2
    me = lax.axis_index("tp")
    place = {"tp": me, "req": lax.axis_index("req")}

    def peer(k):
        where = dict(place, tp=lax.rem(me + k, n))
        return tuple(where[a] for a in order)

    def send(src, dst, sem, k):
        copy = pltpu.make_async_remote_copy(
            src_ref=src,
            dst_ref=dst,
            send_sem=send_sem.at[sem],
            recv_sem=recv_sem.at[sem],
            device_id=peer(k),
            device_id_type=MESH_IDS,
        )
        copy.start()
        return copy

    barrier = pltpu.get_barrier_semaphore()
    for k in (1, n - 1):
        pl.semaphore_signal(barrier, inc=1, device_id=peer(k), device_id_type=MESH_IDS)
    pl.semaphore_wait(barrier, 2)
    right = send(ctx_ref, slots.at[1], 1, 1)
    left = send(ctx_ref, slots.at[3], 3, n - 1)
    tile = 256

    def add_term(block, source, first):
        base = pl.multiple_of(source * width, 8)

        @pl.loop(0, rows // tile)
        def _(i):
            r = pl.ds(pl.multiple_of(i * tile, tile), tile)

            @pl.loop(0, cols // tile)
            def _(j):
                c = pl.ds(pl.multiple_of(j * tile, tile), tile)
                term = jnp.dot(
                    block[r, :], weight_ref[pl.ds(base, width), c], preferred_element_type=jnp.float32
                )
                term = term.astype(jnp.bfloat16).astype(jnp.float32)
                if first:
                    out_ref[r, c] = term
                else:
                    out_ref[r, c] = out_ref[r, c] + term

    add_term(ctx_ref, me, True)
    right.wait_recv()
    onward = send(slots.at[1, pl.ds(0, half)], slots.at[2, pl.ds(0, half)], 2, 1)
    add_term(slots.at[1], lax.rem(me + n - 1, n), False)
    left.wait_recv()
    backward = send(slots.at[3, pl.ds(half, half)], slots.at[2, pl.ds(half, half)], 0, n - 1)
    add_term(slots.at[3], lax.rem(me + 1, n), False)
    onward.wait_recv()
    backward.wait_recv()
    add_term(slots.at[2], lax.rem(me + 2, n), False)

    @pl.loop(0, rows // tile)
    def _(i):
        r = pl.ds(pl.multiple_of(i * tile, tile), tile)
        middle = out_ref[r, :] + tokens_ref[r, :].astype(jnp.float32)
        out_ref[r, :] = middle
        norm_ref[r, :] = layer_norm(middle, gain_ref[...]).astype(norm_ref.dtype)

    for copy in (right, left, onward, backward):
        copy.wait_send()


def exchange_kernel(order, n, keys_ref, values_ref, marks_ref, keys_out, values_out, marks_out,
                    send_sem, recv_sem, local_sem):
    me = lax.axis_index("req")
    place = {"req": me, "tp": lax.axis_index("tp")}
    span = marks_ref.shape[1]

    def peer(d):
        where = dict(place, req=lax.rem(me + d + n, n))
        return tuple(where[a] for a in order)

    def windows(slot):
        part = pl.ds(slot * span, span)
        return (keys_out.at[:, :, part], values_out.at[:, part, :], marks_out.at[:, part])

    sources = (keys_ref, values_ref, marks_ref)
    barrier = pltpu.get_barrier_semaphore()
    for d in NEAR:
        pl.semaphore_signal(barrier, inc=1, device_id=peer(d), device_id_type=MESH_IDS)
    pl.semaphore_wait(barrier, len(NEAR))
    odd = lax.rem(me, 2)

    def send(kind, slices, targets, d):
        out = []
        for a, (src, dst) in enumerate(zip(slices, targets)):
            copy = pltpu.make_async_remote_copy(
                src_ref=src,
                dst_ref=dst,
                send_sem=send_sem.at[3 * kind + a],
                recv_sem=recv_sem.at[3 * kind + a],
                device_id=peer(d),
                device_id_type=MESH_IDS,
            )
            copy.start()
            out.append(copy)
        return out

    right = send(0, sources, windows(1), 1)
    left = send(1, sources, windows(3), -1)
    far = send(2, sources, windows(4 * odd), 2 - 4 * odd)
    local = []
    for a, (src, dst) in enumerate(zip(sources, windows(2))):
        copy = pltpu.make_async_copy(src, dst, local_sem.at[a])
        copy.start()
        local.append(copy)
    for a in range(3):
        right[a].wait_recv()
        left[a].wait_recv()
    relay = send(3, windows(1 + 2 * odd), windows(4 * odd), 1 - 2 * odd)
    for copy in local:
        copy.wait()
    for copy in right + left:
        copy.wait_send()
    for copy in far + relay:
        copy.wait()


def exchange(keys, values, marks, order):
    n = lax.axis_size("req")
    slots = 2 * max(NEAR) + 1
    heads, width, span = keys.shape
    any_spec = pl.BlockSpec(memory_space=pl.ANY)
    keys_all, values_all, marks_all = pl.pallas_call(
        functools.partial(exchange_kernel, order, n),
        out_shape=(
            jax.ShapeDtypeStruct((heads, width, slots * span), keys.dtype),
            jax.ShapeDtypeStruct((heads, slots * span, width), values.dtype),
            jax.ShapeDtypeStruct((1, slots * span), marks.dtype),
        ),
        in_specs=[any_spec] * 3,
        out_specs=(any_spec, any_spec, any_spec),
        scratch_shapes=[
            pltpu.SemaphoreType.DMA((12,)),
            pltpu.SemaphoreType.DMA((12,)),
            pltpu.SemaphoreType.DMA((3,)),
        ],
        compiler_params=pltpu.CompilerParams(collective_id=1, has_side_effects=True),
    )(keys, values, marks.reshape(1, span))
    source = lax.axis_index("req") + jnp.arange(slots * span, dtype=jnp.int32) // span - max(NEAR)
    present = (source >= 0) & (source < n)
    return keys_all, values_all, jnp.where(present, marks_all[0], 0)


def deliver_kernel(order, n, outgoing_ref, received_ref, send_sem, recv_sem, local_sem):
    me = lax.axis_index("req")
    place = {"req": me, "tp": lax.axis_index("tp")}

    def peer(k):
        where = dict(place, req=lax.rem(me + k, n))
        return tuple(where[a] for a in order)

    barrier = pltpu.get_barrier_semaphore()
    for k in range(1, n):
        pl.semaphore_signal(barrier, inc=1, device_id=peer(k), device_id_type=MESH_IDS)
    pl.semaphore_wait(barrier, n - 1)
    copies = []
    for k in range(1, n):
        copy = pltpu.make_async_remote_copy(
            src_ref=outgoing_ref.at[lax.rem(me + k, n)],
            dst_ref=received_ref.at[me],
            send_sem=send_sem.at[k],
            recv_sem=recv_sem.at[k],
            device_id=peer(k),
            device_id_type=MESH_IDS,
        )
        copy.start()
        copies.append(copy)
    own = pltpu.make_async_copy(outgoing_ref.at[me], received_ref.at[me], local_sem.at[0])
    own.start()
    own.wait()
    for copy in copies:
        copy.wait()


def deliver(outgoing, order):
    n = lax.axis_size("req")
    return pl.pallas_call(
        functools.partial(deliver_kernel, order, n),
        out_shape=jax.ShapeDtypeStruct(outgoing.shape, outgoing.dtype),
        in_specs=[pl.BlockSpec(memory_space=pltpu.VMEM)],
        out_specs=pl.BlockSpec(memory_space=pltpu.VMEM),
        scratch_shapes=[
            pltpu.SemaphoreType.DMA((n,)),
            pltpu.SemaphoreType.DMA((n,)),
            pltpu.SemaphoreType.DMA((1,)),
        ],
        compiler_params=pltpu.CompilerParams(collective_id=2, has_side_effects=True),
    )(outgoing)


def project(context, weight, tokens, gain, order):
    n = weight.shape[0] // context.shape[1]
    rows, cols = tokens.shape
    return pl.pallas_call(
        functools.partial(project_kernel, order),
        out_shape=(
            jax.ShapeDtypeStruct((rows, cols), jnp.float32),
            jax.ShapeDtypeStruct((rows, cols), jnp.bfloat16),
        ),
        in_specs=[pl.BlockSpec(memory_space=pltpu.VMEM)] * 4,
        out_specs=(pl.BlockSpec(memory_space=pltpu.VMEM), pl.BlockSpec(memory_space=pltpu.VMEM)),
        scratch_shapes=[
            pltpu.VMEM((n,) + context.shape, context.dtype),
            pltpu.SemaphoreType.DMA((n,)),
            pltpu.SemaphoreType.DMA((n,)),
        ],
        compiler_params=pltpu.CompilerParams(
            collective_id=0, has_side_effects=True, vmem_limit_bytes=48 * 1024 * 1024
        ),
        cost_estimate=pl.CostEstimate(
            flops=2 * rows * cols * weight.shape[0],
            bytes_accessed=4 * rows * cols + 2 * weight.size + 2 * rows * cols + 2 * n * context.size,
            transcendentals=0,
        ),
    )(context, weight, tokens, gain.reshape(1, cols))


def shifted_2(block, axis, distance):
    devices = range(lax.axis_size(axis))
    route = [(i - distance, i) for i in devices if i - distance in devices]
    return lax.ppermute(block, axis, route)


def layer_norm(stream, gain):
    center = jnp.mean(stream, axis=-1, keepdims=True)
    shifted = stream - center
    spread = jnp.mean(shifted * shifted, axis=-1, keepdims=True)
    return shifted * lax.rsqrt(spread + 1e-06) * gain.astype(jnp.float32)


def flash_kernel(bounds, q_ref, qm_ref, k_ref, v_ref, km_ref, o_ref):
    i = pl.program_id(0)
    tile = TILE
    factor = 1.0 / math.sqrt(HD)
    q = q_ref[...]
    qm = qm_ref[...]

    def step(j, carry):
        running_max, running_sum, weighted = carry
        start = pl.multiple_of(j * tile, tile)
        keys = k_ref[:, :, pl.ds(start, tile)]
        values = v_ref[:, pl.ds(start, tile), :]
        km = km_ref[:, pl.ds(start, tile)]
        scores = lax.dot_general(
            q, keys, (((2,), (1,)), ((0,), (0,))), preferred_element_type=jnp.float32
        ) * factor
        masked = jnp.where((qm == km)[None], scores, -1e30)
        new_max = jnp.maximum(running_max, jnp.max(masked, axis=2, keepdims=True))
        probs = jnp.exp(masked - new_max)
        shrink = jnp.exp(running_max - new_max)
        new_sum = running_sum * shrink + jnp.sum(probs, axis=2, keepdims=True)
        update = lax.dot_general(
            probs.astype(jnp.bfloat16), values, (((2,), (1,)), ((0,), (0,))),
            preferred_element_type=jnp.float32,
        )
        return new_max, new_sum, weighted * shrink + update

    heads, rows, width = q.shape
    init = (
        jnp.full((heads, rows, 1), -1e30, jnp.float32),
        jnp.zeros((heads, rows, 1), jnp.float32),
        jnp.zeros((heads, rows, width), jnp.float32),
    )
    _, total, weighted = lax.fori_loop(bounds[0, i], bounds[1, i], step, init)
    o_ref[...] = (weighted / total).astype(o_ref.dtype)


def attention(queries, query_marks, keys, values, key_marks):
    heads, rows, width = queries.shape
    key_rows = keys.shape[2]
    tiles = rows // QTILE
    low = query_marks.reshape(tiles, QTILE).min(axis=1)
    high = query_marks.reshape(tiles, QTILE).max(axis=1)
    valid = (key_marks[None, :] >= low[:, None]) & (key_marks[None, :] <= high[:, None])
    place = jnp.arange(key_rows, dtype=jnp.int32)[None, :]
    first = jnp.min(jnp.where(valid, place, key_rows), axis=1)
    last = jnp.max(jnp.where(valid, place, -1), axis=1)
    bounds = jnp.stack([first // TILE, last // TILE + 1]).astype(jnp.int32)
    return pl.pallas_call(
        flash_kernel,
        out_shape=jax.ShapeDtypeStruct(queries.shape, queries.dtype),
        grid_spec=pltpu.PrefetchScalarGridSpec(
            num_scalar_prefetch=1,
            grid=(tiles,),
            in_specs=[
                pl.BlockSpec((heads, QTILE, width), lambda i, b: (0, i, 0)),
                pl.BlockSpec((QTILE, 1), lambda i, b: (i, 0)),
                pl.BlockSpec((heads, width, key_rows), lambda i, b: (0, 0, 0)),
                pl.BlockSpec((heads, key_rows, width), lambda i, b: (0, 0, 0)),
                pl.BlockSpec((1, key_rows), lambda i, b: (0, 0)),
            ],
            out_specs=pl.BlockSpec((heads, QTILE, width), lambda i, b: (0, i, 0)),
        ),
        compiler_params=pltpu.CompilerParams(vmem_limit_bytes=48 * 1024 * 1024),
        cost_estimate=pl.CostEstimate(
            flops=4 * heads * rows * 2048 * width,
            bytes_accessed=2 * (queries.size * 2 + keys.size + values.size),
            transcendentals=heads * rows * 2048,
        ),
    )(bounds, queries, query_marks.reshape(rows, 1), keys, values, key_marks.reshape(1, key_rows))


def body(
    order,
    tokens,
    segments,
    attend_gain,
    attend_weight,
    output_weight,
    mixer_gain,
    expand_weight,
    reduce_weight,
    output_gain,
    merge_weight,
    merge_index,
    owners,
):
    token_rows = tokens.shape[0]
    head_width = attend_weight.shape[2]
    head_count = head_width // HD
    full_weight = lax.all_gather(output_weight, "tp", axis=0, tiled=True)
    stream = tokens.astype(jnp.float32)
    attend_in = layer_norm(stream, attend_gain).astype(jnp.bfloat16)
    projected = jnp.dot(
        attend_in,
        attend_weight.reshape(attend_weight.shape[0], 3 * head_width),
        preferred_element_type=jnp.float32,
    ).astype(jnp.bfloat16)
    marks = segments + 1

    def by_head(block):
        return jnp.transpose(block.reshape(block.shape[0], head_count, HD), (1, 0, 2))

    keys_all, values_all, key_marks = exchange(
        jnp.transpose(projected[:, head_width : 2 * head_width].reshape(-1, head_count, HD), (1, 2, 0)),
        by_head(projected[:, 2 * head_width :]),
        marks,
        order,
    )
    context = attention(by_head(projected[:, :head_width]), marks, keys_all, values_all, key_marks)
    context = jnp.transpose(context, (1, 0, 2)).reshape(token_rows, head_width)
    middle, mixer_in = project(context, full_weight, tokens, mixer_gain, order)
    expanded = jax.nn.gelu(
        jnp.dot(mixer_in, expand_weight, preferred_element_type=jnp.float32), approximate=False
    ).astype(jnp.bfloat16)
    hidden_terms = jnp.dot(expanded, reduce_weight, preferred_element_type=jnp.float32)
    final_stream = middle + lax.psum(hidden_terms.astype(jnp.bfloat16), "tp").astype(jnp.float32)
    final_normed = layer_norm(final_stream, output_gain).astype(jnp.bfloat16)
    merged_rows = merge_index.shape[0]
    local_index = merge_index - lax.axis_index("req") * token_rows
    picks = (local_index[:, :, None] == jnp.arange(token_rows, dtype=jnp.int32)).astype(jnp.bfloat16)
    merged = jnp.einsum(
        "mkt,tc->mkc", picks, final_normed, preferred_element_type=jnp.float32
    ).astype(jnp.bfloat16)
    feature = jnp.einsum(
        "mkc,kcd->md",
        merged,
        merge_weight.reshape(4, final_normed.shape[1], merge_weight.shape[1]),
        preferred_element_type=jnp.float32,
    ).astype(jnp.bfloat16)
    peers = lax.axis_size("req")
    capacity = 2 * merged_rows // peers
    target = owners[:, 0]
    choose = (target[:, None] == jnp.arange(peers, dtype=jnp.int32)[None, :]).astype(jnp.int32)
    slot = jnp.sum((jnp.cumsum(choose, axis=0) - 1) * choose, axis=1)
    position = target * capacity + slot
    placement = (
        position[:, None] == jnp.arange(peers * capacity, dtype=jnp.int32)[None, :]
    ).astype(jnp.bfloat16)
    outgoing = jnp.einsum(
        "ms,mc->sc", placement, feature, preferred_element_type=jnp.float32
    ).astype(jnp.bfloat16)
    outgoing = outgoing.reshape(peers, capacity, feature.shape[1])
    received = deliver(outgoing, order)
    return received.reshape(1, peers, capacity, feature.shape[1])


def solution(mesh):
    placed = (
        P("req", None),
        P("req"),
        P(),
        P(None, None, "tp"),
        P("tp", None),
        P(),
        P(None, "tp"),
        P("tp", None),
        P(),
        P(None, "tp"),
        P("req", None),
        P("req", None),
    )
    return jax.shard_map(
        functools.partial(body, tuple(mesh.axis_names)), mesh=mesh, in_specs=placed, out_specs=P("req", None, None, "tp"), check_vma=False
    )
```

```python
import functools
import math

import jax
import jax.numpy as jnp
from jax import lax
from jax.experimental import pallas as pl
from jax.experimental.pallas import tpu as pltpu
from jax.sharding import PartitionSpec as P

HD = 80
TILE = 256
QTILE = 512
NEAR = (1, -1, 2, -2)
MESH_IDS = pl.DeviceIdType.MESH


def project_kernel(order, ctx_ref, weight_ref, tokens_ref, gain_ref, out_ref, norm_ref, slots, send_sem,
                   recv_sem):
    n = slots.shape[0]
    rows, width = ctx_ref.shape
    cols = out_ref.shape[1]
    half = rows // 2
    me = lax.axis_index("tp")
    place = {"tp": me, "req": lax.axis_index("req")}

    def peer(k):
        where = dict(place, tp=lax.rem(me + k, n))
        return tuple(where[a] for a in order)

    def send(src, dst, sem, k):
        copy = pltpu.make_async_remote_copy(
            src_ref=src,
            dst_ref=dst,
            send_sem=send_sem.at[sem],
            recv_sem=recv_sem.at[sem],
            device_id=peer(k),
            device_id_type=MESH_IDS,
        )
        copy.start()
        return copy

    barrier = pltpu.get_barrier_semaphore()
    for k in (1, n - 1):
        pl.semaphore_signal(barrier, inc=1, device_id=peer(k), device_id_type=MESH_IDS)
    pl.semaphore_wait(barrier, 2)
    right = send(ctx_ref, slots.at[1], 1, 1)
    left = send(ctx_ref, slots.at[3], 3, n - 1)
    tile = 256

    def add_term(block, source, first):
        base = pl.multiple_of(source * width, 8)

        @pl.loop(0, rows // tile)
        def _(i):
            r = pl.ds(pl.multiple_of(i * tile, tile), tile)

            @pl.loop(0, cols // tile)
            def _(j):
                c = pl.ds(pl.multiple_of(j * tile, tile), tile)
                term = jnp.dot(
                    block[r, :], weight_ref[pl.ds(base, width), c], preferred_element_type=jnp.float32
                )
                term = term.astype(jnp.bfloat16).astype(jnp.float32)
                if first:
                    out_ref[r, c] = term
                else:
                    out_ref[r, c] = out_ref[r, c] + term

    add_term(ctx_ref, me, True)
    right.wait_recv()
    onward = send(slots.at[1, pl.ds(0, half)], slots.at[2, pl.ds(0, half)], 2, 1)
    add_term(slots.at[1], lax.rem(me + n - 1, n), False)
    left.wait_recv()
    backward = send(slots.at[3, pl.ds(half, half)], slots.at[2, pl.ds(half, half)], 0, n - 1)
    add_term(slots.at[3], lax.rem(me + 1, n), False)
    onward.wait_recv()
    backward.wait_recv()
    add_term(slots.at[2], lax.rem(me + 2, n), False)

    @pl.loop(0, rows // tile)
    def _(i):
        r = pl.ds(pl.multiple_of(i * tile, tile), tile)
        middle = out_ref[r, :] + tokens_ref[r, :].astype(jnp.float32)
        out_ref[r, :] = middle
        norm_ref[r, :] = layer_norm(middle, gain_ref[...]).astype(norm_ref.dtype)

    for copy in (right, left, onward, backward):
        copy.wait_send()


def exchange_kernel(order, n, keys_ref, values_ref, marks_ref, keys_out, values_out, marks_out,
                    send_sem, recv_sem, local_sem):
    me = lax.axis_index("req")
    place = {"req": me, "tp": lax.axis_index("tp")}
    span = marks_ref.shape[1]

    def peer(d):
        where = dict(place, req=lax.rem(me + d + n, n))
        return tuple(where[a] for a in order)

    def windows(slot):
        part = pl.ds(slot * span, span)
        return (keys_out.at[:, :, part], values_out.at[:, part, :], marks_out.at[:, part])

    sources = (keys_ref, values_ref, marks_ref)
    barrier = pltpu.get_barrier_semaphore()
    for d in NEAR:
        pl.semaphore_signal(barrier, inc=1, device_id=peer(d), device_id_type=MESH_IDS)
    pl.semaphore_wait(barrier, len(NEAR))
    odd = lax.rem(me, 2)

    def send(kind, slices, targets, d):
        out = []
        for a, (src, dst) in enumerate(zip(slices, targets)):
            copy = pltpu.make_async_remote_copy(
                src_ref=src,
                dst_ref=dst,
                send_sem=send_sem.at[3 * kind + a],
                recv_sem=recv_sem.at[3 * kind + a],
                device_id=peer(d),
                device_id_type=MESH_IDS,
            )
            copy.start()
            out.append(copy)
        return out

    right = send(0, sources, windows(1), 1)
    left = send(1, sources, windows(3), -1)
    far = send(2, sources, windows(4 * odd), 2 - 4 * odd)
    local = []
    for a, (src, dst) in enumerate(zip(sources, windows(2))):
        copy = pltpu.make_async_copy(src, dst, local_sem.at[a])
        copy.start()
        local.append(copy)
    for a in range(3):
        right[a].wait_recv()
        left[a].wait_recv()
    relay = send(3, windows(1 + 2 * odd), windows(4 * odd), 1 - 2 * odd)
    for copy in local:
        copy.wait()
    for copy in right + left:
        copy.wait_send()
    for copy in far + relay:
        copy.wait()


def exchange(keys, values, marks, order):
    n = lax.axis_size("req")
    slots = 2 * max(NEAR) + 1
    heads, width, span = keys.shape
    any_spec = pl.BlockSpec(memory_space=pl.ANY)
    keys_all, values_all, marks_all = pl.pallas_call(
        functools.partial(exchange_kernel, order, n),
        out_shape=(
            jax.ShapeDtypeStruct((heads, width, slots * span), keys.dtype),
            jax.ShapeDtypeStruct((heads, slots * span, width), values.dtype),
            jax.ShapeDtypeStruct((1, slots * span), marks.dtype),
        ),
        in_specs=[any_spec] * 3,
        out_specs=(any_spec, any_spec, any_spec),
        scratch_shapes=[
            pltpu.SemaphoreType.DMA((12,)),
            pltpu.SemaphoreType.DMA((12,)),
            pltpu.SemaphoreType.DMA((3,)),
        ],
        compiler_params=pltpu.CompilerParams(collective_id=1, has_side_effects=True),
    )(keys, values, marks.reshape(1, span))
    source = lax.axis_index("req") + jnp.arange(slots * span, dtype=jnp.int32) // span - max(NEAR)
    present = (source >= 0) & (source < n)
    return keys_all, values_all, jnp.where(present, marks_all[0], 0)


def deliver_kernel(order, n, outgoing_ref, received_ref, send_sem, recv_sem, local_sem):
    me = lax.axis_index("req")
    place = {"req": me, "tp": lax.axis_index("tp")}

    def peer(k):
        where = dict(place, req=lax.rem(me + k, n))
        return tuple(where[a] for a in order)

    barrier = pltpu.get_barrier_semaphore()
    for k in range(1, n):
        pl.semaphore_signal(barrier, inc=1, device_id=peer(k), device_id_type=MESH_IDS)
    pl.semaphore_wait(barrier, n - 1)
    copies = []
    for k in range(1, n):
        copy = pltpu.make_async_remote_copy(
            src_ref=outgoing_ref.at[lax.rem(me + k, n)],
            dst_ref=received_ref.at[me],
            send_sem=send_sem.at[k],
            recv_sem=recv_sem.at[k],
            device_id=peer(k),
            device_id_type=MESH_IDS,
        )
        copy.start()
        copies.append(copy)
    own = pltpu.make_async_copy(outgoing_ref.at[me], received_ref.at[me], local_sem.at[0])
    own.start()
    own.wait()
    for copy in copies:
        copy.wait()


def deliver(outgoing, order):
    n = lax.axis_size("req")
    return pl.pallas_call(
        functools.partial(deliver_kernel, order, n),
        out_shape=jax.ShapeDtypeStruct(outgoing.shape, outgoing.dtype),
        in_specs=[pl.BlockSpec(memory_space=pltpu.VMEM)],
        out_specs=pl.BlockSpec(memory_space=pltpu.VMEM),
        scratch_shapes=[
            pltpu.SemaphoreType.DMA((n,)),
            pltpu.SemaphoreType.DMA((n,)),
            pltpu.SemaphoreType.DMA((1,)),
        ],
        compiler_params=pltpu.CompilerParams(collective_id=2, has_side_effects=True),
    )(outgoing)


def project(context, weight, tokens, gain, order):
    n = weight.shape[0] // context.shape[1]
    rows, cols = tokens.shape
    return pl.pallas_call(
        functools.partial(project_kernel, order),
        out_shape=(
            jax.ShapeDtypeStruct((rows, cols), jnp.float32),
            jax.ShapeDtypeStruct((rows, cols), jnp.bfloat16),
        ),
        in_specs=[pl.BlockSpec(memory_space=pltpu.VMEM)] * 4,
        out_specs=(pl.BlockSpec(memory_space=pltpu.VMEM), pl.BlockSpec(memory_space=pltpu.VMEM)),
        scratch_shapes=[
            pltpu.VMEM((n,) + context.shape, context.dtype),
            pltpu.SemaphoreType.DMA((n,)),
            pltpu.SemaphoreType.DMA((n,)),
        ],
        compiler_params=pltpu.CompilerParams(
            collective_id=0, has_side_effects=True, vmem_limit_bytes=48 * 1024 * 1024
        ),
        cost_estimate=pl.CostEstimate(
            flops=2 * rows * cols * weight.shape[0],
            bytes_accessed=4 * rows * cols + 2 * weight.size + 2 * rows * cols + 2 * n * context.size,
            transcendentals=0,
        ),
    )(context, weight, tokens, gain.reshape(1, cols))


def shifted_2(block, axis, distance):
    devices = range(lax.axis_size(axis))
    route = [(i - distance, i) for i in devices if i - distance in devices]
    return lax.ppermute(block, axis, route)


def layer_norm(stream, gain):
    center = jnp.mean(stream, axis=-1, keepdims=True)
    shifted = stream - center
    spread = jnp.mean(shifted * shifted, axis=-1, keepdims=True)
    return shifted * lax.rsqrt(spread + 1e-06) * gain.astype(jnp.float32)


def flash_kernel(bounds, q_ref, qm_ref, k_ref, v_ref, km_ref, o_ref):
    i = pl.program_id(0)
    tile = TILE
    factor = 1.0 / math.sqrt(HD)
    q = q_ref[...]
    qm = qm_ref[...]

    def step(j, carry):
        running_max, running_sum, weighted = carry
        start = pl.multiple_of(j * tile, tile)
        keys = k_ref[:, :, pl.ds(start, tile)]
        values = v_ref[:, pl.ds(start, tile), :]
        km = km_ref[:, pl.ds(start, tile)]
        scores = lax.dot_general(
            q, keys, (((2,), (1,)), ((0,), (0,))), preferred_element_type=jnp.float32
        ) * factor
        masked = jnp.where((qm == km)[None], scores, -1e30)
        new_max = jnp.maximum(running_max, jnp.max(masked, axis=2, keepdims=True))
        probs = jnp.exp(masked - new_max)
        shrink = jnp.exp(running_max - new_max)
        new_sum = running_sum * shrink + jnp.sum(probs, axis=2, keepdims=True)
        update = lax.dot_general(
            probs.astype(jnp.bfloat16), values, (((2,), (1,)), ((0,), (0,))),
            preferred_element_type=jnp.float32,
        )
        return new_max, new_sum, weighted * shrink + update

    heads, rows, width = q.shape
    init = (
        jnp.full((heads, rows, 1), -1e30, jnp.float32),
        jnp.zeros((heads, rows, 1), jnp.float32),
        jnp.zeros((heads, rows, width), jnp.float32),
    )
    _, total, weighted = lax.fori_loop(bounds[0, i], bounds[1, i], step, init)
    o_ref[...] = (weighted / total).astype(o_ref.dtype)


def attention(queries, query_marks, keys, values, key_marks):
    heads, rows, width = queries.shape
    key_rows = keys.shape[2]
    tiles = rows // QTILE
    low = query_marks.reshape(tiles, QTILE).min(axis=1)
    high = query_marks.reshape(tiles, QTILE).max(axis=1)
    valid = (key_marks[None, :] >= low[:, None]) & (key_marks[None, :] <= high[:, None])
    place = jnp.arange(key_rows, dtype=jnp.int32)[None, :]
    first = jnp.min(jnp.where(valid, place, key_rows), axis=1)
    last = jnp.max(jnp.where(valid, place, -1), axis=1)
    bounds = jnp.stack([first // TILE, last // TILE + 1]).astype(jnp.int32)
    return pl.pallas_call(
        flash_kernel,
        out_shape=jax.ShapeDtypeStruct(queries.shape, queries.dtype),
        grid_spec=pltpu.PrefetchScalarGridSpec(
            num_scalar_prefetch=1,
            grid=(tiles,),
            in_specs=[
                pl.BlockSpec((heads, QTILE, width), lambda i, b: (0, i, 0)),
                pl.BlockSpec((QTILE, 1), lambda i, b: (i, 0)),
                pl.BlockSpec((heads, width, key_rows), lambda i, b: (0, 0, 0)),
                pl.BlockSpec((heads, key_rows, width), lambda i, b: (0, 0, 0)),
                pl.BlockSpec((1, key_rows), lambda i, b: (0, 0)),
            ],
            out_specs=pl.BlockSpec((heads, QTILE, width), lambda i, b: (0, i, 0)),
        ),
        compiler_params=pltpu.CompilerParams(vmem_limit_bytes=48 * 1024 * 1024),
        cost_estimate=pl.CostEstimate(
            flops=4 * heads * rows * 2048 * width,
            bytes_accessed=2 * (queries.size * 2 + keys.size + values.size),
            transcendentals=heads * rows * 2048,
        ),
    )(bounds, queries, query_marks.reshape(rows, 1), keys, values, key_marks.reshape(1, key_rows))


def body(
    order,
    tokens,
    segments,
    attend_gain,
    attend_weight,
    output_weight,
    mixer_gain,
    expand_weight,
    reduce_weight,
    output_gain,
    merge_weight,
    merge_index,
    owners,
):
    token_rows = tokens.shape[0]
    head_width = attend_weight.shape[2]
    head_count = head_width // HD
    full_weight = lax.all_gather(output_weight, "tp", axis=0, tiled=True)
    stream = tokens.astype(jnp.float32)
    attend_in = layer_norm(stream, attend_gain).astype(jnp.bfloat16)
    projected = jnp.dot(
        attend_in,
        attend_weight.reshape(attend_weight.shape[0], 3 * head_width),
        preferred_element_type=jnp.float32,
    ).astype(jnp.bfloat16)
    marks = segments + 1

    def by_head(block):
        return jnp.transpose(block.reshape(block.shape[0], head_count, HD), (1, 0, 2))

    keys_all, values_all, key_marks = exchange(
        jnp.transpose(projected[:, head_width : 2 * head_width].reshape(-1, head_count, HD), (1, 2, 0)),
        by_head(projected[:, 2 * head_width :]),
        marks,
        order,
    )
    context = attention(by_head(projected[:, :head_width]), marks, keys_all, values_all, key_marks)
    context = jnp.transpose(context, (1, 0, 2)).reshape(token_rows, head_width)
    middle, mixer_in = project(context, full_weight, tokens, mixer_gain, order)
    expanded = jax.nn.gelu(
        jnp.dot(mixer_in, expand_weight, preferred_element_type=jnp.float32), approximate=False
    ).astype(jnp.bfloat16)
    hidden_terms = jnp.dot(expanded, reduce_weight, preferred_element_type=jnp.float32)
    final_stream = middle + lax.psum(hidden_terms.astype(jnp.bfloat16), "tp").astype(jnp.float32)
    final_normed = layer_norm(final_stream, output_gain).astype(jnp.bfloat16)
    merged_rows = merge_index.shape[0]
    local_index = merge_index - lax.axis_index("req") * token_rows
    picks = (local_index[:, :, None] == jnp.arange(token_rows, dtype=jnp.int32)).astype(jnp.bfloat16)
    merged = jnp.einsum(
        "mkt,tc->mkc", picks, final_normed, preferred_element_type=jnp.float32
    ).astype(jnp.bfloat16)
    feature = jnp.einsum(
        "mkc,kcd->md",
        merged,
        merge_weight.reshape(4, final_normed.shape[1], merge_weight.shape[1]),
        preferred_element_type=jnp.float32,
    ).astype(jnp.bfloat16)
    peers = lax.axis_size("req")
    capacity = 2 * merged_rows // peers
    target = owners[:, 0]
    choose = (target[:, None] == jnp.arange(peers, dtype=jnp.int32)[None, :]).astype(jnp.int32)
    slot = jnp.sum((jnp.cumsum(choose, axis=0) - 1) * choose, axis=1)
    position = target * capacity + slot
    placement = (
        position[:, None] == jnp.arange(peers * capacity, dtype=jnp.int32)[None, :]
    ).astype(jnp.bfloat16)
    outgoing = jnp.einsum(
        "ms,mc->sc", placement, feature, preferred_element_type=jnp.float32
    ).astype(jnp.bfloat16)
    outgoing = outgoing.reshape(peers, capacity, feature.shape[1])
    received = deliver(outgoing, order)
    return received.reshape(1, peers, capacity, feature.shape[1])


def solution(mesh):
    placed = (
        P("req", None),
        P("req"),
        P(),
        P(None, None, "tp"),
        P("tp", None),
        P(),
        P(None, "tp"),
        P("tp", None),
        P(),
        P(None, "tp"),
        P("req", None),
        P("req", None),
    )
    return jax.shard_map(
        functools.partial(body, tuple(mesh.axis_names)), mesh=mesh, in_specs=placed, out_specs=P("req", None, None, "tp"), check_vma=False
    )
```

```python
import functools
import math

import jax
import jax.numpy as jnp
from jax import lax
from jax.experimental import pallas as pl
from jax.experimental.pallas import tpu as pltpu
from jax.sharding import PartitionSpec as P

HD = 80
TILE = 256
NEAR = (1, -1, 2, -2)
MESH_IDS = pl.DeviceIdType.MESH


def project_kernel(order, ctx_ref, weight_ref, tokens_ref, gain_ref, out_ref, norm_ref, slots, send_sem,
                   recv_sem):
    n = slots.shape[0]
    rows, width = ctx_ref.shape
    cols = out_ref.shape[1]
    half = rows // 2
    me = lax.axis_index("tp")
    place = {"tp": me, "req": lax.axis_index("req")}

    def peer(k):
        where = dict(place, tp=lax.rem(me + k, n))
        return tuple(where[a] for a in order)

    def send(src, dst, sem, k):
        copy = pltpu.make_async_remote_copy(
            src_ref=src,
            dst_ref=dst,
            send_sem=send_sem.at[sem],
            recv_sem=recv_sem.at[sem],
            device_id=peer(k),
            device_id_type=MESH_IDS,
        )
        copy.start()
        return copy

    barrier = pltpu.get_barrier_semaphore()
    for k in (1, n - 1):
        pl.semaphore_signal(barrier, inc=1, device_id=peer(k), device_id_type=MESH_IDS)
    pl.semaphore_wait(barrier, 2)
    right = send(ctx_ref, slots.at[1], 1, 1)
    left = send(ctx_ref, slots.at[3], 3, n - 1)
    tile = 256

    def add_term(block, source, first):
        base = pl.multiple_of(source * width, 8)

        @pl.loop(0, rows // tile)
        def _(i):
            r = pl.ds(pl.multiple_of(i * tile, tile), tile)

            @pl.loop(0, cols // tile)
            def _(j):
                c = pl.ds(pl.multiple_of(j * tile, tile), tile)
                term = jnp.dot(
                    block[r, :], weight_ref[pl.ds(base, width), c], preferred_element_type=jnp.float32
                )
                term = term.astype(jnp.bfloat16).astype(jnp.float32)
                if first:
                    out_ref[r, c] = term
                else:
                    out_ref[r, c] = out_ref[r, c] + term

    add_term(ctx_ref, me, True)
    right.wait_recv()
    onward = send(slots.at[1, pl.ds(0, half)], slots.at[2, pl.ds(0, half)], 2, 1)
    add_term(slots.at[1], lax.rem(me + n - 1, n), False)
    left.wait_recv()
    backward = send(slots.at[3, pl.ds(half, half)], slots.at[2, pl.ds(half, half)], 0, n - 1)
    add_term(slots.at[3], lax.rem(me + 1, n), False)
    onward.wait_recv()
    backward.wait_recv()
    add_term(slots.at[2], lax.rem(me + 2, n), False)

    @pl.loop(0, rows // tile)
    def _(i):
        r = pl.ds(pl.multiple_of(i * tile, tile), tile)
        middle = out_ref[r, :] + tokens_ref[r, :].astype(jnp.float32)
        out_ref[r, :] = middle
        norm_ref[r, :] = layer_norm(middle, gain_ref[...]).astype(norm_ref.dtype)

    for copy in (right, left, onward, backward):
        copy.wait_send()


def exchange_kernel(order, n, keys_ref, values_ref, marks_ref, keys_out, values_out, marks_out,
                    send_sem, recv_sem, local_sem):
    me = lax.axis_index("req")
    place = {"req": me, "tp": lax.axis_index("tp")}
    span = marks_ref.shape[1]

    def peer(d):
        where = dict(place, req=lax.rem(me + d + n, n))
        return tuple(where[a] for a in order)

    def windows(slot):
        part = pl.ds(slot * span, span)
        return (keys_out.at[:, :, part], values_out.at[:, part, :], marks_out.at[:, part])

    sources = (keys_ref, values_ref, marks_ref)
    barrier = pltpu.get_barrier_semaphore()
    for d in NEAR:
        pl.semaphore_signal(barrier, inc=1, device_id=peer(d), device_id_type=MESH_IDS)
    pl.semaphore_wait(barrier, len(NEAR))
    odd = lax.rem(me, 2)

    def send(kind, slices, targets, d):
        out = []
        for a, (src, dst) in enumerate(zip(slices, targets)):
            copy = pltpu.make_async_remote_copy(
                src_ref=src,
                dst_ref=dst,
                send_sem=send_sem.at[3 * kind + a],
                recv_sem=recv_sem.at[3 * kind + a],
                device_id=peer(d),
                device_id_type=MESH_IDS,
            )
            copy.start()
            out.append(copy)
        return out

    right = send(0, sources, windows(1), 1)
    left = send(1, sources, windows(3), -1)
    far = send(2, sources, windows(4 * odd), 2 - 4 * odd)
    local = []
    for a, (src, dst) in enumerate(zip(sources, windows(2))):
        copy = pltpu.make_async_copy(src, dst, local_sem.at[a])
        copy.start()
        local.append(copy)
    for a in range(3):
        right[a].wait_recv()
        left[a].wait_recv()
    relay = send(3, windows(1 + 2 * odd), windows(4 * odd), 1 - 2 * odd)
    for copy in local:
        copy.wait()
    for copy in right + left:
        copy.wait_send()
    for copy in far + relay:
        copy.wait()


def exchange(keys, values, marks, order):
    n = lax.axis_size("req")
    slots = 2 * max(NEAR) + 1
    heads, width, span = keys.shape
    any_spec = pl.BlockSpec(memory_space=pl.ANY)
    keys_all, values_all, marks_all = pl.pallas_call(
        functools.partial(exchange_kernel, order, n),
        out_shape=(
            jax.ShapeDtypeStruct((heads, width, slots * span), keys.dtype),
            jax.ShapeDtypeStruct((heads, slots * span, width), values.dtype),
            jax.ShapeDtypeStruct((1, slots * span), marks.dtype),
        ),
        in_specs=[any_spec] * 3,
        out_specs=(any_spec, any_spec, any_spec),
        scratch_shapes=[
            pltpu.SemaphoreType.DMA((12,)),
            pltpu.SemaphoreType.DMA((12,)),
            pltpu.SemaphoreType.DMA((3,)),
        ],
        compiler_params=pltpu.CompilerParams(collective_id=1, has_side_effects=True),
    )(keys, values, marks.reshape(1, span))
    source = lax.axis_index("req") + jnp.arange(slots * span, dtype=jnp.int32) // span - max(NEAR)
    present = (source >= 0) & (source < n)
    return keys_all, values_all, jnp.where(present, marks_all[0], 0)


def deliver_kernel(order, n, outgoing_ref, received_ref, send_sem, recv_sem, local_sem):
    me = lax.axis_index("req")
    place = {"req": me, "tp": lax.axis_index("tp")}

    def peer(k):
        where = dict(place, req=lax.rem(me + k, n))
        return tuple(where[a] for a in order)

    barrier = pltpu.get_barrier_semaphore()
    for k in range(1, n):
        pl.semaphore_signal(barrier, inc=1, device_id=peer(k), device_id_type=MESH_IDS)
    pl.semaphore_wait(barrier, n - 1)
    copies = []
    for k in range(1, n):
        copy = pltpu.make_async_remote_copy(
            src_ref=outgoing_ref.at[lax.rem(me + k, n)],
            dst_ref=received_ref.at[me],
            send_sem=send_sem.at[k],
            recv_sem=recv_sem.at[k],
            device_id=peer(k),
            device_id_type=MESH_IDS,
        )
        copy.start()
        copies.append(copy)
    own = pltpu.make_async_copy(outgoing_ref.at[me], received_ref.at[me], local_sem.at[0])
    own.start()
    own.wait()
    for copy in copies:
        copy.wait()


def deliver(outgoing, order):
    n = lax.axis_size("req")
    return pl.pallas_call(
        functools.partial(deliver_kernel, order, n),
        out_shape=jax.ShapeDtypeStruct(outgoing.shape, outgoing.dtype),
        in_specs=[pl.BlockSpec(memory_space=pltpu.VMEM)],
        out_specs=pl.BlockSpec(memory_space=pltpu.VMEM),
        scratch_shapes=[
            pltpu.SemaphoreType.DMA((n,)),
            pltpu.SemaphoreType.DMA((n,)),
            pltpu.SemaphoreType.DMA((1,)),
        ],
        compiler_params=pltpu.CompilerParams(collective_id=2, has_side_effects=True),
    )(outgoing)


def project(context, weight, tokens, gain, order):
    n = weight.shape[0] // context.shape[1]
    rows, cols = tokens.shape
    return pl.pallas_call(
        functools.partial(project_kernel, order),
        out_shape=(
            jax.ShapeDtypeStruct((rows, cols), jnp.float32),
            jax.ShapeDtypeStruct((rows, cols), jnp.bfloat16),
        ),
        in_specs=[pl.BlockSpec(memory_space=pltpu.VMEM)] * 4,
        out_specs=(pl.BlockSpec(memory_space=pltpu.VMEM), pl.BlockSpec(memory_space=pltpu.VMEM)),
        scratch_shapes=[
            pltpu.VMEM((n,) + context.shape, context.dtype),
            pltpu.SemaphoreType.DMA((n,)),
            pltpu.SemaphoreType.DMA((n,)),
        ],
        compiler_params=pltpu.CompilerParams(
            collective_id=0, has_side_effects=True, vmem_limit_bytes=48 * 1024 * 1024
        ),
        cost_estimate=pl.CostEstimate(
            flops=2 * rows * cols * weight.shape[0],
            bytes_accessed=4 * rows * cols + 2 * weight.size + 2 * rows * cols + 2 * n * context.size,
            transcendentals=0,
        ),
    )(context, weight, tokens, gain.reshape(1, cols))


def shifted_2(block, axis, distance):
    devices = range(lax.axis_size(axis))
    route = [(i - distance, i) for i in devices if i - distance in devices]
    return lax.ppermute(block, axis, route)


def layer_norm(stream, gain):
    center = jnp.mean(stream, axis=-1, keepdims=True)
    shifted = stream - center
    spread = jnp.mean(shifted * shifted, axis=-1, keepdims=True)
    return shifted * lax.rsqrt(spread + 1e-06) * gain.astype(jnp.float32)


def flash_kernel(bounds, q_ref, qm_ref, k_ref, v_ref, km_ref, o_ref):
    i = pl.program_id(0)
    tile = TILE
    factor = 1.0 / math.sqrt(HD)
    q = q_ref[...]
    qm = qm_ref[...]

    def step(j, carry):
        running_max, running_sum, weighted = carry
        start = pl.multiple_of(j * tile, tile)
        keys = k_ref[:, :, pl.ds(start, tile)]
        values = v_ref[:, pl.ds(start, tile), :]
        km = km_ref[:, pl.ds(start, tile)]
        scores = lax.dot_general(
            q, keys, (((2,), (1,)), ((0,), (0,))), preferred_element_type=jnp.float32
        ) * factor
        masked = jnp.where((qm == km)[None], scores, -1e30)
        new_max = jnp.maximum(running_max, jnp.max(masked, axis=2, keepdims=True))
        probs = jnp.exp(masked - new_max)
        shrink = jnp.exp(running_max - new_max)
        new_sum = running_sum * shrink + jnp.sum(probs, axis=2, keepdims=True)
        update = lax.dot_general(
            probs.astype(jnp.bfloat16), values, (((2,), (1,)), ((0,), (0,))),
            preferred_element_type=jnp.float32,
        )
        return new_max, new_sum, weighted * shrink + update

    heads, rows, width = q.shape
    init = (
        jnp.full((heads, rows, 1), -1e30, jnp.float32),
        jnp.zeros((heads, rows, 1), jnp.float32),
        jnp.zeros((heads, rows, width), jnp.float32),
    )
    _, total, weighted = lax.fori_loop(bounds[0, i], bounds[1, i], step, init)
    result = (weighted / total).astype(o_ref.dtype)
    for h in range(heads):
        o_ref[:, h * width : (h + 1) * width] = result[h]


def attention(queries, query_marks, keys, values, key_marks):
    heads, rows, width = queries.shape
    key_rows = keys.shape[2]
    tiles = rows // TILE
    low = query_marks.reshape(tiles, TILE).min(axis=1)
    high = query_marks.reshape(tiles, TILE).max(axis=1)
    valid = (key_marks[None, :] >= low[:, None]) & (key_marks[None, :] <= high[:, None])
    place = jnp.arange(key_rows, dtype=jnp.int32)[None, :]
    first = jnp.min(jnp.where(valid, place, key_rows), axis=1)
    last = jnp.max(jnp.where(valid, place, -1), axis=1)
    bounds = jnp.stack([first // TILE, last // TILE + 1]).astype(jnp.int32)
    return pl.pallas_call(
        flash_kernel,
        out_shape=jax.ShapeDtypeStruct((rows, heads * width), queries.dtype),
        grid_spec=pltpu.PrefetchScalarGridSpec(
            num_scalar_prefetch=1,
            grid=(tiles,),
            in_specs=[
                pl.BlockSpec((heads, TILE, width), lambda i, b: (0, i, 0)),
                pl.BlockSpec((TILE, 1), lambda i, b: (i, 0)),
                pl.BlockSpec((heads, width, key_rows), lambda i, b: (0, 0, 0)),
                pl.BlockSpec((heads, key_rows, width), lambda i, b: (0, 0, 0)),
                pl.BlockSpec((1, key_rows), lambda i, b: (0, 0)),
            ],
            out_specs=pl.BlockSpec((TILE, heads * width), lambda i, b: (i, 0)),
        ),
        compiler_params=pltpu.CompilerParams(vmem_limit_bytes=48 * 1024 * 1024),
        cost_estimate=pl.CostEstimate(
            flops=4 * heads * rows * 2048 * width,
            bytes_accessed=2 * (queries.size * 2 + keys.size + values.size),
            transcendentals=heads * rows * 2048,
        ),
    )(bounds, queries, query_marks.reshape(rows, 1), keys, values, key_marks.reshape(1, key_rows))


def body(
    order,
    tokens,
    segments,
    attend_gain,
    attend_weight,
    output_weight,
    mixer_gain,
    expand_weight,
    reduce_weight,
    output_gain,
    merge_weight,
    merge_index,
    owners,
):
    token_rows = tokens.shape[0]
    head_width = attend_weight.shape[2]
    head_count = head_width // HD
    full_weight = lax.all_gather(output_weight, "tp", axis=0, tiled=True)
    stream = tokens.astype(jnp.float32)
    attend_in = layer_norm(stream, attend_gain).astype(jnp.bfloat16)
    projected = jnp.dot(
        attend_in,
        attend_weight.reshape(attend_weight.shape[0], 3 * head_width),
        preferred_element_type=jnp.float32,
    ).astype(jnp.bfloat16)
    marks = segments + 1

    def by_head(block):
        return jnp.transpose(block.reshape(block.shape[0], head_count, HD), (1, 0, 2))

    keys_all, values_all, key_marks = exchange(
        jnp.transpose(projected[:, head_width : 2 * head_width].reshape(-1, head_count, HD), (1, 2, 0)),
        by_head(projected[:, 2 * head_width :]),
        marks,
        order,
    )
    context = attention(by_head(projected[:, :head_width]), marks, keys_all, values_all, key_marks)
    middle, mixer_in = project(context, full_weight, tokens, mixer_gain, order)
    expanded = jax.nn.gelu(
        jnp.dot(mixer_in, expand_weight, preferred_element_type=jnp.float32), approximate=False
    ).astype(jnp.bfloat16)
    hidden_terms = jnp.dot(expanded, reduce_weight, preferred_element_type=jnp.float32)
    final_stream = middle + lax.psum(hidden_terms.astype(jnp.bfloat16), "tp").astype(jnp.float32)
    final_normed = layer_norm(final_stream, output_gain).astype(jnp.bfloat16)
    merged_rows = merge_index.shape[0]
    local_index = merge_index - lax.axis_index("req") * token_rows
    picks = (local_index[:, :, None] == jnp.arange(token_rows, dtype=jnp.int32)).astype(jnp.bfloat16)
    merged = jnp.einsum(
        "mkt,tc->mkc", picks, final_normed, preferred_element_type=jnp.float32
    ).astype(jnp.bfloat16)
    feature = jnp.einsum(
        "mkc,kcd->md",
        merged,
        merge_weight.reshape(4, final_normed.shape[1], merge_weight.shape[1]),
        preferred_element_type=jnp.float32,
    ).astype(jnp.bfloat16)
    peers = lax.axis_size("req")
    capacity = 2 * merged_rows // peers
    target = owners[:, 0]
    choose = (target[:, None] == jnp.arange(peers, dtype=jnp.int32)[None, :]).astype(jnp.int32)
    slot = jnp.sum((jnp.cumsum(choose, axis=0) - 1) * choose, axis=1)
    position = target * capacity + slot
    placement = (
        position[:, None] == jnp.arange(peers * capacity, dtype=jnp.int32)[None, :]
    ).astype(jnp.bfloat16)
    outgoing = jnp.einsum(
        "ms,mc->sc", placement, feature, preferred_element_type=jnp.float32
    ).astype(jnp.bfloat16)
    outgoing = outgoing.reshape(peers, capacity, feature.shape[1])
    received = deliver(outgoing, order)
    return received.reshape(1, peers, capacity, feature.shape[1])


def solution(mesh):
    placed = (
        P("req", None),
        P("req"),
        P(),
        P(None, None, "tp"),
        P("tp", None),
        P(),
        P(None, "tp"),
        P("tp", None),
        P(),
        P(None, "tp"),
        P("req", None),
        P("req", None),
    )
    return jax.shard_map(
        functools.partial(body, tuple(mesh.axis_names)), mesh=mesh, in_specs=placed, out_specs=P("req", None, None, "tp"), check_vma=False
    )
```

```python
import functools
import math

import jax
import jax.numpy as jnp
from jax import lax
from jax.experimental import pallas as pl
from jax.experimental.pallas import tpu as pltpu
from jax.sharding import PartitionSpec as P

HD = 80
TILE = 256
NEAR = (1, -1, 2, -2)
MESH_IDS = pl.DeviceIdType.MESH


def project_kernel(order, ctx_ref, weight_ref, tokens_ref, gain_ref, out_ref, norm_ref, slots, send_sem,
                   recv_sem):
    n = slots.shape[0]
    rows, width = ctx_ref.shape
    cols = out_ref.shape[1]
    half = rows // 2
    me = lax.axis_index("tp")
    place = {"tp": me, "req": lax.axis_index("req")}

    def peer(k):
        where = dict(place, tp=lax.rem(me + k, n))
        return tuple(where[a] for a in order)

    def send(src, dst, sem, k):
        copy = pltpu.make_async_remote_copy(
            src_ref=src,
            dst_ref=dst,
            send_sem=send_sem.at[sem],
            recv_sem=recv_sem.at[sem],
            device_id=peer(k),
            device_id_type=MESH_IDS,
        )
        copy.start()
        return copy

    barrier = pltpu.get_barrier_semaphore()
    for k in (1, n - 1):
        pl.semaphore_signal(barrier, inc=1, device_id=peer(k), device_id_type=MESH_IDS)
    pl.semaphore_wait(barrier, 2)
    right = send(ctx_ref, slots.at[1], 1, 1)
    left = send(ctx_ref, slots.at[3], 3, n - 1)
    tile = 256

    def add_term(block, source, first):
        base = pl.multiple_of(source * width, 8)

        @pl.loop(0, rows // tile)
        def _(i):
            r = pl.ds(pl.multiple_of(i * tile, tile), tile)

            @pl.loop(0, cols // tile)
            def _(j):
                c = pl.ds(pl.multiple_of(j * tile, tile), tile)
                term = jnp.dot(
                    block[r, :], weight_ref[pl.ds(base, width), c], preferred_element_type=jnp.float32
                )
                term = term.astype(jnp.bfloat16).astype(jnp.float32)
                if first:
                    out_ref[r, c] = term
                else:
                    out_ref[r, c] = out_ref[r, c] + term

    add_term(ctx_ref, me, True)
    right.wait_recv()
    onward = send(slots.at[1, pl.ds(0, half)], slots.at[2, pl.ds(0, half)], 2, 1)
    add_term(slots.at[1], lax.rem(me + n - 1, n), False)
    left.wait_recv()
    backward = send(slots.at[3, pl.ds(half, half)], slots.at[2, pl.ds(half, half)], 0, n - 1)
    add_term(slots.at[3], lax.rem(me + 1, n), False)
    onward.wait_recv()
    backward.wait_recv()
    add_term(slots.at[2], lax.rem(me + 2, n), False)

    @pl.loop(0, rows // tile)
    def _(i):
        r = pl.ds(pl.multiple_of(i * tile, tile), tile)
        middle = out_ref[r, :] + tokens_ref[r, :].astype(jnp.float32)
        out_ref[r, :] = middle
        norm_ref[r, :] = layer_norm(middle, gain_ref[...]).astype(norm_ref.dtype)

    for copy in (right, left, onward, backward):
        copy.wait_send()


def exchange_kernel(order, n, keys_ref, values_ref, marks_ref, keys_out, values_out, marks_out,
                    send_sem, recv_sem, local_sem):
    me = lax.axis_index("req")
    place = {"req": me, "tp": lax.axis_index("tp")}
    span = marks_ref.shape[1]

    def peer(d):
        where = dict(place, req=lax.rem(me + d + n, n))
        return tuple(where[a] for a in order)

    def windows(slot):
        part = pl.ds(slot * span, span)
        return (keys_out.at[:, :, part], values_out.at[:, part, :], marks_out.at[:, part])

    sources = (keys_ref, values_ref, marks_ref)
    barrier = pltpu.get_barrier_semaphore()
    for d in NEAR:
        pl.semaphore_signal(barrier, inc=1, device_id=peer(d), device_id_type=MESH_IDS)
    pl.semaphore_wait(barrier, len(NEAR))
    odd = lax.rem(me, 2)

    def send(kind, slices, targets, d):
        out = []
        for a, (src, dst) in enumerate(zip(slices, targets)):
            copy = pltpu.make_async_remote_copy(
                src_ref=src,
                dst_ref=dst,
                send_sem=send_sem.at[3 * kind + a],
                recv_sem=recv_sem.at[3 * kind + a],
                device_id=peer(d),
                device_id_type=MESH_IDS,
            )
            copy.start()
            out.append(copy)
        return out

    right = send(0, sources, windows(1), 1)
    left = send(1, sources, windows(3), -1)
    far = send(2, sources, windows(4 * odd), 2 - 4 * odd)
    local = []
    for a, (src, dst) in enumerate(zip(sources, windows(2))):
        copy = pltpu.make_async_copy(src, dst, local_sem.at[a])
        copy.start()
        local.append(copy)
    for a in range(3):
        right[a].wait_recv()
        left[a].wait_recv()
    relay = send(3, windows(1 + 2 * odd), windows(4 * odd), 1 - 2 * odd)
    for copy in local:
        copy.wait()
    for copy in right + left:
        copy.wait_send()
    for copy in far + relay:
        copy.wait()


def exchange(keys, values, marks, order):
    n = lax.axis_size("req")
    slots = 2 * max(NEAR) + 1
    heads, width, span = keys.shape
    any_spec = pl.BlockSpec(memory_space=pl.ANY)
    keys_all, values_all, marks_all = pl.pallas_call(
        functools.partial(exchange_kernel, order, n),
        out_shape=(
            jax.ShapeDtypeStruct((heads, width, slots * span), keys.dtype),
            jax.ShapeDtypeStruct((heads, slots * span, width), values.dtype),
            jax.ShapeDtypeStruct((1, slots * span), marks.dtype),
        ),
        in_specs=[any_spec] * 3,
        out_specs=(any_spec, any_spec, any_spec),
        scratch_shapes=[
            pltpu.SemaphoreType.DMA((12,)),
            pltpu.SemaphoreType.DMA((12,)),
            pltpu.SemaphoreType.DMA((3,)),
        ],
        compiler_params=pltpu.CompilerParams(collective_id=1, has_side_effects=True),
    )(keys, values, marks.reshape(1, span))
    source = lax.axis_index("req") + jnp.arange(slots * span, dtype=jnp.int32) // span - max(NEAR)
    present = (source >= 0) & (source < n)
    return keys_all, values_all, jnp.where(present, marks_all[0], 0)


def deliver_kernel(order, n, outgoing_ref, received_ref, send_sem, recv_sem, local_sem):
    me = lax.axis_index("req")
    place = {"req": me, "tp": lax.axis_index("tp")}

    def peer(k):
        where = dict(place, req=lax.rem(me + k, n))
        return tuple(where[a] for a in order)

    barrier = pltpu.get_barrier_semaphore()
    for k in range(1, n):
        pl.semaphore_signal(barrier, inc=1, device_id=peer(k), device_id_type=MESH_IDS)
    pl.semaphore_wait(barrier, n - 1)
    copies = []
    for k in range(1, n):
        copy = pltpu.make_async_remote_copy(
            src_ref=outgoing_ref.at[lax.rem(me + k, n)],
            dst_ref=received_ref.at[me],
            send_sem=send_sem.at[k],
            recv_sem=recv_sem.at[k],
            device_id=peer(k),
            device_id_type=MESH_IDS,
        )
        copy.start()
        copies.append(copy)
    own = pltpu.make_async_copy(outgoing_ref.at[me], received_ref.at[me], local_sem.at[0])
    own.start()
    own.wait()
    for copy in copies:
        copy.wait()


def deliver(outgoing, order):
    n = lax.axis_size("req")
    return pl.pallas_call(
        functools.partial(deliver_kernel, order, n),
        out_shape=jax.ShapeDtypeStruct(outgoing.shape, outgoing.dtype),
        in_specs=[pl.BlockSpec(memory_space=pltpu.VMEM)],
        out_specs=pl.BlockSpec(memory_space=pltpu.VMEM),
        scratch_shapes=[
            pltpu.SemaphoreType.DMA((n,)),
            pltpu.SemaphoreType.DMA((n,)),
            pltpu.SemaphoreType.DMA((1,)),
        ],
        compiler_params=pltpu.CompilerParams(collective_id=2, has_side_effects=True),
    )(outgoing)


def project(context, weight, tokens, gain, order):
    n = weight.shape[0] // context.shape[1]
    rows, cols = tokens.shape
    return pl.pallas_call(
        functools.partial(project_kernel, order),
        out_shape=(
            jax.ShapeDtypeStruct((rows, cols), jnp.float32),
            jax.ShapeDtypeStruct((rows, cols), jnp.bfloat16),
        ),
        in_specs=[pl.BlockSpec(memory_space=pltpu.VMEM)] * 4,
        out_specs=(pl.BlockSpec(memory_space=pltpu.VMEM), pl.BlockSpec(memory_space=pltpu.VMEM)),
        scratch_shapes=[
            pltpu.VMEM((n,) + context.shape, context.dtype),
            pltpu.SemaphoreType.DMA((n,)),
            pltpu.SemaphoreType.DMA((n,)),
        ],
        compiler_params=pltpu.CompilerParams(
            collective_id=0, has_side_effects=True, vmem_limit_bytes=48 * 1024 * 1024
        ),
        cost_estimate=pl.CostEstimate(
            flops=2 * rows * cols * weight.shape[0],
            bytes_accessed=4 * rows * cols + 2 * weight.size + 2 * rows * cols + 2 * n * context.size,
            transcendentals=0,
        ),
    )(context, weight, tokens, gain.reshape(1, cols))


def shifted_2(block, axis, distance):
    devices = range(lax.axis_size(axis))
    route = [(i - distance, i) for i in devices if i - distance in devices]
    return lax.ppermute(block, axis, route)


def layer_norm(stream, gain):
    center = jnp.mean(stream, axis=-1, keepdims=True)
    shifted = stream - center
    spread = jnp.mean(shifted * shifted, axis=-1, keepdims=True)
    return shifted * lax.rsqrt(spread + 1e-06) * gain.astype(jnp.float32)


def flash_kernel(bounds, q_ref, qm_ref, k_ref, v_ref, km_ref, o_ref):
    i = pl.program_id(0)
    tile = TILE
    factor = 1.0 / math.sqrt(HD)
    heads = k_ref.shape[0]
    q = jnp.stack([q_ref[:, h * HD : (h + 1) * HD] for h in range(heads)])
    qm = qm_ref[...]

    def step(j, carry):
        running_max, running_sum, weighted = carry
        start = pl.multiple_of(j * tile, tile)
        keys = k_ref[:, :, pl.ds(start, tile)]
        values = v_ref[:, pl.ds(start, tile), :]
        km = km_ref[:, pl.ds(start, tile)]
        scores = lax.dot_general(
            q, keys, (((2,), (1,)), ((0,), (0,))), preferred_element_type=jnp.float32
        ) * factor
        masked = jnp.where((qm == km)[None], scores, -1e30)
        new_max = jnp.maximum(running_max, jnp.max(masked, axis=2, keepdims=True))
        probs = jnp.exp(masked - new_max)
        shrink = jnp.exp(running_max - new_max)
        new_sum = running_sum * shrink + jnp.sum(probs, axis=2, keepdims=True)
        update = lax.dot_general(
            probs.astype(jnp.bfloat16), values, (((2,), (1,)), ((0,), (0,))),
            preferred_element_type=jnp.float32,
        )
        return new_max, new_sum, weighted * shrink + update

    heads, rows, width = q.shape
    init = (
        jnp.full((heads, rows, 1), -1e30, jnp.float32),
        jnp.zeros((heads, rows, 1), jnp.float32),
        jnp.zeros((heads, rows, width), jnp.float32),
    )
    _, total, weighted = lax.fori_loop(bounds[0, i], bounds[1, i], step, init)
    result = (weighted / total).astype(o_ref.dtype)
    for h in range(heads):
        o_ref[:, h * width : (h + 1) * width] = result[h]


def attention(queries, query_marks, keys, values, key_marks):
    heads = keys.shape[0]
    rows, width = queries.shape[0], queries.shape[1] // heads
    key_rows = keys.shape[2]
    tiles = rows // TILE
    low = query_marks.reshape(tiles, TILE).min(axis=1)
    high = query_marks.reshape(tiles, TILE).max(axis=1)
    valid = (key_marks[None, :] >= low[:, None]) & (key_marks[None, :] <= high[:, None])
    place = jnp.arange(key_rows, dtype=jnp.int32)[None, :]
    first = jnp.min(jnp.where(valid, place, key_rows), axis=1)
    last = jnp.max(jnp.where(valid, place, -1), axis=1)
    bounds = jnp.stack([first // TILE, last // TILE + 1]).astype(jnp.int32)
    return pl.pallas_call(
        flash_kernel,
        out_shape=jax.ShapeDtypeStruct((rows, heads * width), queries.dtype),
        grid_spec=pltpu.PrefetchScalarGridSpec(
            num_scalar_prefetch=1,
            grid=(tiles,),
            in_specs=[
                pl.BlockSpec((TILE, heads * width), lambda i, b: (i, 0)),
                pl.BlockSpec((TILE, 1), lambda i, b: (i, 0)),
                pl.BlockSpec((heads, width, key_rows), lambda i, b: (0, 0, 0)),
                pl.BlockSpec((heads, key_rows, width), lambda i, b: (0, 0, 0)),
                pl.BlockSpec((1, key_rows), lambda i, b: (0, 0)),
            ],
            out_specs=pl.BlockSpec((TILE, heads * width), lambda i, b: (i, 0)),
        ),
        compiler_params=pltpu.CompilerParams(vmem_limit_bytes=48 * 1024 * 1024),
        cost_estimate=pl.CostEstimate(
            flops=4 * heads * rows * 2048 * width,
            bytes_accessed=2 * (queries.size * 2 + keys.size + values.size),
            transcendentals=heads * rows * 2048,
        ),
    )(bounds, queries, query_marks.reshape(rows, 1), keys, values, key_marks.reshape(1, key_rows))


def body(
    order,
    tokens,
    segments,
    attend_gain,
    attend_weight,
    output_weight,
    mixer_gain,
    expand_weight,
    reduce_weight,
    output_gain,
    merge_weight,
    merge_index,
    owners,
):
    token_rows = tokens.shape[0]
    head_width = attend_weight.shape[2]
    head_count = head_width // HD
    full_weight = lax.all_gather(output_weight, "tp", axis=0, tiled=True)
    stream = tokens.astype(jnp.float32)
    attend_in = layer_norm(stream, attend_gain).astype(jnp.bfloat16)
    projected = jnp.dot(
        attend_in,
        attend_weight.reshape(attend_weight.shape[0], 3 * head_width),
        preferred_element_type=jnp.float32,
    ).astype(jnp.bfloat16)
    marks = segments + 1

    def by_head(block):
        return jnp.transpose(block.reshape(block.shape[0], head_count, HD), (1, 0, 2))

    keys_all, values_all, key_marks = exchange(
        jnp.transpose(projected[:, head_width : 2 * head_width].reshape(-1, head_count, HD), (1, 2, 0)),
        by_head(projected[:, 2 * head_width :]),
        marks,
        order,
    )
    context = attention(projected[:, :head_width], marks, keys_all, values_all, key_marks)
    middle, mixer_in = project(context, full_weight, tokens, mixer_gain, order)
    expanded = jax.nn.gelu(
        jnp.dot(mixer_in, expand_weight, preferred_element_type=jnp.float32), approximate=False
    ).astype(jnp.bfloat16)
    hidden_terms = jnp.dot(expanded, reduce_weight, preferred_element_type=jnp.float32)
    final_stream = middle + lax.psum(hidden_terms.astype(jnp.bfloat16), "tp").astype(jnp.float32)
    final_normed = layer_norm(final_stream, output_gain).astype(jnp.bfloat16)
    merged_rows = merge_index.shape[0]
    local_index = merge_index - lax.axis_index("req") * token_rows
    picks = (local_index[:, :, None] == jnp.arange(token_rows, dtype=jnp.int32)).astype(jnp.bfloat16)
    merged = jnp.einsum(
        "mkt,tc->mkc", picks, final_normed, preferred_element_type=jnp.float32
    ).astype(jnp.bfloat16)
    feature = jnp.einsum(
        "mkc,kcd->md",
        merged,
        merge_weight.reshape(4, final_normed.shape[1], merge_weight.shape[1]),
        preferred_element_type=jnp.float32,
    ).astype(jnp.bfloat16)
    peers = lax.axis_size("req")
    capacity = 2 * merged_rows // peers
    target = owners[:, 0]
    choose = (target[:, None] == jnp.arange(peers, dtype=jnp.int32)[None, :]).astype(jnp.int32)
    slot = jnp.sum((jnp.cumsum(choose, axis=0) - 1) * choose, axis=1)
    position = target * capacity + slot
    placement = (
        position[:, None] == jnp.arange(peers * capacity, dtype=jnp.int32)[None, :]
    ).astype(jnp.bfloat16)
    outgoing = jnp.einsum(
        "ms,mc->sc", placement, feature, preferred_element_type=jnp.float32
    ).astype(jnp.bfloat16)
    outgoing = outgoing.reshape(peers, capacity, feature.shape[1])
    received = deliver(outgoing, order)
    return received.reshape(1, peers, capacity, feature.shape[1])


def solution(mesh):
    placed = (
        P("req", None),
        P("req"),
        P(),
        P(None, None, "tp"),
        P("tp", None),
        P(),
        P(None, "tp"),
        P("tp", None),
        P(),
        P(None, "tp"),
        P("req", None),
        P("req", None),
    )
    return jax.shard_map(
        functools.partial(body, tuple(mesh.axis_names)), mesh=mesh, in_specs=placed, out_specs=P("req", None, None, "tp"), check_vma=False
    )
```

```python
import functools
import math

import jax
import jax.numpy as jnp
from jax import lax
from jax.experimental import pallas as pl
from jax.experimental.pallas import tpu as pltpu
from jax.sharding import PartitionSpec as P

HD = 80
TILE = 256
NEAR = (1, -1, 2, -2)
MESH_IDS = pl.DeviceIdType.MESH


def project_kernel(order, ctx_ref, weight_ref, tokens_ref, gain_ref, out_ref, norm_ref, slots, send_sem,
                   recv_sem):
    n = slots.shape[0]
    rows, width = ctx_ref.shape
    cols = out_ref.shape[1]
    half = rows // 2
    me = lax.axis_index("tp")
    place = {"tp": me, "req": lax.axis_index("req")}

    def peer(k):
        where = dict(place, tp=lax.rem(me + k, n))
        return tuple(where[a] for a in order)

    def send(src, dst, sem, k):
        copy = pltpu.make_async_remote_copy(
            src_ref=src,
            dst_ref=dst,
            send_sem=send_sem.at[sem],
            recv_sem=recv_sem.at[sem],
            device_id=peer(k),
            device_id_type=MESH_IDS,
        )
        copy.start()
        return copy

    barrier = pltpu.get_barrier_semaphore()
    for k in (1, n - 1):
        pl.semaphore_signal(barrier, inc=1, device_id=peer(k), device_id_type=MESH_IDS)
    pl.semaphore_wait(barrier, 2)
    right = send(ctx_ref, slots.at[1], 1, 1)
    left = send(ctx_ref, slots.at[3], 3, n - 1)
    tile = 256

    def add_term(block, source, first):
        base = pl.multiple_of(source * width, 8)

        @pl.loop(0, rows // tile)
        def _(i):
            r = pl.ds(pl.multiple_of(i * tile, tile), tile)

            @pl.loop(0, cols // tile)
            def _(j):
                c = pl.ds(pl.multiple_of(j * tile, tile), tile)
                term = jnp.dot(
                    block[r, :], weight_ref[pl.ds(base, width), c], preferred_element_type=jnp.float32
                )
                term = term.astype(jnp.bfloat16).astype(jnp.float32)
                if first:
                    out_ref[r, c] = term
                else:
                    out_ref[r, c] = out_ref[r, c] + term

    add_term(ctx_ref, me, True)
    right.wait_recv()
    onward = send(slots.at[1, pl.ds(0, half)], slots.at[2, pl.ds(0, half)], 2, 1)
    add_term(slots.at[1], lax.rem(me + n - 1, n), False)
    left.wait_recv()
    backward = send(slots.at[3, pl.ds(half, half)], slots.at[2, pl.ds(half, half)], 0, n - 1)
    add_term(slots.at[3], lax.rem(me + 1, n), False)
    onward.wait_recv()
    backward.wait_recv()
    add_term(slots.at[2], lax.rem(me + 2, n), False)

    @pl.loop(0, rows // tile)
    def _(i):
        r = pl.ds(pl.multiple_of(i * tile, tile), tile)
        middle = out_ref[r, :] + tokens_ref[r, :].astype(jnp.float32)
        out_ref[r, :] = middle
        norm_ref[r, :] = layer_norm(middle, gain_ref[...]).astype(norm_ref.dtype)

    for copy in (right, left, onward, backward):
        copy.wait_send()


def exchange_kernel(order, n, keys_ref, values_ref, marks_ref, keys_out, values_out, marks_out,
                    send_sem, recv_sem, local_sem):
    me = lax.axis_index("req")
    place = {"req": me, "tp": lax.axis_index("tp")}
    span = marks_ref.shape[1]

    def peer(d):
        where = dict(place, req=lax.rem(me + d + n, n))
        return tuple(where[a] for a in order)

    def windows(slot):
        part = pl.ds(slot * span, span)
        return (keys_out.at[:, :, part], values_out.at[:, part, :], marks_out.at[:, part])

    sources = (keys_ref, values_ref, marks_ref)
    barrier = pltpu.get_barrier_semaphore()
    for d in NEAR:
        pl.semaphore_signal(barrier, inc=1, device_id=peer(d), device_id_type=MESH_IDS)
    pl.semaphore_wait(barrier, len(NEAR))
    odd = lax.rem(me, 2)

    def send(kind, slices, targets, d):
        out = []
        for a, (src, dst) in enumerate(zip(slices, targets)):
            copy = pltpu.make_async_remote_copy(
                src_ref=src,
                dst_ref=dst,
                send_sem=send_sem.at[3 * kind + a],
                recv_sem=recv_sem.at[3 * kind + a],
                device_id=peer(d),
                device_id_type=MESH_IDS,
            )
            copy.start()
            out.append(copy)
        return out

    right = send(0, sources, windows(1), 1)
    left = send(1, sources, windows(3), -1)
    far = send(2, sources, windows(4 * odd), 2 - 4 * odd)
    local = []
    for a, (src, dst) in enumerate(zip(sources, windows(2))):
        copy = pltpu.make_async_copy(src, dst, local_sem.at[a])
        copy.start()
        local.append(copy)
    for a in range(3):
        right[a].wait_recv()
        left[a].wait_recv()
    relay = send(3, windows(1 + 2 * odd), windows(4 * odd), 1 - 2 * odd)
    for copy in local:
        copy.wait()
    for copy in right + left:
        copy.wait_send()
    for copy in far + relay:
        copy.wait()


def exchange(keys, values, marks, order):
    n = lax.axis_size("req")
    slots = 2 * max(NEAR) + 1
    heads, width, span = keys.shape
    any_spec = pl.BlockSpec(memory_space=pl.ANY)
    keys_all, values_all, marks_all = pl.pallas_call(
        functools.partial(exchange_kernel, order, n),
        out_shape=(
            jax.ShapeDtypeStruct((heads, width, slots * span), keys.dtype),
            jax.ShapeDtypeStruct((heads, slots * span, width), values.dtype),
            jax.ShapeDtypeStruct((1, slots * span), marks.dtype),
        ),
        in_specs=[any_spec] * 3,
        out_specs=(any_spec, any_spec, any_spec),
        scratch_shapes=[
            pltpu.SemaphoreType.DMA((12,)),
            pltpu.SemaphoreType.DMA((12,)),
            pltpu.SemaphoreType.DMA((3,)),
        ],
        compiler_params=pltpu.CompilerParams(collective_id=1, has_side_effects=True),
    )(keys, values, marks.reshape(1, span))
    source = lax.axis_index("req") + jnp.arange(slots * span, dtype=jnp.int32) // span - max(NEAR)
    present = (source >= 0) & (source < n)
    return keys_all, values_all, jnp.where(present, marks_all[0], 0)


def deliver_kernel(order, n, outgoing_ref, received_ref, send_sem, recv_sem, local_sem):
    me = lax.axis_index("req")
    place = {"req": me, "tp": lax.axis_index("tp")}

    def peer(k):
        where = dict(place, req=lax.rem(me + k, n))
        return tuple(where[a] for a in order)

    barrier = pltpu.get_barrier_semaphore()
    for k in range(1, n):
        pl.semaphore_signal(barrier, inc=1, device_id=peer(k), device_id_type=MESH_IDS)
    pl.semaphore_wait(barrier, n - 1)
    copies = []
    for k in range(1, n):
        copy = pltpu.make_async_remote_copy(
            src_ref=outgoing_ref.at[lax.rem(me + k, n)],
            dst_ref=received_ref.at[me],
            send_sem=send_sem.at[k],
            recv_sem=recv_sem.at[k],
            device_id=peer(k),
            device_id_type=MESH_IDS,
        )
        copy.start()
        copies.append(copy)
    own = pltpu.make_async_copy(outgoing_ref.at[me], received_ref.at[me], local_sem.at[0])
    own.start()
    own.wait()
    for copy in copies:
        copy.wait()


def deliver(outgoing, order):
    n = lax.axis_size("req")
    return pl.pallas_call(
        functools.partial(deliver_kernel, order, n),
        out_shape=jax.ShapeDtypeStruct(outgoing.shape, outgoing.dtype),
        in_specs=[pl.BlockSpec(memory_space=pltpu.VMEM)],
        out_specs=pl.BlockSpec(memory_space=pltpu.VMEM),
        scratch_shapes=[
            pltpu.SemaphoreType.DMA((n,)),
            pltpu.SemaphoreType.DMA((n,)),
            pltpu.SemaphoreType.DMA((1,)),
        ],
        compiler_params=pltpu.CompilerParams(collective_id=2, has_side_effects=True),
    )(outgoing)


def norm_kernel(*refs):
    *inputs, gain_ref, out_ref = refs
    stream = inputs[0][...].astype(jnp.float32)
    for extra in inputs[1:]:
        stream = stream + extra[...].astype(jnp.float32)
    out_ref[...] = layer_norm(stream, gain_ref[...]).astype(out_ref.dtype)


def norm_rows(inputs, gain):
    rows, cols = inputs[0].shape
    block = pl.BlockSpec((TILE, cols), lambda i: (i, 0))
    return pl.pallas_call(
        norm_kernel,
        out_shape=jax.ShapeDtypeStruct((rows, cols), jnp.bfloat16),
        grid=(rows // TILE,),
        in_specs=[block] * len(inputs) + [pl.BlockSpec((1, cols), lambda i: (0, 0))],
        out_specs=block,
    )(*inputs, gain.reshape(1, cols))


def project(context, weight, tokens, gain, order):
    n = weight.shape[0] // context.shape[1]
    rows, cols = tokens.shape
    return pl.pallas_call(
        functools.partial(project_kernel, order),
        out_shape=(
            jax.ShapeDtypeStruct((rows, cols), jnp.float32),
            jax.ShapeDtypeStruct((rows, cols), jnp.bfloat16),
        ),
        in_specs=[pl.BlockSpec(memory_space=pltpu.VMEM)] * 4,
        out_specs=(pl.BlockSpec(memory_space=pltpu.VMEM), pl.BlockSpec(memory_space=pltpu.VMEM)),
        scratch_shapes=[
            pltpu.VMEM((n,) + context.shape, context.dtype),
            pltpu.SemaphoreType.DMA((n,)),
            pltpu.SemaphoreType.DMA((n,)),
        ],
        compiler_params=pltpu.CompilerParams(
            collective_id=0, has_side_effects=True, vmem_limit_bytes=48 * 1024 * 1024
        ),
        cost_estimate=pl.CostEstimate(
            flops=2 * rows * cols * weight.shape[0],
            bytes_accessed=4 * rows * cols + 2 * weight.size + 2 * rows * cols + 2 * n * context.size,
            transcendentals=0,
        ),
    )(context, weight, tokens, gain.reshape(1, cols))


def shifted_2(block, axis, distance):
    devices = range(lax.axis_size(axis))
    route = [(i - distance, i) for i in devices if i - distance in devices]
    return lax.ppermute(block, axis, route)


def layer_norm(stream, gain):
    center = jnp.mean(stream, axis=-1, keepdims=True)
    shifted = stream - center
    spread = jnp.mean(shifted * shifted, axis=-1, keepdims=True)
    return shifted * lax.rsqrt(spread + 1e-06) * gain.astype(jnp.float32)


def flash_kernel(bounds, q_ref, qm_ref, k_ref, v_ref, km_ref, o_ref):
    i = pl.program_id(0)
    tile = TILE
    factor = 1.0 / math.sqrt(HD)
    q = q_ref[...]
    qm = qm_ref[...]

    def step(j, carry):
        running_max, running_sum, weighted = carry
        start = pl.multiple_of(j * tile, tile)
        keys = k_ref[:, :, pl.ds(start, tile)]
        values = v_ref[:, pl.ds(start, tile), :]
        km = km_ref[:, pl.ds(start, tile)]
        scores = lax.dot_general(
            q, keys, (((2,), (1,)), ((0,), (0,))), preferred_element_type=jnp.float32
        ) * factor
        masked = jnp.where((qm == km)[None], scores, -1e30)
        new_max = jnp.maximum(running_max, jnp.max(masked, axis=2, keepdims=True))
        probs = jnp.exp(masked - new_max)
        shrink = jnp.exp(running_max - new_max)
        new_sum = running_sum * shrink + jnp.sum(probs, axis=2, keepdims=True)
        update = lax.dot_general(
            probs.astype(jnp.bfloat16), values, (((2,), (1,)), ((0,), (0,))),
            preferred_element_type=jnp.float32,
        )
        return new_max, new_sum, weighted * shrink + update

    heads, rows, width = q.shape
    init = (
        jnp.full((heads, rows, 1), -1e30, jnp.float32),
        jnp.zeros((heads, rows, 1), jnp.float32),
        jnp.zeros((heads, rows, width), jnp.float32),
    )
    _, total, weighted = lax.fori_loop(bounds[0, i], bounds[1, i], step, init)
    result = (weighted / total).astype(o_ref.dtype)
    for h in range(heads):
        o_ref[:, h * width : (h + 1) * width] = result[h]


def attention(queries, query_marks, keys, values, key_marks):
    heads, rows, width = queries.shape
    key_rows = keys.shape[2]
    tiles = rows // TILE
    low = query_marks.reshape(tiles, TILE).min(axis=1)
    high = query_marks.reshape(tiles, TILE).max(axis=1)
    valid = (key_marks[None, :] >= low[:, None]) & (key_marks[None, :] <= high[:, None])
    place = jnp.arange(key_rows, dtype=jnp.int32)[None, :]
    first = jnp.min(jnp.where(valid, place, key_rows), axis=1)
    last = jnp.max(jnp.where(valid, place, -1), axis=1)
    bounds = jnp.stack([first // TILE, last // TILE + 1]).astype(jnp.int32)
    return pl.pallas_call(
        flash_kernel,
        out_shape=jax.ShapeDtypeStruct((rows, heads * width), queries.dtype),
        grid_spec=pltpu.PrefetchScalarGridSpec(
            num_scalar_prefetch=1,
            grid=(tiles,),
            in_specs=[
                pl.BlockSpec((heads, TILE, width), lambda i, b: (0, i, 0)),
                pl.BlockSpec((TILE, 1), lambda i, b: (i, 0)),
                pl.BlockSpec((heads, width, key_rows), lambda i, b: (0, 0, 0)),
                pl.BlockSpec((heads, key_rows, width), lambda i, b: (0, 0, 0)),
                pl.BlockSpec((1, key_rows), lambda i, b: (0, 0)),
            ],
            out_specs=pl.BlockSpec((TILE, heads * width), lambda i, b: (i, 0)),
        ),
        compiler_params=pltpu.CompilerParams(vmem_limit_bytes=48 * 1024 * 1024),
        cost_estimate=pl.CostEstimate(
            flops=4 * heads * rows * 2048 * width,
            bytes_accessed=2 * (queries.size * 2 + keys.size + values.size),
            transcendentals=heads * rows * 2048,
        ),
    )(bounds, queries, query_marks.reshape(rows, 1), keys, values, key_marks.reshape(1, key_rows))


def body(
    order,
    tokens,
    segments,
    attend_gain,
    attend_weight,
    output_weight,
    mixer_gain,
    expand_weight,
    reduce_weight,
    output_gain,
    merge_weight,
    merge_index,
    owners,
):
    token_rows = tokens.shape[0]
    head_width = attend_weight.shape[2]
    head_count = head_width // HD
    full_weight = lax.all_gather(output_weight, "tp", axis=0, tiled=True)
    stream = tokens.astype(jnp.float32)
    attend_in = layer_norm(stream, attend_gain).astype(jnp.bfloat16)
    projected = jnp.dot(
        attend_in,
        attend_weight.reshape(attend_weight.shape[0], 3 * head_width),
        preferred_element_type=jnp.float32,
    ).astype(jnp.bfloat16)
    marks = segments + 1

    def by_head(block):
        return jnp.transpose(block.reshape(block.shape[0], head_count, HD), (1, 0, 2))

    keys_all, values_all, key_marks = exchange(
        jnp.transpose(projected[:, head_width : 2 * head_width].reshape(-1, head_count, HD), (1, 2, 0)),
        by_head(projected[:, 2 * head_width :]),
        marks,
        order,
    )
    context = attention(by_head(projected[:, :head_width]), marks, keys_all, values_all, key_marks)
    middle, mixer_in = project(context, full_weight, tokens, mixer_gain, order)
    expanded = jax.nn.gelu(
        jnp.dot(mixer_in, expand_weight, preferred_element_type=jnp.float32), approximate=False
    ).astype(jnp.bfloat16)
    hidden_terms = jnp.dot(expanded, reduce_weight, preferred_element_type=jnp.float32)
    final_normed = norm_rows([middle, lax.psum(hidden_terms.astype(jnp.bfloat16), "tp")], output_gain)
    merged_rows = merge_index.shape[0]
    local_index = merge_index - lax.axis_index("req") * token_rows
    picks = (local_index[:, :, None] == jnp.arange(token_rows, dtype=jnp.int32)).astype(jnp.bfloat16)
    merged = jnp.einsum(
        "mkt,tc->mkc", picks, final_normed, preferred_element_type=jnp.float32
    ).astype(jnp.bfloat16)
    feature = jnp.einsum(
        "mkc,kcd->md",
        merged,
        merge_weight.reshape(4, final_normed.shape[1], merge_weight.shape[1]),
        preferred_element_type=jnp.float32,
    ).astype(jnp.bfloat16)
    peers = lax.axis_size("req")
    capacity = 2 * merged_rows // peers
    target = owners[:, 0]
    choose = (target[:, None] == jnp.arange(peers, dtype=jnp.int32)[None, :]).astype(jnp.int32)
    slot = jnp.sum((jnp.cumsum(choose, axis=0) - 1) * choose, axis=1)
    position = target * capacity + slot
    placement = (
        position[:, None] == jnp.arange(peers * capacity, dtype=jnp.int32)[None, :]
    ).astype(jnp.bfloat16)
    outgoing = jnp.einsum(
        "ms,mc->sc", placement, feature, preferred_element_type=jnp.float32
    ).astype(jnp.bfloat16)
    outgoing = outgoing.reshape(peers, capacity, feature.shape[1])
    received = deliver(outgoing, order)
    return received.reshape(1, peers, capacity, feature.shape[1])


def solution(mesh):
    placed = (
        P("req", None),
        P("req"),
        P(),
        P(None, None, "tp"),
        P("tp", None),
        P(),
        P(None, "tp"),
        P("tp", None),
        P(),
        P(None, "tp"),
        P("req", None),
        P("req", None),
    )
    return jax.shard_map(
        functools.partial(body, tuple(mesh.axis_names)), mesh=mesh, in_specs=placed, out_specs=P("req", None, None, "tp"), check_vma=False
    )
```

```python
import functools
import math

import jax
import jax.numpy as jnp
from jax import lax
from jax.experimental import pallas as pl
from jax.experimental.pallas import tpu as pltpu
from jax.sharding import PartitionSpec as P

HD = 80
TILE = 256
WIDE = 640
NEAR = (1, -1, 2, -2)
MESH_IDS = pl.DeviceIdType.MESH


def project_kernel(order, ctx_ref, weight_ref, tokens_ref, gain_ref, out_ref, norm_ref, slots, send_sem,
                   recv_sem):
    n = slots.shape[0]
    rows, width = ctx_ref.shape
    cols = out_ref.shape[1]
    half = rows // 2
    me = lax.axis_index("tp")
    place = {"tp": me, "req": lax.axis_index("req")}

    def peer(k):
        where = dict(place, tp=lax.rem(me + k, n))
        return tuple(where[a] for a in order)

    def send(src, dst, sem, k):
        copy = pltpu.make_async_remote_copy(
            src_ref=src,
            dst_ref=dst,
            send_sem=send_sem.at[sem],
            recv_sem=recv_sem.at[sem],
            device_id=peer(k),
            device_id_type=MESH_IDS,
        )
        copy.start()
        return copy

    barrier = pltpu.get_barrier_semaphore()
    for k in (1, n - 1):
        pl.semaphore_signal(barrier, inc=1, device_id=peer(k), device_id_type=MESH_IDS)
    pl.semaphore_wait(barrier, 2)
    right = send(ctx_ref, slots.at[1], 1, 1)
    left = send(ctx_ref, slots.at[3], 3, n - 1)
    tile = 256

    def add_term(block, source, first):
        base = pl.multiple_of(source * width, 8)

        @pl.loop(0, rows // tile)
        def _(i):
            r = pl.ds(pl.multiple_of(i * tile, tile), tile)

            @pl.loop(0, cols // WIDE)
            def _(j):
                c = pl.ds(pl.multiple_of(j * WIDE, WIDE), WIDE)
                term = jnp.dot(
                    block[r, :], weight_ref[pl.ds(base, width), c], preferred_element_type=jnp.float32
                )
                term = term.astype(jnp.bfloat16).astype(jnp.float32)
                if first:
                    out_ref[r, c] = term
                else:
                    out_ref[r, c] = out_ref[r, c] + term

    add_term(ctx_ref, me, True)
    right.wait_recv()
    onward = send(slots.at[1, pl.ds(0, half)], slots.at[2, pl.ds(0, half)], 2, 1)
    add_term(slots.at[1], lax.rem(me + n - 1, n), False)
    left.wait_recv()
    backward = send(slots.at[3, pl.ds(half, half)], slots.at[2, pl.ds(half, half)], 0, n - 1)
    add_term(slots.at[3], lax.rem(me + 1, n), False)
    onward.wait_recv()
    backward.wait_recv()
    add_term(slots.at[2], lax.rem(me + 2, n), False)

    @pl.loop(0, rows // tile)
    def _(i):
        r = pl.ds(pl.multiple_of(i * tile, tile), tile)
        middle = out_ref[r, :] + tokens_ref[r, :].astype(jnp.float32)
        out_ref[r, :] = middle
        norm_ref[r, :] = layer_norm(middle, gain_ref[...]).astype(norm_ref.dtype)

    for copy in (right, left, onward, backward):
        copy.wait_send()


def exchange_kernel(order, n, keys_ref, values_ref, marks_ref, keys_out, values_out, marks_out,
                    send_sem, recv_sem, local_sem):
    me = lax.axis_index("req")
    place = {"req": me, "tp": lax.axis_index("tp")}
    span = marks_ref.shape[1]

    def peer(d):
        where = dict(place, req=lax.rem(me + d + n, n))
        return tuple(where[a] for a in order)

    def windows(slot):
        part = pl.ds(slot * span, span)
        return (keys_out.at[:, :, part], values_out.at[:, part, :], marks_out.at[:, part])

    sources = (keys_ref, values_ref, marks_ref)
    barrier = pltpu.get_barrier_semaphore()
    for d in NEAR:
        pl.semaphore_signal(barrier, inc=1, device_id=peer(d), device_id_type=MESH_IDS)
    pl.semaphore_wait(barrier, len(NEAR))
    odd = lax.rem(me, 2)

    def send(kind, slices, targets, d):
        out = []
        for a, (src, dst) in enumerate(zip(slices, targets)):
            copy = pltpu.make_async_remote_copy(
                src_ref=src,
                dst_ref=dst,
                send_sem=send_sem.at[3 * kind + a],
                recv_sem=recv_sem.at[3 * kind + a],
                device_id=peer(d),
                device_id_type=MESH_IDS,
            )
            copy.start()
            out.append(copy)
        return out

    right = send(0, sources, windows(1), 1)
    left = send(1, sources, windows(3), -1)
    far = send(2, sources, windows(4 * odd), 2 - 4 * odd)
    local = []
    for a, (src, dst) in enumerate(zip(sources, windows(2))):
        copy = pltpu.make_async_copy(src, dst, local_sem.at[a])
        copy.start()
        local.append(copy)
    for a in range(3):
        right[a].wait_recv()
        left[a].wait_recv()
    relay = send(3, windows(1 + 2 * odd), windows(4 * odd), 1 - 2 * odd)
    for copy in local:
        copy.wait()
    for copy in right + left:
        copy.wait_send()
    for copy in far + relay:
        copy.wait()


def exchange(keys, values, marks, order):
    n = lax.axis_size("req")
    slots = 2 * max(NEAR) + 1
    heads, width, span = keys.shape
    any_spec = pl.BlockSpec(memory_space=pl.ANY)
    keys_all, values_all, marks_all = pl.pallas_call(
        functools.partial(exchange_kernel, order, n),
        out_shape=(
            jax.ShapeDtypeStruct((heads, width, slots * span), keys.dtype),
            jax.ShapeDtypeStruct((heads, slots * span, width), values.dtype),
            jax.ShapeDtypeStruct((1, slots * span), marks.dtype),
        ),
        in_specs=[any_spec] * 3,
        out_specs=(any_spec, any_spec, any_spec),
        scratch_shapes=[
            pltpu.SemaphoreType.DMA((12,)),
            pltpu.SemaphoreType.DMA((12,)),
            pltpu.SemaphoreType.DMA((3,)),
        ],
        compiler_params=pltpu.CompilerParams(collective_id=1, has_side_effects=True),
    )(keys, values, marks.reshape(1, span))
    source = lax.axis_index("req") + jnp.arange(slots * span, dtype=jnp.int32) // span - max(NEAR)
    present = (source >= 0) & (source < n)
    return keys_all, values_all, jnp.where(present, marks_all[0], 0)


def deliver_kernel(order, n, outgoing_ref, received_ref, send_sem, recv_sem, local_sem):
    me = lax.axis_index("req")
    place = {"req": me, "tp": lax.axis_index("tp")}

    def peer(k):
        where = dict(place, req=lax.rem(me + k, n))
        return tuple(where[a] for a in order)

    barrier = pltpu.get_barrier_semaphore()
    for k in range(1, n):
        pl.semaphore_signal(barrier, inc=1, device_id=peer(k), device_id_type=MESH_IDS)
    pl.semaphore_wait(barrier, n - 1)
    copies = []
    for k in range(1, n):
        copy = pltpu.make_async_remote_copy(
            src_ref=outgoing_ref.at[lax.rem(me + k, n)],
            dst_ref=received_ref.at[me],
            send_sem=send_sem.at[k],
            recv_sem=recv_sem.at[k],
            device_id=peer(k),
            device_id_type=MESH_IDS,
        )
        copy.start()
        copies.append(copy)
    own = pltpu.make_async_copy(outgoing_ref.at[me], received_ref.at[me], local_sem.at[0])
    own.start()
    own.wait()
    for copy in copies:
        copy.wait()


def deliver(outgoing, order):
    n = lax.axis_size("req")
    return pl.pallas_call(
        functools.partial(deliver_kernel, order, n),
        out_shape=jax.ShapeDtypeStruct(outgoing.shape, outgoing.dtype),
        in_specs=[pl.BlockSpec(memory_space=pltpu.VMEM)],
        out_specs=pl.BlockSpec(memory_space=pltpu.VMEM),
        scratch_shapes=[
            pltpu.SemaphoreType.DMA((n,)),
            pltpu.SemaphoreType.DMA((n,)),
            pltpu.SemaphoreType.DMA((1,)),
        ],
        compiler_params=pltpu.CompilerParams(collective_id=2, has_side_effects=True),
    )(outgoing)


def norm_kernel(*refs):
    *inputs, gain_ref, out_ref = refs
    stream = inputs[0][...].astype(jnp.float32)
    for extra in inputs[1:]:
        stream = stream + extra[...].astype(jnp.float32)
    out_ref[...] = layer_norm(stream, gain_ref[...]).astype(out_ref.dtype)


def norm_rows(inputs, gain):
    rows, cols = inputs[0].shape
    block = pl.BlockSpec((TILE, cols), lambda i: (i, 0))
    return pl.pallas_call(
        norm_kernel,
        out_shape=jax.ShapeDtypeStruct((rows, cols), jnp.bfloat16),
        grid=(rows // TILE,),
        in_specs=[block] * len(inputs) + [pl.BlockSpec((1, cols), lambda i: (0, 0))],
        out_specs=block,
    )(*inputs, gain.reshape(1, cols))


def project(context, weight, tokens, gain, order):
    n = weight.shape[0] // context.shape[1]
    rows, cols = tokens.shape
    return pl.pallas_call(
        functools.partial(project_kernel, order),
        out_shape=(
            jax.ShapeDtypeStruct((rows, cols), jnp.float32),
            jax.ShapeDtypeStruct((rows, cols), jnp.bfloat16),
        ),
        in_specs=[pl.BlockSpec(memory_space=pltpu.VMEM)] * 4,
        out_specs=(pl.BlockSpec(memory_space=pltpu.VMEM), pl.BlockSpec(memory_space=pltpu.VMEM)),
        scratch_shapes=[
            pltpu.VMEM((n,) + context.shape, context.dtype),
            pltpu.SemaphoreType.DMA((n,)),
            pltpu.SemaphoreType.DMA((n,)),
        ],
        compiler_params=pltpu.CompilerParams(
            collective_id=0, has_side_effects=True, vmem_limit_bytes=48 * 1024 * 1024
        ),
        cost_estimate=pl.CostEstimate(
            flops=2 * rows * cols * weight.shape[0],
            bytes_accessed=4 * rows * cols + 2 * weight.size + 2 * rows * cols + 2 * n * context.size,
            transcendentals=0,
        ),
    )(context, weight, tokens, gain.reshape(1, cols))


def shifted_2(block, axis, distance):
    devices = range(lax.axis_size(axis))
    route = [(i - distance, i) for i in devices if i - distance in devices]
    return lax.ppermute(block, axis, route)


def layer_norm(stream, gain):
    center = jnp.mean(stream, axis=-1, keepdims=True)
    shifted = stream - center
    spread = jnp.mean(shifted * shifted, axis=-1, keepdims=True)
    return shifted * lax.rsqrt(spread + 1e-06) * gain.astype(jnp.float32)


def flash_kernel(bounds, q_ref, qm_ref, k_ref, v_ref, km_ref, o_ref):
    i = pl.program_id(0)
    tile = TILE
    factor = 1.0 / math.sqrt(HD)
    q = q_ref[...]
    qm = qm_ref[...]

    def step(j, carry):
        running_max, running_sum, weighted = carry
        start = pl.multiple_of(j * tile, tile)
        keys = k_ref[:, :, pl.ds(start, tile)]
        values = v_ref[:, pl.ds(start, tile), :]
        km = km_ref[:, pl.ds(start, tile)]
        scores = lax.dot_general(
            q, keys, (((2,), (1,)), ((0,), (0,))), preferred_element_type=jnp.float32
        ) * factor
        masked = jnp.where((qm == km)[None], scores, -1e30)
        new_max = jnp.maximum(running_max, jnp.max(masked, axis=2, keepdims=True))
        probs = jnp.exp(masked - new_max)
        shrink = jnp.exp(running_max - new_max)
        new_sum = running_sum * shrink + jnp.sum(probs, axis=2, keepdims=True)
        update = lax.dot_general(
            probs.astype(jnp.bfloat16), values, (((2,), (1,)), ((0,), (0,))),
            preferred_element_type=jnp.float32,
        )
        return new_max, new_sum, weighted * shrink + update

    heads, rows, width = q.shape
    init = (
        jnp.full((heads, rows, 1), -1e30, jnp.float32),
        jnp.zeros((heads, rows, 1), jnp.float32),
        jnp.zeros((heads, rows, width), jnp.float32),
    )
    _, total, weighted = lax.fori_loop(bounds[0, i], bounds[1, i], step, init)
    result = (weighted / total).astype(o_ref.dtype)
    for h in range(heads):
        o_ref[:, h * width : (h + 1) * width] = result[h]


def attention(queries, query_marks, keys, values, key_marks):
    heads, rows, width = queries.shape
    key_rows = keys.shape[2]
    tiles = rows // TILE
    low = query_marks.reshape(tiles, TILE).min(axis=1)
    high = query_marks.reshape(tiles, TILE).max(axis=1)
    valid = (key_marks[None, :] >= low[:, None]) & (key_marks[None, :] <= high[:, None])
    place = jnp.arange(key_rows, dtype=jnp.int32)[None, :]
    first = jnp.min(jnp.where(valid, place, key_rows), axis=1)
    last = jnp.max(jnp.where(valid, place, -1), axis=1)
    bounds = jnp.stack([first // TILE, last // TILE + 1]).astype(jnp.int32)
    return pl.pallas_call(
        flash_kernel,
        out_shape=jax.ShapeDtypeStruct((rows, heads * width), queries.dtype),
        grid_spec=pltpu.PrefetchScalarGridSpec(
            num_scalar_prefetch=1,
            grid=(tiles,),
            in_specs=[
                pl.BlockSpec((heads, TILE, width), lambda i, b: (0, i, 0)),
                pl.BlockSpec((TILE, 1), lambda i, b: (i, 0)),
                pl.BlockSpec((heads, width, key_rows), lambda i, b: (0, 0, 0)),
                pl.BlockSpec((heads, key_rows, width), lambda i, b: (0, 0, 0)),
                pl.BlockSpec((1, key_rows), lambda i, b: (0, 0)),
            ],
            out_specs=pl.BlockSpec((TILE, heads * width), lambda i, b: (i, 0)),
        ),
        compiler_params=pltpu.CompilerParams(vmem_limit_bytes=48 * 1024 * 1024),
        cost_estimate=pl.CostEstimate(
            flops=4 * heads * rows * 2048 * width,
            bytes_accessed=2 * (queries.size * 2 + keys.size + values.size),
            transcendentals=heads * rows * 2048,
        ),
    )(bounds, queries, query_marks.reshape(rows, 1), keys, values, key_marks.reshape(1, key_rows))


def body(
    order,
    tokens,
    segments,
    attend_gain,
    attend_weight,
    output_weight,
    mixer_gain,
    expand_weight,
    reduce_weight,
    output_gain,
    merge_weight,
    merge_index,
    owners,
):
    token_rows = tokens.shape[0]
    head_width = attend_weight.shape[2]
    head_count = head_width // HD
    full_weight = lax.all_gather(output_weight, "tp", axis=0, tiled=True)
    stream = tokens.astype(jnp.float32)
    attend_in = layer_norm(stream, attend_gain).astype(jnp.bfloat16)
    projected = jnp.dot(
        attend_in,
        attend_weight.reshape(attend_weight.shape[0], 3 * head_width),
        preferred_element_type=jnp.float32,
    ).astype(jnp.bfloat16)
    marks = segments + 1

    def by_head(block):
        return jnp.transpose(block.reshape(block.shape[0], head_count, HD), (1, 0, 2))

    keys_all, values_all, key_marks = exchange(
        jnp.transpose(projected[:, head_width : 2 * head_width].reshape(-1, head_count, HD), (1, 2, 0)),
        by_head(projected[:, 2 * head_width :]),
        marks,
        order,
    )
    context = attention(by_head(projected[:, :head_width]), marks, keys_all, values_all, key_marks)
    middle, mixer_in = project(context, full_weight, tokens, mixer_gain, order)
    expanded = jax.nn.gelu(
        jnp.dot(mixer_in, expand_weight, preferred_element_type=jnp.float32), approximate=False
    ).astype(jnp.bfloat16)
    hidden_terms = jnp.dot(expanded, reduce_weight, preferred_element_type=jnp.float32)
    final_normed = norm_rows([middle, lax.psum(hidden_terms.astype(jnp.bfloat16), "tp")], output_gain)
    merged_rows = merge_index.shape[0]
    local_index = merge_index - lax.axis_index("req") * token_rows
    picks = (local_index[:, :, None] == jnp.arange(token_rows, dtype=jnp.int32)).astype(jnp.bfloat16)
    merged = jnp.einsum(
        "mkt,tc->mkc", picks, final_normed, preferred_element_type=jnp.float32
    ).astype(jnp.bfloat16)
    feature = jnp.einsum(
        "mkc,kcd->md",
        merged,
        merge_weight.reshape(4, final_normed.shape[1], merge_weight.shape[1]),
        preferred_element_type=jnp.float32,
    ).astype(jnp.bfloat16)
    peers = lax.axis_size("req")
    capacity = 2 * merged_rows // peers
    target = owners[:, 0]
    choose = (target[:, None] == jnp.arange(peers, dtype=jnp.int32)[None, :]).astype(jnp.int32)
    slot = jnp.sum((jnp.cumsum(choose, axis=0) - 1) * choose, axis=1)
    position = target * capacity + slot
    placement = (
        position[:, None] == jnp.arange(peers * capacity, dtype=jnp.int32)[None, :]
    ).astype(jnp.bfloat16)
    outgoing = jnp.einsum(
        "ms,mc->sc", placement, feature, preferred_element_type=jnp.float32
    ).astype(jnp.bfloat16)
    outgoing = outgoing.reshape(peers, capacity, feature.shape[1])
    received = deliver(outgoing, order)
    return received.reshape(1, peers, capacity, feature.shape[1])


def solution(mesh):
    placed = (
        P("req", None),
        P("req"),
        P(),
        P(None, None, "tp"),
        P("tp", None),
        P(),
        P(None, "tp"),
        P("tp", None),
        P(),
        P(None, "tp"),
        P("req", None),
        P("req", None),
    )
    return jax.shard_map(
        functools.partial(body, tuple(mesh.axis_names)), mesh=mesh, in_specs=placed, out_specs=P("req", None, None, "tp"), check_vma=False
    )
```

```python
import functools
import math

import jax
import jax.numpy as jnp
from jax import lax
from jax.experimental import pallas as pl
from jax.experimental.pallas import tpu as pltpu
from jax.sharding import PartitionSpec as P

HD = 80
TILE = 256
WIDE = 1280
NEAR = (1, -1, 2, -2)
MESH_IDS = pl.DeviceIdType.MESH


def project_kernel(order, ctx_ref, weight_ref, tokens_ref, gain_ref, out_ref, norm_ref, slots, send_sem,
                   recv_sem):
    n = slots.shape[0]
    rows, width = ctx_ref.shape
    cols = out_ref.shape[1]
    half = rows // 2
    me = lax.axis_index("tp")
    place = {"tp": me, "req": lax.axis_index("req")}

    def peer(k):
        where = dict(place, tp=lax.rem(me + k, n))
        return tuple(where[a] for a in order)

    def send(src, dst, sem, k):
        copy = pltpu.make_async_remote_copy(
            src_ref=src,
            dst_ref=dst,
            send_sem=send_sem.at[sem],
            recv_sem=recv_sem.at[sem],
            device_id=peer(k),
            device_id_type=MESH_IDS,
        )
        copy.start()
        return copy

    barrier = pltpu.get_barrier_semaphore()
    for k in (1, n - 1):
        pl.semaphore_signal(barrier, inc=1, device_id=peer(k), device_id_type=MESH_IDS)
    pl.semaphore_wait(barrier, 2)
    right = send(ctx_ref, slots.at[1], 1, 1)
    left = send(ctx_ref, slots.at[3], 3, n - 1)
    tile = 256

    def add_term(block, source, first):
        base = pl.multiple_of(source * width, 8)

        @pl.loop(0, rows // tile)
        def _(i):
            r = pl.ds(pl.multiple_of(i * tile, tile), tile)

            @pl.loop(0, cols // WIDE)
            def _(j):
                c = pl.ds(pl.multiple_of(j * WIDE, WIDE), WIDE)
                term = jnp.dot(
                    block[r, :], weight_ref[pl.ds(base, width), c], preferred_element_type=jnp.float32
                )
                term = term.astype(jnp.bfloat16).astype(jnp.float32)
                if first:
                    out_ref[r, c] = term
                else:
                    out_ref[r, c] = out_ref[r, c] + term

    add_term(ctx_ref, me, True)
    right.wait_recv()
    onward = send(slots.at[1, pl.ds(0, half)], slots.at[2, pl.ds(0, half)], 2, 1)
    add_term(slots.at[1], lax.rem(me + n - 1, n), False)
    left.wait_recv()
    backward = send(slots.at[3, pl.ds(half, half)], slots.at[2, pl.ds(half, half)], 0, n - 1)
    add_term(slots.at[3], lax.rem(me + 1, n), False)
    onward.wait_recv()
    backward.wait_recv()
    add_term(slots.at[2], lax.rem(me + 2, n), False)

    @pl.loop(0, rows // tile)
    def _(i):
        r = pl.ds(pl.multiple_of(i * tile, tile), tile)
        middle = out_ref[r, :] + tokens_ref[r, :].astype(jnp.float32)
        out_ref[r, :] = middle
        norm_ref[r, :] = layer_norm(middle, gain_ref[...]).astype(norm_ref.dtype)

    for copy in (right, left, onward, backward):
        copy.wait_send()


def exchange_kernel(order, n, keys_ref, values_ref, marks_ref, keys_out, values_out, marks_out,
                    send_sem, recv_sem, local_sem):
    me = lax.axis_index("req")
    place = {"req": me, "tp": lax.axis_index("tp")}
    span = marks_ref.shape[1]

    def peer(d):
        where = dict(place, req=lax.rem(me + d + n, n))
        return tuple(where[a] for a in order)

    def windows(slot):
        part = pl.ds(slot * span, span)
        return (keys_out.at[:, :, part], values_out.at[:, part, :], marks_out.at[:, part])

    sources = (keys_ref, values_ref, marks_ref)
    barrier = pltpu.get_barrier_semaphore()
    for d in NEAR:
        pl.semaphore_signal(barrier, inc=1, device_id=peer(d), device_id_type=MESH_IDS)
    pl.semaphore_wait(barrier, len(NEAR))
    odd = lax.rem(me, 2)

    def send(kind, slices, targets, d):
        out = []
        for a, (src, dst) in enumerate(zip(slices, targets)):
            copy = pltpu.make_async_remote_copy(
                src_ref=src,
                dst_ref=dst,
                send_sem=send_sem.at[3 * kind + a],
                recv_sem=recv_sem.at[3 * kind + a],
                device_id=peer(d),
                device_id_type=MESH_IDS,
            )
            copy.start()
            out.append(copy)
        return out

    right = send(0, sources, windows(1), 1)
    left = send(1, sources, windows(3), -1)
    far = send(2, sources, windows(4 * odd), 2 - 4 * odd)
    local = []
    for a, (src, dst) in enumerate(zip(sources, windows(2))):
        copy = pltpu.make_async_copy(src, dst, local_sem.at[a])
        copy.start()
        local.append(copy)
    for a in range(3):
        right[a].wait_recv()
        left[a].wait_recv()
    relay = send(3, windows(1 + 2 * odd), windows(4 * odd), 1 - 2 * odd)
    for copy in local:
        copy.wait()
    for copy in right + left:
        copy.wait_send()
    for copy in far + relay:
        copy.wait()


def exchange(keys, values, marks, order):
    n = lax.axis_size("req")
    slots = 2 * max(NEAR) + 1
    heads, width, span = keys.shape
    any_spec = pl.BlockSpec(memory_space=pl.ANY)
    keys_all, values_all, marks_all = pl.pallas_call(
        functools.partial(exchange_kernel, order, n),
        out_shape=(
            jax.ShapeDtypeStruct((heads, width, slots * span), keys.dtype),
            jax.ShapeDtypeStruct((heads, slots * span, width), values.dtype),
            jax.ShapeDtypeStruct((1, slots * span), marks.dtype),
        ),
        in_specs=[any_spec] * 3,
        out_specs=(any_spec, any_spec, any_spec),
        scratch_shapes=[
            pltpu.SemaphoreType.DMA((12,)),
            pltpu.SemaphoreType.DMA((12,)),
            pltpu.SemaphoreType.DMA((3,)),
        ],
        compiler_params=pltpu.CompilerParams(collective_id=1, has_side_effects=True),
    )(keys, values, marks.reshape(1, span))
    source = lax.axis_index("req") + jnp.arange(slots * span, dtype=jnp.int32) // span - max(NEAR)
    present = (source >= 0) & (source < n)
    return keys_all, values_all, jnp.where(present, marks_all[0], 0)


def deliver_kernel(order, n, outgoing_ref, received_ref, send_sem, recv_sem, local_sem):
    me = lax.axis_index("req")
    place = {"req": me, "tp": lax.axis_index("tp")}

    def peer(k):
        where = dict(place, req=lax.rem(me + k, n))
        return tuple(where[a] for a in order)

    barrier = pltpu.get_barrier_semaphore()
    for k in range(1, n):
        pl.semaphore_signal(barrier, inc=1, device_id=peer(k), device_id_type=MESH_IDS)
    pl.semaphore_wait(barrier, n - 1)
    copies = []
    for k in range(1, n):
        copy = pltpu.make_async_remote_copy(
            src_ref=outgoing_ref.at[lax.rem(me + k, n)],
            dst_ref=received_ref.at[me],
            send_sem=send_sem.at[k],
            recv_sem=recv_sem.at[k],
            device_id=peer(k),
            device_id_type=MESH_IDS,
        )
        copy.start()
        copies.append(copy)
    own = pltpu.make_async_copy(outgoing_ref.at[me], received_ref.at[me], local_sem.at[0])
    own.start()
    own.wait()
    for copy in copies:
        copy.wait()


def deliver(outgoing, order):
    n = lax.axis_size("req")
    return pl.pallas_call(
        functools.partial(deliver_kernel, order, n),
        out_shape=jax.ShapeDtypeStruct(outgoing.shape, outgoing.dtype),
        in_specs=[pl.BlockSpec(memory_space=pltpu.VMEM)],
        out_specs=pl.BlockSpec(memory_space=pltpu.VMEM),
        scratch_shapes=[
            pltpu.SemaphoreType.DMA((n,)),
            pltpu.SemaphoreType.DMA((n,)),
            pltpu.SemaphoreType.DMA((1,)),
        ],
        compiler_params=pltpu.CompilerParams(collective_id=2, has_side_effects=True),
    )(outgoing)


def norm_kernel(*refs):
    *inputs, gain_ref, out_ref = refs
    stream = inputs[0][...].astype(jnp.float32)
    for extra in inputs[1:]:
        stream = stream + extra[...].astype(jnp.float32)
    out_ref[...] = layer_norm(stream, gain_ref[...]).astype(out_ref.dtype)


def norm_rows(inputs, gain):
    rows, cols = inputs[0].shape
    block = pl.BlockSpec((TILE, cols), lambda i: (i, 0))
    return pl.pallas_call(
        norm_kernel,
        out_shape=jax.ShapeDtypeStruct((rows, cols), jnp.bfloat16),
        grid=(rows // TILE,),
        in_specs=[block] * len(inputs) + [pl.BlockSpec((1, cols), lambda i: (0, 0))],
        out_specs=block,
    )(*inputs, gain.reshape(1, cols))


def project(context, weight, tokens, gain, order):
    n = weight.shape[0] // context.shape[1]
    rows, cols = tokens.shape
    return pl.pallas_call(
        functools.partial(project_kernel, order),
        out_shape=(
            jax.ShapeDtypeStruct((rows, cols), jnp.float32),
            jax.ShapeDtypeStruct((rows, cols), jnp.bfloat16),
        ),
        in_specs=[pl.BlockSpec(memory_space=pltpu.VMEM)] * 4,
        out_specs=(pl.BlockSpec(memory_space=pltpu.VMEM), pl.BlockSpec(memory_space=pltpu.VMEM)),
        scratch_shapes=[
            pltpu.VMEM((n,) + context.shape, context.dtype),
            pltpu.SemaphoreType.DMA((n,)),
            pltpu.SemaphoreType.DMA((n,)),
        ],
        compiler_params=pltpu.CompilerParams(
            collective_id=0, has_side_effects=True, vmem_limit_bytes=48 * 1024 * 1024
        ),
        cost_estimate=pl.CostEstimate(
            flops=2 * rows * cols * weight.shape[0],
            bytes_accessed=4 * rows * cols + 2 * weight.size + 2 * rows * cols + 2 * n * context.size,
            transcendentals=0,
        ),
    )(context, weight, tokens, gain.reshape(1, cols))


def shifted_2(block, axis, distance):
    devices = range(lax.axis_size(axis))
    route = [(i - distance, i) for i in devices if i - distance in devices]
    return lax.ppermute(block, axis, route)


def layer_norm(stream, gain):
    center = jnp.mean(stream, axis=-1, keepdims=True)
    shifted = stream - center
    spread = jnp.mean(shifted * shifted, axis=-1, keepdims=True)
    return shifted * lax.rsqrt(spread + 1e-06) * gain.astype(jnp.float32)


def flash_kernel(bounds, q_ref, qm_ref, k_ref, v_ref, km_ref, o_ref):
    i = pl.program_id(0)
    tile = TILE
    factor = 1.0 / math.sqrt(HD)
    q = q_ref[...]
    qm = qm_ref[...]

    def step(j, carry):
        running_max, running_sum, weighted = carry
        start = pl.multiple_of(j * tile, tile)
        keys = k_ref[:, :, pl.ds(start, tile)]
        values = v_ref[:, pl.ds(start, tile), :]
        km = km_ref[:, pl.ds(start, tile)]
        scores = lax.dot_general(
            q, keys, (((2,), (1,)), ((0,), (0,))), preferred_element_type=jnp.float32
        ) * factor
        masked = jnp.where((qm == km)[None], scores, -1e30)
        new_max = jnp.maximum(running_max, jnp.max(masked, axis=2, keepdims=True))
        probs = jnp.exp(masked - new_max)
        shrink = jnp.exp(running_max - new_max)
        new_sum = running_sum * shrink + jnp.sum(probs, axis=2, keepdims=True)
        update = lax.dot_general(
            probs.astype(jnp.bfloat16), values, (((2,), (1,)), ((0,), (0,))),
            preferred_element_type=jnp.float32,
        )
        return new_max, new_sum, weighted * shrink + update

    heads, rows, width = q.shape
    init = (
        jnp.full((heads, rows, 1), -1e30, jnp.float32),
        jnp.zeros((heads, rows, 1), jnp.float32),
        jnp.zeros((heads, rows, width), jnp.float32),
    )
    _, total, weighted = lax.fori_loop(bounds[0, i], bounds[1, i], step, init)
    result = (weighted / total).astype(o_ref.dtype)
    for h in range(heads):
        o_ref[:, h * width : (h + 1) * width] = result[h]


def attention(queries, query_marks, keys, values, key_marks):
    heads, rows, width = queries.shape
    key_rows = keys.shape[2]
    tiles = rows // TILE
    low = query_marks.reshape(tiles, TILE).min(axis=1)
    high = query_marks.reshape(tiles, TILE).max(axis=1)
    valid = (key_marks[None, :] >= low[:, None]) & (key_marks[None, :] <= high[:, None])
    place = jnp.arange(key_rows, dtype=jnp.int32)[None, :]
    first = jnp.min(jnp.where(valid, place, key_rows), axis=1)
    last = jnp.max(jnp.where(valid, place, -1), axis=1)
    bounds = jnp.stack([first // TILE, last // TILE + 1]).astype(jnp.int32)
    return pl.pallas_call(
        flash_kernel,
        out_shape=jax.ShapeDtypeStruct((rows, heads * width), queries.dtype),
        grid_spec=pltpu.PrefetchScalarGridSpec(
            num_scalar_prefetch=1,
            grid=(tiles,),
            in_specs=[
                pl.BlockSpec((heads, TILE, width), lambda i, b: (0, i, 0)),
                pl.BlockSpec((TILE, 1), lambda i, b: (i, 0)),
                pl.BlockSpec((heads, width, key_rows), lambda i, b: (0, 0, 0)),
                pl.BlockSpec((heads, key_rows, width), lambda i, b: (0, 0, 0)),
                pl.BlockSpec((1, key_rows), lambda i, b: (0, 0)),
            ],
            out_specs=pl.BlockSpec((TILE, heads * width), lambda i, b: (i, 0)),
        ),
        compiler_params=pltpu.CompilerParams(vmem_limit_bytes=48 * 1024 * 1024),
        cost_estimate=pl.CostEstimate(
            flops=4 * heads * rows * 2048 * width,
            bytes_accessed=2 * (queries.size * 2 + keys.size + values.size),
            transcendentals=heads * rows * 2048,
        ),
    )(bounds, queries, query_marks.reshape(rows, 1), keys, values, key_marks.reshape(1, key_rows))


def body(
    order,
    tokens,
    segments,
    attend_gain,
    attend_weight,
    output_weight,
    mixer_gain,
    expand_weight,
    reduce_weight,
    output_gain,
    merge_weight,
    merge_index,
    owners,
):
    token_rows = tokens.shape[0]
    head_width = attend_weight.shape[2]
    head_count = head_width // HD
    full_weight = lax.all_gather(output_weight, "tp", axis=0, tiled=True)
    stream = tokens.astype(jnp.float32)
    attend_in = layer_norm(stream, attend_gain).astype(jnp.bfloat16)
    projected = jnp.dot(
        attend_in,
        attend_weight.reshape(attend_weight.shape[0], 3 * head_width),
        preferred_element_type=jnp.float32,
    ).astype(jnp.bfloat16)
    marks = segments + 1

    def by_head(block):
        return jnp.transpose(block.reshape(block.shape[0], head_count, HD), (1, 0, 2))

    keys_all, values_all, key_marks = exchange(
        jnp.transpose(projected[:, head_width : 2 * head_width].reshape(-1, head_count, HD), (1, 2, 0)),
        by_head(projected[:, 2 * head_width :]),
        marks,
        order,
    )
    context = attention(by_head(projected[:, :head_width]), marks, keys_all, values_all, key_marks)
    middle, mixer_in = project(context, full_weight, tokens, mixer_gain, order)
    expanded = jax.nn.gelu(
        jnp.dot(mixer_in, expand_weight, preferred_element_type=jnp.float32), approximate=False
    ).astype(jnp.bfloat16)
    hidden_terms = jnp.dot(expanded, reduce_weight, preferred_element_type=jnp.float32)
    final_normed = norm_rows([middle, lax.psum(hidden_terms.astype(jnp.bfloat16), "tp")], output_gain)
    merged_rows = merge_index.shape[0]
    local_index = merge_index - lax.axis_index("req") * token_rows
    picks = (local_index[:, :, None] == jnp.arange(token_rows, dtype=jnp.int32)).astype(jnp.bfloat16)
    merged = jnp.einsum(
        "mkt,tc->mkc", picks, final_normed, preferred_element_type=jnp.float32
    ).astype(jnp.bfloat16)
    feature = jnp.einsum(
        "mkc,kcd->md",
        merged,
        merge_weight.reshape(4, final_normed.shape[1], merge_weight.shape[1]),
        preferred_element_type=jnp.float32,
    ).astype(jnp.bfloat16)
    peers = lax.axis_size("req")
    capacity = 2 * merged_rows // peers
    target = owners[:, 0]
    choose = (target[:, None] == jnp.arange(peers, dtype=jnp.int32)[None, :]).astype(jnp.int32)
    slot = jnp.sum((jnp.cumsum(choose, axis=0) - 1) * choose, axis=1)
    position = target * capacity + slot
    placement = (
        position[:, None] == jnp.arange(peers * capacity, dtype=jnp.int32)[None, :]
    ).astype(jnp.bfloat16)
    outgoing = jnp.einsum(
        "ms,mc->sc", placement, feature, preferred_element_type=jnp.float32
    ).astype(jnp.bfloat16)
    outgoing = outgoing.reshape(peers, capacity, feature.shape[1])
    received = deliver(outgoing, order)
    return received.reshape(1, peers, capacity, feature.shape[1])


def solution(mesh):
    placed = (
        P("req", None),
        P("req"),
        P(),
        P(None, None, "tp"),
        P("tp", None),
        P(),
        P(None, "tp"),
        P("tp", None),
        P(),
        P(None, "tp"),
        P("req", None),
        P("req", None),
    )
    return jax.shard_map(
        functools.partial(body, tuple(mesh.axis_names)), mesh=mesh, in_specs=placed, out_specs=P("req", None, None, "tp"), check_vma=False
    )
```

```python
import functools
import math

import jax
import jax.numpy as jnp
from jax import lax
from jax.experimental import pallas as pl
from jax.experimental.pallas import tpu as pltpu
from jax.sharding import PartitionSpec as P

HD = 80
TILE = 256
WIDE = 1280
NEAR = (1, -1, 2, -2)
MESH_IDS = pl.DeviceIdType.MESH


def project_kernel(order, ctx_ref, weight_ref, tokens_ref, gain_ref, out_ref, norm_ref, slots, send_sem,
                   recv_sem):
    n = slots.shape[0]
    rows, width = ctx_ref.shape
    cols = out_ref.shape[1]
    half = rows // 2
    me = lax.axis_index("tp")
    place = {"tp": me, "req": lax.axis_index("req")}

    def peer(k):
        where = dict(place, tp=lax.rem(me + k, n))
        return tuple(where[a] for a in order)

    def send(src, dst, sem, k):
        copy = pltpu.make_async_remote_copy(
            src_ref=src,
            dst_ref=dst,
            send_sem=send_sem.at[sem],
            recv_sem=recv_sem.at[sem],
            device_id=peer(k),
            device_id_type=MESH_IDS,
        )
        copy.start()
        return copy

    barrier = pltpu.get_barrier_semaphore()
    for k in (1, n - 1):
        pl.semaphore_signal(barrier, inc=1, device_id=peer(k), device_id_type=MESH_IDS)
    pl.semaphore_wait(barrier, 2)
    right = send(ctx_ref, slots.at[1], 1, 1)
    left = send(ctx_ref, slots.at[3], 3, n - 1)
    tile = 512

    def add_term(block, source, first):
        base = pl.multiple_of(source * width, 8)

        @pl.loop(0, rows // tile)
        def _(i):
            r = pl.ds(pl.multiple_of(i * tile, tile), tile)

            @pl.loop(0, cols // WIDE)
            def _(j):
                c = pl.ds(pl.multiple_of(j * WIDE, WIDE), WIDE)
                term = jnp.dot(
                    block[r, :], weight_ref[pl.ds(base, width), c], preferred_element_type=jnp.float32
                )
                term = term.astype(jnp.bfloat16).astype(jnp.float32)
                if first:
                    out_ref[r, c] = term
                else:
                    out_ref[r, c] = out_ref[r, c] + term

    add_term(ctx_ref, me, True)
    right.wait_recv()
    onward = send(slots.at[1, pl.ds(0, half)], slots.at[2, pl.ds(0, half)], 2, 1)
    add_term(slots.at[1], lax.rem(me + n - 1, n), False)
    left.wait_recv()
    backward = send(slots.at[3, pl.ds(half, half)], slots.at[2, pl.ds(half, half)], 0, n - 1)
    add_term(slots.at[3], lax.rem(me + 1, n), False)
    onward.wait_recv()
    backward.wait_recv()
    add_term(slots.at[2], lax.rem(me + 2, n), False)

    @pl.loop(0, rows // tile)
    def _(i):
        r = pl.ds(pl.multiple_of(i * tile, tile), tile)
        middle = out_ref[r, :] + tokens_ref[r, :].astype(jnp.float32)
        out_ref[r, :] = middle
        norm_ref[r, :] = layer_norm(middle, gain_ref[...]).astype(norm_ref.dtype)

    for copy in (right, left, onward, backward):
        copy.wait_send()


def exchange_kernel(order, n, keys_ref, values_ref, marks_ref, keys_out, values_out, marks_out,
                    send_sem, recv_sem, local_sem):
    me = lax.axis_index("req")
    place = {"req": me, "tp": lax.axis_index("tp")}
    span = marks_ref.shape[1]

    def peer(d):
        where = dict(place, req=lax.rem(me + d + n, n))
        return tuple(where[a] for a in order)

    def windows(slot):
        part = pl.ds(slot * span, span)
        return (keys_out.at[:, :, part], values_out.at[:, part, :], marks_out.at[:, part])

    sources = (keys_ref, values_ref, marks_ref)
    barrier = pltpu.get_barrier_semaphore()
    for d in NEAR:
        pl.semaphore_signal(barrier, inc=1, device_id=peer(d), device_id_type=MESH_IDS)
    pl.semaphore_wait(barrier, len(NEAR))
    odd = lax.rem(me, 2)

    def send(kind, slices, targets, d):
        out = []
        for a, (src, dst) in enumerate(zip(slices, targets)):
            copy = pltpu.make_async_remote_copy(
                src_ref=src,
                dst_ref=dst,
                send_sem=send_sem.at[3 * kind + a],
                recv_sem=recv_sem.at[3 * kind + a],
                device_id=peer(d),
                device_id_type=MESH_IDS,
            )
            copy.start()
            out.append(copy)
        return out

    right = send(0, sources, windows(1), 1)
    left = send(1, sources, windows(3), -1)
    far = send(2, sources, windows(4 * odd), 2 - 4 * odd)
    local = []
    for a, (src, dst) in enumerate(zip(sources, windows(2))):
        copy = pltpu.make_async_copy(src, dst, local_sem.at[a])
        copy.start()
        local.append(copy)
    for a in range(3):
        right[a].wait_recv()
        left[a].wait_recv()
    relay = send(3, windows(1 + 2 * odd), windows(4 * odd), 1 - 2 * odd)
    for copy in local:
        copy.wait()
    for copy in right + left:
        copy.wait_send()
    for copy in far + relay:
        copy.wait()


def exchange(keys, values, marks, order):
    n = lax.axis_size("req")
    slots = 2 * max(NEAR) + 1
    heads, width, span = keys.shape
    any_spec = pl.BlockSpec(memory_space=pl.ANY)
    keys_all, values_all, marks_all = pl.pallas_call(
        functools.partial(exchange_kernel, order, n),
        out_shape=(
            jax.ShapeDtypeStruct((heads, width, slots * span), keys.dtype),
            jax.ShapeDtypeStruct((heads, slots * span, width), values.dtype),
            jax.ShapeDtypeStruct((1, slots * span), marks.dtype),
        ),
        in_specs=[any_spec] * 3,
        out_specs=(any_spec, any_spec, any_spec),
        scratch_shapes=[
            pltpu.SemaphoreType.DMA((12,)),
            pltpu.SemaphoreType.DMA((12,)),
            pltpu.SemaphoreType.DMA((3,)),
        ],
        compiler_params=pltpu.CompilerParams(collective_id=1, has_side_effects=True),
    )(keys, values, marks.reshape(1, span))
    source = lax.axis_index("req") + jnp.arange(slots * span, dtype=jnp.int32) // span - max(NEAR)
    present = (source >= 0) & (source < n)
    return keys_all, values_all, jnp.where(present, marks_all[0], 0)


def deliver_kernel(order, n, outgoing_ref, received_ref, send_sem, recv_sem, local_sem):
    me = lax.axis_index("req")
    place = {"req": me, "tp": lax.axis_index("tp")}

    def peer(k):
        where = dict(place, req=lax.rem(me + k, n))
        return tuple(where[a] for a in order)

    barrier = pltpu.get_barrier_semaphore()
    for k in range(1, n):
        pl.semaphore_signal(barrier, inc=1, device_id=peer(k), device_id_type=MESH_IDS)
    pl.semaphore_wait(barrier, n - 1)
    copies = []
    for k in range(1, n):
        copy = pltpu.make_async_remote_copy(
            src_ref=outgoing_ref.at[lax.rem(me + k, n)],
            dst_ref=received_ref.at[me],
            send_sem=send_sem.at[k],
            recv_sem=recv_sem.at[k],
            device_id=peer(k),
            device_id_type=MESH_IDS,
        )
        copy.start()
        copies.append(copy)
    own = pltpu.make_async_copy(outgoing_ref.at[me], received_ref.at[me], local_sem.at[0])
    own.start()
    own.wait()
    for copy in copies:
        copy.wait()


def deliver(outgoing, order):
    n = lax.axis_size("req")
    return pl.pallas_call(
        functools.partial(deliver_kernel, order, n),
        out_shape=jax.ShapeDtypeStruct(outgoing.shape, outgoing.dtype),
        in_specs=[pl.BlockSpec(memory_space=pltpu.VMEM)],
        out_specs=pl.BlockSpec(memory_space=pltpu.VMEM),
        scratch_shapes=[
            pltpu.SemaphoreType.DMA((n,)),
            pltpu.SemaphoreType.DMA((n,)),
            pltpu.SemaphoreType.DMA((1,)),
        ],
        compiler_params=pltpu.CompilerParams(collective_id=2, has_side_effects=True),
    )(outgoing)


def norm_kernel(*refs):
    *inputs, gain_ref, out_ref = refs
    stream = inputs[0][...].astype(jnp.float32)
    for extra in inputs[1:]:
        stream = stream + extra[...].astype(jnp.float32)
    out_ref[...] = layer_norm(stream, gain_ref[...]).astype(out_ref.dtype)


def norm_rows(inputs, gain):
    rows, cols = inputs[0].shape
    block = pl.BlockSpec((TILE, cols), lambda i: (i, 0))
    return pl.pallas_call(
        norm_kernel,
        out_shape=jax.ShapeDtypeStruct((rows, cols), jnp.bfloat16),
        grid=(rows // TILE,),
        in_specs=[block] * len(inputs) + [pl.BlockSpec((1, cols), lambda i: (0, 0))],
        out_specs=block,
    )(*inputs, gain.reshape(1, cols))


def project(context, weight, tokens, gain, order):
    n = weight.shape[0] // context.shape[1]
    rows, cols = tokens.shape
    return pl.pallas_call(
        functools.partial(project_kernel, order),
        out_shape=(
            jax.ShapeDtypeStruct((rows, cols), jnp.float32),
            jax.ShapeDtypeStruct((rows, cols), jnp.bfloat16),
        ),
        in_specs=[pl.BlockSpec(memory_space=pltpu.VMEM)] * 4,
        out_specs=(pl.BlockSpec(memory_space=pltpu.VMEM), pl.BlockSpec(memory_space=pltpu.VMEM)),
        scratch_shapes=[
            pltpu.VMEM((n,) + context.shape, context.dtype),
            pltpu.SemaphoreType.DMA((n,)),
            pltpu.SemaphoreType.DMA((n,)),
        ],
        compiler_params=pltpu.CompilerParams(
            collective_id=0, has_side_effects=True, vmem_limit_bytes=48 * 1024 * 1024
        ),
        cost_estimate=pl.CostEstimate(
            flops=2 * rows * cols * weight.shape[0],
            bytes_accessed=4 * rows * cols + 2 * weight.size + 2 * rows * cols + 2 * n * context.size,
            transcendentals=0,
        ),
    )(context, weight, tokens, gain.reshape(1, cols))


def shifted_2(block, axis, distance):
    devices = range(lax.axis_size(axis))
    route = [(i - distance, i) for i in devices if i - distance in devices]
    return lax.ppermute(block, axis, route)


def layer_norm(stream, gain):
    center = jnp.mean(stream, axis=-1, keepdims=True)
    shifted = stream - center
    spread = jnp.mean(shifted * shifted, axis=-1, keepdims=True)
    return shifted * lax.rsqrt(spread + 1e-06) * gain.astype(jnp.float32)


def flash_kernel(bounds, q_ref, qm_ref, k_ref, v_ref, km_ref, o_ref):
    i = pl.program_id(0)
    tile = TILE
    factor = 1.0 / math.sqrt(HD)
    q = q_ref[...]
    qm = qm_ref[...]

    def step(j, carry):
        running_max, running_sum, weighted = carry
        start = pl.multiple_of(j * tile, tile)
        keys = k_ref[:, :, pl.ds(start, tile)]
        values = v_ref[:, pl.ds(start, tile), :]
        km = km_ref[:, pl.ds(start, tile)]
        scores = lax.dot_general(
            q, keys, (((2,), (1,)), ((0,), (0,))), preferred_element_type=jnp.float32
        ) * factor
        masked = jnp.where((qm == km)[None], scores, -1e30)
        new_max = jnp.maximum(running_max, jnp.max(masked, axis=2, keepdims=True))
        probs = jnp.exp(masked - new_max)
        shrink = jnp.exp(running_max - new_max)
        new_sum = running_sum * shrink + jnp.sum(probs, axis=2, keepdims=True)
        update = lax.dot_general(
            probs.astype(jnp.bfloat16), values, (((2,), (1,)), ((0,), (0,))),
            preferred_element_type=jnp.float32,
        )
        return new_max, new_sum, weighted * shrink + update

    heads, rows, width = q.shape
    init = (
        jnp.full((heads, rows, 1), -1e30, jnp.float32),
        jnp.zeros((heads, rows, 1), jnp.float32),
        jnp.zeros((heads, rows, width), jnp.float32),
    )
    _, total, weighted = lax.fori_loop(bounds[0, i], bounds[1, i], step, init)
    result = (weighted / total).astype(o_ref.dtype)
    for h in range(heads):
        o_ref[:, h * width : (h + 1) * width] = result[h]


def attention(queries, query_marks, keys, values, key_marks):
    heads, rows, width = queries.shape
    key_rows = keys.shape[2]
    tiles = rows // TILE
    low = query_marks.reshape(tiles, TILE).min(axis=1)
    high = query_marks.reshape(tiles, TILE).max(axis=1)
    valid = (key_marks[None, :] >= low[:, None]) & (key_marks[None, :] <= high[:, None])
    place = jnp.arange(key_rows, dtype=jnp.int32)[None, :]
    first = jnp.min(jnp.where(valid, place, key_rows), axis=1)
    last = jnp.max(jnp.where(valid, place, -1), axis=1)
    bounds = jnp.stack([first // TILE, last // TILE + 1]).astype(jnp.int32)
    return pl.pallas_call(
        flash_kernel,
        out_shape=jax.ShapeDtypeStruct((rows, heads * width), queries.dtype),
        grid_spec=pltpu.PrefetchScalarGridSpec(
            num_scalar_prefetch=1,
            grid=(tiles,),
            in_specs=[
                pl.BlockSpec((heads, TILE, width), lambda i, b: (0, i, 0)),
                pl.BlockSpec((TILE, 1), lambda i, b: (i, 0)),
                pl.BlockSpec((heads, width, key_rows), lambda i, b: (0, 0, 0)),
                pl.BlockSpec((heads, key_rows, width), lambda i, b: (0, 0, 0)),
                pl.BlockSpec((1, key_rows), lambda i, b: (0, 0)),
            ],
            out_specs=pl.BlockSpec((TILE, heads * width), lambda i, b: (i, 0)),
        ),
        compiler_params=pltpu.CompilerParams(vmem_limit_bytes=48 * 1024 * 1024),
        cost_estimate=pl.CostEstimate(
            flops=4 * heads * rows * 2048 * width,
            bytes_accessed=2 * (queries.size * 2 + keys.size + values.size),
            transcendentals=heads * rows * 2048,
        ),
    )(bounds, queries, query_marks.reshape(rows, 1), keys, values, key_marks.reshape(1, key_rows))


def body(
    order,
    tokens,
    segments,
    attend_gain,
    attend_weight,
    output_weight,
    mixer_gain,
    expand_weight,
    reduce_weight,
    output_gain,
    merge_weight,
    merge_index,
    owners,
):
    token_rows = tokens.shape[0]
    head_width = attend_weight.shape[2]
    head_count = head_width // HD
    full_weight = lax.all_gather(output_weight, "tp", axis=0, tiled=True)
    stream = tokens.astype(jnp.float32)
    attend_in = layer_norm(stream, attend_gain).astype(jnp.bfloat16)
    projected = jnp.dot(
        attend_in,
        attend_weight.reshape(attend_weight.shape[0], 3 * head_width),
        preferred_element_type=jnp.float32,
    ).astype(jnp.bfloat16)
    marks = segments + 1

    def by_head(block):
        return jnp.transpose(block.reshape(block.shape[0], head_count, HD), (1, 0, 2))

    keys_all, values_all, key_marks = exchange(
        jnp.transpose(projected[:, head_width : 2 * head_width].reshape(-1, head_count, HD), (1, 2, 0)),
        by_head(projected[:, 2 * head_width :]),
        marks,
        order,
    )
    context = attention(by_head(projected[:, :head_width]), marks, keys_all, values_all, key_marks)
    middle, mixer_in = project(context, full_weight, tokens, mixer_gain, order)
    expanded = jax.nn.gelu(
        jnp.dot(mixer_in, expand_weight, preferred_element_type=jnp.float32), approximate=False
    ).astype(jnp.bfloat16)
    hidden_terms = jnp.dot(expanded, reduce_weight, preferred_element_type=jnp.float32)
    final_normed = norm_rows([middle, lax.psum(hidden_terms.astype(jnp.bfloat16), "tp")], output_gain)
    merged_rows = merge_index.shape[0]
    local_index = merge_index - lax.axis_index("req") * token_rows
    picks = (local_index[:, :, None] == jnp.arange(token_rows, dtype=jnp.int32)).astype(jnp.bfloat16)
    merged = jnp.einsum(
        "mkt,tc->mkc", picks, final_normed, preferred_element_type=jnp.float32
    ).astype(jnp.bfloat16)
    feature = jnp.einsum(
        "mkc,kcd->md",
        merged,
        merge_weight.reshape(4, final_normed.shape[1], merge_weight.shape[1]),
        preferred_element_type=jnp.float32,
    ).astype(jnp.bfloat16)
    peers = lax.axis_size("req")
    capacity = 2 * merged_rows // peers
    target = owners[:, 0]
    choose = (target[:, None] == jnp.arange(peers, dtype=jnp.int32)[None, :]).astype(jnp.int32)
    slot = jnp.sum((jnp.cumsum(choose, axis=0) - 1) * choose, axis=1)
    position = target * capacity + slot
    placement = (
        position[:, None] == jnp.arange(peers * capacity, dtype=jnp.int32)[None, :]
    ).astype(jnp.bfloat16)
    outgoing = jnp.einsum(
        "ms,mc->sc", placement, feature, preferred_element_type=jnp.float32
    ).astype(jnp.bfloat16)
    outgoing = outgoing.reshape(peers, capacity, feature.shape[1])
    received = deliver(outgoing, order)
    return received.reshape(1, peers, capacity, feature.shape[1])


def solution(mesh):
    placed = (
        P("req", None),
        P("req"),
        P(),
        P(None, None, "tp"),
        P("tp", None),
        P(),
        P(None, "tp"),
        P("tp", None),
        P(),
        P(None, "tp"),
        P("req", None),
        P("req", None),
    )
    return jax.shard_map(
        functools.partial(body, tuple(mesh.axis_names)), mesh=mesh, in_specs=placed, out_specs=P("req", None, None, "tp"), check_vma=False
    )
```
